32 devices in a mesh: gx: 4 (over y, x), gy: 4 (over z), gz: 2 (over core).
Axes of the slice: x: 2, y: 2, z: 4, core: 2. Of those that a mesh axis runs over, the one named last changes fastest.
Arguments:
- metric: float32 [6, 64, 128, 256], P(None, 'gx', 'gy', 'gz'), may hold values from -0.9 to 3, as said below
- mass: float32 [64, 128, 256], P('gx', 'gy', 'gz'), may hold values from 0.5 to 2
- shift: float32 [1], replicated, may hold values from 20 to 80
- loads: float32 [4, 64, 128, 256], P(None, 'gx', 'gy', 'gz'), may hold values from -16 to 16
- inputs: float32 [4, 64, 128, 256], P(None, 'gx', 'gy', 'gz'), may hold values from -0.2762136 to 0.2762136
Outputs:
- residual_factor: float32 [4, 64, 128, 256], P(None, 'gx', 'gy', 'gz')
- feedback: float32 [4, 64, 128, 256], P(None, 'gx', 'gy', 'gz')
The draws below stay inside these ranges and needn't reach their ends.
Inputs may be any that keep to these rules, and one draw needn't show every extreme that they name: `metric`: each node's six factors form a symmetric positive definite matrix: diagonal entries between 0.3 and 3, off-diagonal entries at most 0.3 times the geometric mean of their two diagonal entries in magnitude.
All inputs are finite; a program needn't handle non-finite values.
Results may differ from the reference program's by a relative error of at most 0.00029.
Values sent between devices are 32-bit elements; how exact they have to be, the bound alone decides.
A program may use at most 128 MiB of HBM per device.

```python
import math
import jax
import jax.numpy as jnp
import numpy as np
from jax import lax

COLUMNS = 4
INPUTS = 4
STEPS = 5
NX = 64
NY = 128
NZ = 256


def ramp_profile():
    first = jnp.arange(NX, dtype=jnp.float32) / NX
    second = jnp.arange(NY, dtype=jnp.float32) / NY
    third = jnp.arange(NZ, dtype=jnp.float32) / NZ
    return 0.5 * (1.0 + first)[:, None, None] * (1.0 + second)[None, :, None] * (1.0 + third)[None, None, :]


def rough_field(key, salt, count, factor):
    key = jax.random.fold_in(key, salt)
    shape = (count, NX, NY, NZ)
    base = jnp.clip(jax.random.normal(key, shape, jnp.float32), -4.0, 4.0)
    return base * ramp_profile()[None] * factor


def draw_loads(key, part):
    return rough_field(key, 11, COLUMNS, 1.0)


def draw_inputs(key, part):
    return rough_field(key, 23, INPUTS, 25.0 / math.sqrt(NX * NY * NZ))


def draw_metric(key, part):
    first, second = jax.random.split(jax.random.fold_in(key, 37), 2)
    shape = (3, NX, NY, NZ)
    levels = jax.random.uniform(first, shape, jnp.float32, 0.0, 1.0)
    diagonal = 0.3 * jnp.exp(levels * math.log(10.0))
    ratio = jax.random.uniform(second, shape, jnp.float32, -0.3, 0.3)
    cross_one = ratio[0] * jnp.sqrt(diagonal[0] * diagonal[1])
    cross_two = ratio[1] * jnp.sqrt(diagonal[0] * diagonal[2])
    cross_three = ratio[2] * jnp.sqrt(diagonal[1] * diagonal[2])
    return jnp.stack([diagonal[0], diagonal[1], diagonal[2], cross_one, cross_two, cross_three], 0)


def steps_of(own_key, dims, shards, low, top_value):
    factor_of = 1.0
    for axis_at, parts in shards:
        draws = jax.random.uniform(jax.random.fold_in(jax.random.fold_in(own_key, 6), axis_at), (parts,), jnp.float32, low / len(shards), top_value / len(shards))
        factor_of = factor_of * jnp.repeat(jnp.exp(draws), dims[axis_at] // parts).reshape((-1,) + (1,) * (len(dims) - 1 - axis_at))
    return factor_of


def setup_inputs(seed: int = 0) -> dict:
    key_of = jax.random.split(jax.random.key(seed), 6)
    return {
        "metric": draw_metric(jax.random.fold_in(key_of[5], 71), 0),
        "mass": jnp.clip(jnp.exp(math.log(2.0) - 1.3862944 * jax.random.uniform(key_of[1], (NX, NY, NZ), jnp.float32) ** steps_of(key_of[1], (NX, NY, NZ), ((0, 4), (1, 4), (2, 2)), -0.2, 0.2)), 0.5, 2.0),
        "shift": jnp.clip(jax.random.uniform(key_of[2], (1,), jnp.float32, 20.0, 80.0), 20.0, 80.0),
        "loads": draw_loads(jax.random.fold_in(key_of[5], 71), 0),
        "inputs": draw_inputs(jax.random.fold_in(key_of[5], 71), 0),
    }


gll_points = (-1.0, -0.8717401485096066, -0.5917001814331423, -0.2092992179024789, 0.2092992179024789, 0.5917001814331423, 0.8717401485096066, 1.0)
gll_ends = (-14.0, 0.0, 0.0, 0.0, 0.0, 0.0, 0.0, 14.0)

def gll_table():
    points = np.array(gll_points)
    values = (429.0 * points ** 7 - 693.0 * points ** 5 + 315.0 * points ** 3 - 35.0 * points) / 16.0
    table = np.zeros((8, 8))
    for row in range(8):
        for column in range(8):
            if row != column:
                table[row, column] = values[row] / (values[column] * (points[row] - points[column]))
    table[0, 0] = -14.0
    table[7, 7] = 14.0
    return table

def derive_first(field, matrix):
    width, height, depth = field.shape
    shaped = field.reshape(width // 8, 8, height, depth)
    return jnp.einsum('ma,eayz->emyz', matrix, shaped, precision=lax.Precision.HIGHEST).reshape(field.shape)

def derive_second(field, matrix):
    width, height, depth = field.shape
    shaped = field.reshape(width, height // 8, 8, depth)
    return jnp.einsum('mb,xebz->xemz', matrix, shaped, precision=lax.Precision.HIGHEST).reshape(field.shape)

def derive_third(field, matrix):
    width, height, depth = field.shape
    shaped = field.reshape(width, height, depth // 8, 8)
    return jnp.einsum('mk,xyek->xyem', matrix, shaped, precision=lax.Precision.HIGHEST).reshape(field.shape)

def pair_fold(padded, dim):
    length = padded.shape[dim] - 2
    phase = jnp.arange(length) % 8
    shape = [1] * padded.ndim
    shape[dim] = length
    upper = (phase == 7).reshape(shape)
    lower = (phase == 0).reshape(shape)
    middle = lax.slice_in_dim(padded, 1, length + 1, axis=dim)
    after = lax.slice_in_dim(padded, 2, length + 2, axis=dim)
    before = lax.slice_in_dim(padded, 0, length, axis=dim)
    return middle + jnp.where(upper, after, 0.0) + jnp.where(lower, before, 0.0)

def assemble_one(field):
    for dim in (0, 1, 2):
        widths = [(0, 0), (0, 0), (0, 0)]
        widths[dim] = (1, 1)
        field = pair_fold(jnp.pad(field, widths), dim)
    return field

def assemble(stack):
    return lax.map(assemble_one, stack)

def column_apply(field, metric, scaled_mass, table):
    slope_first = derive_first(field, table)
    slope_second = derive_second(field, table)
    slope_third = derive_third(field, table)
    flux_first = metric[0] * slope_first + metric[3] * slope_second + metric[4] * slope_third
    flux_second = metric[3] * slope_first + metric[1] * slope_second + metric[5] * slope_third
    flux_third = metric[4] * slope_first + metric[5] * slope_second + metric[2] * slope_third
    result = derive_first(flux_first, table.T) + derive_second(flux_second, table.T)
    return result + derive_third(flux_third, table.T) + scaled_mass * field

def reference(metric, mass, shift, loads, inputs):
    table_np = gll_table()
    table = jnp.asarray(table_np, jnp.float32)
    squares = table * table
    width, height, depth = mass.shape
    ends_np = np.array(gll_ends)
    ends_first = jnp.asarray(np.tile(ends_np, width // 8), jnp.float32)[:, None, None]
    ends_second = jnp.asarray(np.tile(ends_np, height // 8), jnp.float32)[None, :, None]
    ends_third = jnp.asarray(np.tile(ends_np, depth // 8), jnp.float32)[None, None, :]
    scale = shift[0]
    scaled_mass = scale * mass
    jdiag = derive_first(metric[0], squares.T) + derive_second(metric[1], squares.T) + derive_third(metric[2], squares.T)
    cross = ends_first * ends_second * metric[3] + ends_first * ends_third * metric[4] + ends_second * ends_third * metric[5]
    jdiag = jdiag + 2.0 * cross + scaled_mass
    stacked = jnp.concatenate([jnp.ones((1, width, height, depth), jnp.float32), jdiag[None], mass[None], loads, inputs], 0)
    assembled = assemble(stacked)
    columns = loads.shape[0]
    weight = 1.0 / assembled[0]
    precond = 1.0 / assembled[1]
    mtotal = assembled[2]
    rhs = assembled[3:3 + columns]
    drive = assembled[3 + columns:]

    def operate(field):
        return assemble(lax.map(lambda single: column_apply(single, metric, scaled_mass, table), field))

    def products(first, second):
        return jnp.sum(first * second * weight, axis=(1, 2, 3))
    solution = jnp.zeros_like(rhs)
    residual = rhs
    smooth = precond * residual
    direction = smooth
    energy = products(residual, smooth)
    for step in range(STEPS):
        image = operate(direction)
        alpha = energy / products(direction, image)
        solution = solution + alpha[:, None, None, None] * direction
        residual = residual - alpha[:, None, None, None] * image
        smooth = precond * residual
        fresh = products(residual, smooth)
        direction = smooth + (fresh / energy)[:, None, None, None] * direction
        energy = fresh
    coupling = jnp.einsum('cxyz,jxyz->cj', solution * weight, drive, precision=lax.Precision.HIGHEST)
    identity = jnp.eye(columns, dtype=jnp.float32)
    ymat = identity + jnp.dot(coupling, coupling.T, precision=lax.Precision.HIGHEST)
    factor = jnp.linalg.cholesky(ymat)
    inverse = jax.scipy.linalg.cho_solve((factor, True), identity)
    gain_coef = jax.scipy.linalg.cho_solve((factor, True), coupling)
    heat = mtotal * solution
    twice = 2.0 * scale
    residual_factor = rhs - twice * jnp.einsum('cxyz,cj->jxyz', heat, inverse, precision=lax.Precision.HIGHEST)
    feedback = twice * jnp.einsum('cxyz,cj->jxyz', heat, gain_coef, precision=lax.Precision.HIGHEST)
    return (residual_factor, feedback)
```

```python
import functools

import jax
import jax.numpy as jnp
import numpy as np
from jax import lax
from jax.experimental import pallas as pl
from jax.experimental.pallas import tpu as pltpu
from jax.sharding import PartitionSpec as P

STEPS = 5
THETA = (1.25, 0.2, 2.3, 0.7)
MESH = pl.DeviceIdType.MESH
F32 = jnp.float32
BF16 = jnp.bfloat16

gll_points = (
    -1.0,
    -0.8717401485096066,
    -0.5917001814331423,
    -0.2092992179024789,
    0.2092992179024789,
    0.5917001814331423,
    0.8717401485096066,
    1.0,
)


def gll_table():
    points = np.array(gll_points)
    values = (429.0 * points**7 - 693.0 * points**5 + 315.0 * points**3 - 35.0 * points) / 16.0
    table = np.zeros((8, 8))
    for row in range(8):
        for column in range(8):
            if row != column:
                table[row, column] = values[row] / (values[column] * (points[row] - points[column]))
    table[0, 0] = -14.0
    table[7, 7] = 14.0
    return table


TABLE = gll_table()
SQUARES = TABLE * TABLE


def halves(matrix):
    full = np.asarray(matrix, np.float32)
    high = full.astype(jnp.bfloat16)
    low = (full - high.astype(np.float32)).astype(jnp.bfloat16)
    return high, low


def right_matrices(depth):
    eye = np.eye(depth // 8)
    out = []
    for m in (TABLE.T, TABLE, SQUARES):
        high, low = halves(np.kron(eye, m))
        out.append(np.block([[high, low], [high, np.zeros_like(low)]]))
    return np.stack(out)


def mix_lines(matrix, lines, even_matrix=False):
    even = [lines[j] + lines[7 - j] for j in range(4)]
    odd = [lines[j] - lines[7 - j] for j in range(4)]
    out = [None] * 8
    for i in range(4):
        p = q = None
        for j in range(4):
            a = float(np.float32(0.5 * (matrix[i, j] + matrix[i, 7 - j])))
            b = float(np.float32(0.5 * (matrix[i, j] - matrix[i, 7 - j])))
            p = a * even[j] if p is None else p + a * even[j]
            q = b * odd[j] if q is None else q + b * odd[j]
        out[i] = q + p
        out[7 - i] = p - q if even_matrix else q - p
    return out


def right_apply(lz, kind, v):
    high = v.astype(BF16)
    low = (v - high.astype(F32)).astype(BF16)
    depth = v.shape[1]
    both = jnp.dot(
        jnp.concatenate([high, low], axis=1), lz[kind], preferred_element_type=F32
    )
    return both[:, :depth] + both[:, depth:]


def kernel(
    dims, counts,
    metric, mass, shift, loads, inputs, lz,
    rf, fb,
    stage, ostage, met, inp, vecs, w, pre, mts, rhs, sm, s2, s3, f2, rr, acc, rows,
    xs, xr, ys, yr, er, zs, zr, asend, arecv,
    insem, outsem, ssem, rsem, sendr, recvr,
):
    C, X, Y, Z = dims
    nx, ny, nz = counts
    N = nx * ny * nz
    E, F = X // 8, Y // 8
    LOADS, MASS, METRIC, INPUTS = 0, C, C + 1, C + 7
    gx, gy, gz = lax.axis_index("gx"), lax.axis_index("gy"), lax.axis_index("gz")
    me = (gx * ny + gy) * nz + gz
    sh = shift[0]

    def block(n):
        return pl.ds(8 * n, 8)

    sources = (
        (loads, LOADS, C), (mass, MASS, 1), (metric, METRIC, 6), (inputs, INPUTS, C),
    )

    def fetch(q, e):
        ref, first, count = sources[q]
        if q == 1:
            src = ref.at[pl.ds(8 * e, 8)]
            dst = stage.at[first, :, pl.ds(Y * e, Y)]
        else:
            src = ref.at[:, pl.ds(8 * e, 8)]
            dst = stage.at[pl.ds(first, count), :, pl.ds(Y * e, Y)]
        return pltpu.make_async_copy(src, dst, insem.at[q, e])

    for q in range(4):
        for e in range(E):
            fetch(q, e).start()

    def coords(number):
        rest = lax.div(number, nz)
        return (lax.div(rest, ny), lax.rem(rest, ny), lax.rem(number, nz))

    for ref in (xr, yr, er, zr):
        ref[...] = jnp.zeros(ref.shape, F32)
    barrier = pltpu.get_barrier_semaphore()

    def greet(i, carry):
        pl.semaphore_signal(
            barrier, inc=1, device_id=coords(lax.rem(me + i, N)), device_id_type=MESH
        )
        return carry

    lax.fori_loop(1, N, greet, 0)

    def raw(f, ix, iy):
        return stage[f, ix, pl.ds(iy, 8, stride=8), :]

    lane = lax.broadcasted_iota(jnp.int32, (8, Z), 1)
    sub = lax.broadcasted_iota(jnp.int32, (8, Z), 0)
    ye = sub % F
    inner0 = (lane % 8 == 0) & (lane > 0)
    inner7 = (lane % 8 == 7) & (lane < Z - 1)
    rim = (lane == 0) | (lane == Z - 1)
    slot_of_lane = ((lane + 1) % Z) // 2
    ix_of_lane, iy_of_lane = slot_of_lane // 8, slot_of_lane % 8

    def corner(hx, hy):
        return hx * (8 - F) + hy * (F - 1)

    directions = [
        (dx, dy, dz)
        for dx in (-1, 0, 1) for dy in (-1, 0, 1) for dz in (-1, 0, 1)
        if (dx, dy, dz) != (0, 0, 0)
    ]

    def there(d):
        ok = None
        for place, step, count in zip((gx, gy, gz), d, (nx, ny, nz)):
            if step:
                one = place > 0 if step < 0 else place < count - 1
                ok = one if ok is None else ok & one
        return ok

    def message(i, d, sslot, rslot):
        dx, dy, dz = d
        hx, hy, hz = (dx + 1) // 2, (dy + 1) // 2, (dz + 1) // 2
        if dz == 0:
            if dy == 0:
                src, dst = xs.at[sslot, hx], xr.at[rslot, 1 - hx]
            elif dx == 0:
                src, dst = ys.at[sslot, hy], yr.at[rslot, 1 - hy]
            else:
                row = 8 * (56 * hx + 7 * hy) + corner(hx, hy)
                src = w.at[sslot, pl.ds(row, 1)]
                dst = er.at[rslot, 2 * (1 - hx) + (1 - hy), pl.ds(corner(1 - hx, 1 - hy), 1)]
        else:
            if dx and dy:
                a, b, count = corner(hx, hy), corner(1 - hx, 1 - hy), 1
            elif dx:
                a, b, count = hx * (8 - F), (1 - hx) * (8 - F), F
            else:
                a, b, count = 0, 0, 8
            src = zs.at[sslot, pl.ds(a, count)]
            dst = zr.at[rslot, 1 - hz, 3 * (1 - dx) + (1 - dy), pl.ds(b, count)]
        return pltpu.make_async_remote_copy(
            src_ref=src,
            dst_ref=dst,
            send_sem=ssem.at[sslot, i],
            recv_sem=rsem.at[rslot, i],
            device_id=(gx + dx, gy + dy, gz + dz),
            device_id_type=MESH,
        )

    def fold(a):
        for ix in range(8):
            low, high = 8 * ix, 8 * ix + 7
            v0, v7 = w[a, block(low), :], w[a, block(high), :]
            w[a, block(low), :] = v0 + jnp.where(ye > 0, pltpu.roll(v7, 1, 0), 0.0)
            w[a, block(high), :] = v7 + jnp.where(ye < F - 1, pltpu.roll(v0, 7, 0), 0.0)
        for iy in range(8):
            v0, v7 = w[a, block(iy), :], w[a, block(56 + iy), :]
            w[a, block(iy), :] = v0 + jnp.where(sub >= F, pltpu.roll(v7, F, 0), 0.0)
            w[a, block(56 + iy), :] = v7 + jnp.where(sub < 8 - F, pltpu.roll(v0, 8 - F, 0), 0.0)
        packed = jnp.zeros((8, Z), F32)
        for n in range(64):
            v = w[a, block(n), :]
            v = v + jnp.where(
                inner0, pltpu.roll(v, 1, 1), jnp.where(inner7, pltpu.roll(v, Z - 1, 1), 0.0)
            )
            w[a, block(n), :] = v
            moved = pltpu.roll(v, 2 * n, 1) if n else v
            packed = jnp.where(slot_of_lane == n, moved, packed)
        zs[a] = packed
        for h in range(2):
            for j in range(8 // E):
                out = None
                for g in range(E):
                    v = w[a, block(56 * h + j * E + g), :]
                    q = (g * F + h * F) % 8
                    v = pltpu.roll(v, q, 0) if q else v
                    out = v if out is None else jnp.where(sub // F == g, v, out)
                xs[a, h, 8 * j : 8 * j + 8, :] = out
            for j in range(8 // F):
                out = None
                for g in range(F):
                    v = w[a, block(8 * (j * F + g) + 7 * h), :]
                    q = (g - h * (F - 1)) % 8
                    v = pltpu.roll(v, q, 0) if q else v
                    out = v if out is None else jnp.where(ye == g, v, out)
                ys[a, h, 8 * j : 8 * j + 8, :] = out

    def send(a, rslot):
        for i, d in enumerate(directions):
            @pl.when(there(d))
            def _():
                message(i, d, a, rslot).start()

    def collect(a, rslot):
        for i, d in enumerate(directions):
            @pl.when(there(tuple(-q for q in d)))
            def _():
                message(i, d, a, rslot).wait_recv()
        for i, d in enumerate(directions):
            @pl.when(there(d))
            def _():
                message(i, d, a, rslot).wait_send()
        for h in range(2):
            for j in range(8 // E):
                got = xr[rslot, h, 8 * j : 8 * j + 8, :]
                for g in range(E):
                    q = (h * (8 - F) - g * F) % 8
                    v = pltpu.roll(got, q, 0) if q else got
                    mask = sub >= 8 - F if h else sub < F
                    at = block(56 * h + j * E + g)
                    w[a, at, :] = w[a, at, :] + jnp.where(mask, v, 0.0)
        for h in range(2):
            for j in range(8 // F):
                got = yr[rslot, h, 8 * j : 8 * j + 8, :]
                for g in range(F):
                    q = (h * (F - 1) - g) % 8
                    v = pltpu.roll(got, q, 0) if q else got
                    at = block(8 * (j * F + g) + 7 * h)
                    w[a, at, :] = w[a, at, :] + jnp.where(ye == h * (F - 1), v, 0.0)
        for hx in range(2):
            for hy in range(2):
                at = block(56 * hx + 7 * hy)
                w[a, at, :] = w[a, at, :] + er[rslot, 2 * hx + hy]
        sides = []
        for h in range(2):
            total = zr[rslot, h, 4]
            for dx in (-1, 0, 1):
                for dy in (-1, 0, 1):
                    if dx == 0 and dy == 0:
                        continue
                    v = zr[rslot, h, 3 * (dx + 1) + dy + 1]
                    if dx == 0:
                        v = pltpu.roll(v, (dy * (F - 1)) % 8, 0)
                    v = pltpu.roll(v, (2 * (56 * dx + 7 * dy)) % Z, 1)
                    mask = None
                    if dx:
                        mask = ix_of_lane == (7 if dx > 0 else 0)
                    if dy:
                        more = iy_of_lane == (7 if dy > 0 else 0)
                        mask = more if mask is None else mask & more
                    if dx == 0:
                        mask = mask & (ye == (F - 1 if dy > 0 else 0))
                    total = total + jnp.where(mask, v, 0.0)
            sides.append(total)
        return jnp.where(
            lane % 2 == 0, pltpu.roll(sides[0], 1, 1), pltpu.roll(sides[1], Z - 1, 1)
        )

    def along_z(both, n):
        v = pltpu.roll(both, (Z - 2 * n) % Z, 1) if n else both
        return jnp.where(rim, v, 0.0)

    for e in range(E):
        fetch(0, e).wait()
    for c in range(C):
        for ix in range(8):
            for iy in range(8):
                w[c, block(8 * ix + iy), :] = raw(LOADS + c, ix, iy)
    for q in (1, 2):
        for e in range(E):
            fetch(q, e).wait()
    for ix in range(8):
        for iy in range(8):
            n = 8 * ix + iy
            t = sh * raw(MASS, ix, iy)
            sm[block(n), :] = t
            w[C + 1, block(n), :] = t
            for f in range(6):
                met[f, block(n), :] = raw(METRIC + f, ix, iy)
    for part in range(2):
        at = pl.ds(256 * part, 256)
        s3[at, :] = right_apply(lz, 2, met[2, at, :])
    for ix in range(8):
        line = mix_lines(SQUARES.T, [met[1, block(8 * ix + iy), :] for iy in range(8)], True)
        for iy in range(8):
            s2[block(8 * ix + iy), :] = line[iy]
    ends = (-14.0,) + (0.0,) * 6 + (14.0,)
    ends_z = jnp.where(lane % 8 == 0, -14.0, jnp.where(lane % 8 == 7, 14.0, 0.0))
    for iy in range(8):
        line = mix_lines(SQUARES.T, [met[0, block(8 * ix + iy), :] for ix in range(8)], True)
        for ix in range(8):
            at = block(8 * ix + iy)
            total = line[ix] + s2[at, :] + s3[at, :] + sm[at, :]
            if ends[ix] and ends[iy]:
                total = total + (2.0 * ends[ix] * ends[iy]) * met[3, at, :]
            if ends[ix]:
                total = total + (2.0 * ends[ix]) * (ends_z * met[4, at, :])
            if ends[iy]:
                total = total + (2.0 * ends[iy]) * (ends_z * met[5, at, :])
            w[C, at, :] = total

    def fold_all(a, carry):
        fold(a)
        return carry

    lax.fori_loop(0, C + 2, fold_all, 0)
    for c in range(C):
        vecs[c] = jnp.zeros((512, Z), F32)
    acc[...] = jnp.zeros(acc.shape, F32)
    rows[...] = jnp.zeros(rows.shape, F32)

    pl.semaphore_wait(barrier, N - 1)
    for a in (C,) + tuple(range(C)) + (C + 1,):
        send(a, C + a)

    for e in range(E):
        fetch(3, e).wait()
    for j in range(C):
        for ix in range(8):
            for iy in range(8):
                inp[j, block(8 * ix + iy), :] = raw(INPUTS + j, ix, iy)

    both = collect(C, 2 * C)
    for n in range(64):
        pre[block(n), :] = 1.0 / (w[C, block(n), :] + along_z(both, n))

    def unit(u, carry):
        k = u // C
        c = u % C
        theta = jnp.where(
            k == 0, 0.0,
            jnp.where(k == 1, THETA[0], jnp.where(k == 2, THETA[1], jnp.where(k == 3, THETA[2], THETA[3]))),
        ).astype(F32)
        both = collect(c, ((k + 1) % 2) * C + c)
        for n in range(64):
            at = block(n)
            t = w[c, at, :] + along_z(both, n)
            w[c, at, :] = t
            vecs[u + C, at, :] = pre[at, :] * t - theta * vecs[u, at, :]

        @pl.when(k == 0)
        def _():
            g = None
            for ix in range(8):
                for iy in range(8):
                    at = block(8 * ix + iy)
                    rhs[c, at, :] = w[c, at, :]
                    t = vecs[u + C, at, :] * raw(LOADS + c, ix, iy)
                    g = t if g is None else g + t
            acc[C + c] = g

        for part in range(2):
            at = pl.ds(256 * part, 256)
            s3[at, :] = right_apply(lz, 0, vecs[u + C, at, :])
        for ix in range(8):
            line = mix_lines(TABLE, [vecs[u + C, block(8 * ix + iy), :] for iy in range(8)])
            for iy in range(8):
                s2[block(8 * ix + iy), :] = line[iy]
        for iy in range(8):
            va = [vecs[u + C, block(8 * ix + iy), :] for ix in range(8)]
            s1 = mix_lines(TABLE, va)
            f1 = []
            for ix in range(8):
                at = block(8 * ix + iy)
                a, b, g = s1[ix], s2[at, :], s3[at, :]
                m12, m13, m23 = met[3, at, :], met[4, at, :], met[5, at, :]
                f1.append(met[0, at, :] * a + m12 * b + m13 * g)
                f2[at, :] = m12 * a + met[1, at, :] * b + m23 * g
                s3[at, :] = m13 * a + m23 * b + met[2, at, :] * g
            r1 = mix_lines(TABLE.T, f1)
            for ix in range(8):
                at = block(8 * ix + iy)
                rr[at, :] = r1[ix] + sm[at, :] * va[ix]
        for part in range(2):
            at = pl.ds(256 * part, 256)
            rr[at, :] = rr[at, :] + right_apply(lz, 1, s3[at, :])
        sums = [None] * (C + 2)
        for ix in range(8):
            r2 = mix_lines(TABLE.T, [f2[block(8 * ix + iy), :] for iy in range(8)])
            for iy in range(8):
                at = block(8 * ix + iy)
                out = r2[iy] + rr[at, :]
                w[c, at, :] = out
                v = vecs[u + C, at, :]
                terms = [v * out, vecs[u, at, :] * out] + [v * inp[j, at, :] for j in range(C)]
                sums = [t if s is None else s + t for s, t in zip(sums, terms)]
        base = k * (C + 2) * C + c
        acc[base] = sums[0]

        @pl.when(k > 0)
        def _():
            acc[base + C] = sums[1]

        for j in range(C):
            acc[base + (2 + j) * C] = sums[2 + j]

        @pl.when(k < STEPS - 1)
        def _():
            fold(c)
            send(c, (k % 2) * C + c)

        return carry

    lax.fori_loop(0, STEPS * C, unit, 0)

    for q in range(STEPS * (C + 2) * C):
        rows[q : q + 1, :] = jnp.sum(acc[q], axis=0, keepdims=True)
    part = jnp.sum(rows[...].T, axis=0, keepdims=True)
    asend[...] = part
    arecv[me] = part

    def reduce_copy(i, slot):
        return pltpu.make_async_remote_copy(
            src_ref=asend,
            dst_ref=arecv.at[slot],
            send_sem=sendr.at[i],
            recv_sem=recvr.at[slot],
            device_id=coords(lax.rem(me + i, N)),
            device_id_type=MESH,
        )

    def push(i, carry):
        reduce_copy(i, me).start()
        return carry

    lax.fori_loop(1, N, push, 0)
    both = collect(C + 1, 2 * C + 1)
    for n in range(64):
        mts[block(n), :] = w[C + 1, block(n), :] + along_z(both, n)

    def arrive(i, carry):
        reduce_copy(i, lax.rem(me + i, N)).wait_recv()
        return carry

    lax.fori_loop(1, N, arrive, 0)
    total = jnp.sum(arecv[...], axis=0)

    def entry(k, m):
        q = (128 - (k * (C + 2) + m) * C) % 128
        return pltpu.roll(total, q, 1) if q else total

    G = [[None] * STEPS for _ in range(STEPS)]
    for k in range(STEPS):
        G[k][k] = entry(k, 0)
        if k:
            G[k - 1][k] = entry(k, 1)
    g = [entry(0, 1)]
    for gap in range(2, STEPS):
        for i in range(STEPS - gap):
            j = i + gap - 1
            G[i][j + 1] = G[i + 1][j] + float(THETA[i] - THETA[j]) * G[i][j]
    for i in range(1, STEPS):
        g.append(G[0][i - 1] - float(THETA[i - 1]) * g[i - 1])
    L = [[None] * STEPS for _ in range(STEPS)]
    inv = []
    for j in range(STEPS):
        lines = []
        for i in range(j, STEPS):
            t = G[j][i]
            for q in range(j):
                t = t - L[i][q] * lower[q][j]
            lines.append(t)
        if j == 0:
            lower = []
        lower.append([None] * j + lines)
        inv.append(1.0 / lines[0])
        for i in range(j + 1, STEPS):
            L[i][j] = lines[i - j] * inv[j]
    y = list(g)
    for i in range(STEPS):
        for q in range(i):
            y[i] = y[i] - L[i][q] * y[q]
    y = [t * d for t, d in zip(y, inv)]
    for i in reversed(range(STEPS)):
        for q in range(i + 1, STEPS):
            y[i] = y[i] - L[q][i] * y[q]
    couple = []
    for j in range(C):
        t = y[0] * entry(0, 2 + j)
        for k in range(1, STEPS):
            t = t + y[k] * entry(k, 2 + j)
        couple.append(t)

    def spread(line, c):
        return jnp.broadcast_to(line[:, c : c + 1], (8, Z))

    kk = [[spread(couple[j], c) for j in range(C)] for c in range(C)]
    ymat = [[None] * C for _ in range(C)]
    for a in range(C):
        for b in range(C):
            if b < a:
                ymat[a][b] = ymat[b][a]
                continue
            t = kk[a][0] * kk[b][0]
            for j in range(1, C):
                t = t + kk[a][j] * kk[b][j]
            ymat[a][b] = t + 1.0 if a == b else t
    one = jnp.ones((8, Z), F32)
    nil = jnp.zeros((8, Z), F32)
    right = [[one if a == b else nil for b in range(C)] + kk[a] for a in range(C)]
    for a in range(C):
        scale = 1.0 / ymat[a][a]
        ymat[a] = [t * scale for t in ymat[a]]
        right[a] = [t * scale for t in right[a]]
        for b in range(C):
            if b != a:
                q = ymat[b][a]
                ymat[b] = [t - q * s for t, s in zip(ymat[b], ymat[a])]
                right[b] = [t - q * s for t, s in zip(right[b], right[a])]
    coef = [[2.0 * right[c][j] for j in range(2 * C)] for c in range(C)]
    mixing = [[spread(y[k], c) for k in range(STEPS)] for c in range(C)]

    for ix in range(8):
        for iy in range(8):
            at = block(8 * ix + iy)
            m = mts[at, :]
            heat = []
            for c in range(C):
                t = mixing[c][0] * vecs[C + c, at, :]
                for k in range(1, STEPS):
                    t = t + mixing[c][k] * vecs[(k + 1) * C + c, at, :]
                heat.append(m * t)
            for j in range(C):
                t = heat[0] * coef[0][j]
                s = heat[0] * coef[0][C + j]
                for c in range(1, C):
                    t = t + heat[c] * coef[c][j]
                    s = s + heat[c] * coef[c][C + j]
                to = pl.ds(iy, 8, stride=8)
                ostage[j, ix, to, :] = rhs[j, at, :] - t
                ostage[C + j, ix, to, :] = s

    def store(q, e):
        return pltpu.make_async_copy(
            ostage.at[pl.ds(C * q, C), :, pl.ds(Y * e, Y)],
            (rf, fb)[q].at[:, pl.ds(8 * e, 8)],
            outsem.at[q, e],
        )

    for q in range(2):
        for e in range(E):
            store(q, e).start()

    def depart(i, carry):
        reduce_copy(i, me).wait_send()
        return carry

    lax.fori_loop(1, N, depart, 0)
    for q in range(2):
        for e in range(E):
            store(q, e).wait()


def local(counts, metric, mass, shift, loads, inputs):
    C, X, Y, Z = loads.shape
    E, F = X // 8, Y // 8
    assert E * F == 8 and Z >= 128 and STEPS * (C + 2) * C <= 128
    N = counts[0] * counts[1] * counts[2]
    lz = jnp.asarray(right_matrices(Z))
    vm = lambda *shape: pltpu.VMEM(shape, F32)
    dma = pltpu.SemaphoreType.DMA
    anywhere = pl.BlockSpec(memory_space=pl.ANY)
    return pl.pallas_call(
        functools.partial(kernel, (C, X, Y, Z), counts),
        out_shape=[jax.ShapeDtypeStruct(loads.shape, F32)] * 2,
        in_specs=[anywhere, anywhere, pl.BlockSpec(memory_space=pltpu.SMEM), anywhere, anywhere,
                  pl.BlockSpec(memory_space=pltpu.VMEM)],
        out_specs=[anywhere, anywhere],
        scratch_shapes=[
            vm(2 * C + 7, 8, 64, Z), vm(2 * C, 8, 64, Z), vm(6, 512, Z), vm(C, 512, Z),
            vm((STEPS + 1) * C, 512, Z), vm(C + 2, 512, Z), vm(512, Z), vm(512, Z),
            vm(C, 512, Z), vm(512, Z), vm(512, Z), vm(512, Z), vm(512, Z), vm(512, Z),
            vm(128, 8, Z), vm(128, Z),
            vm(C + 2, 2, 64 // E, Z), vm(2 * C + 2, 2, 64 // E, Z),
            vm(C + 2, 2, 64 // F, Z), vm(2 * C + 2, 2, 64 // F, Z),
            vm(2 * C + 2, 4, 8, Z), vm(C + 2, 8, Z), vm(2 * C + 2, 2, 9, 8, Z),
            vm(1, 128), vm(N, 1, 128),
            dma((4, E)), dma((2, E)), dma((C + 2, 26)), dma((2 * C + 2, 26)), dma((N,)), dma((N,)),
        ],
        compiler_params=pltpu.CompilerParams(
            collective_id=0, has_side_effects=True, vmem_limit_bytes=56 << 20
        ),
    )(metric, mass, shift, loads, inputs, lz)


def solution(mesh):
    counts = tuple(mesh.shape[a] for a in ("gx", "gy", "gz"))
    return jax.shard_map(
        functools.partial(local, counts),
        mesh=mesh,
        in_specs=(
            P(None, "gx", "gy", "gz"),
            P("gx", "gy", "gz"),
            P(),
            P(None, "gx", "gy", "gz"),
            P(None, "gx", "gy", "gz"),
        ),
        out_specs=(P(None, "gx", "gy", "gz"), P(None, "gx", "gy", "gz")),
        check_vma=False,
    )
```

```python
import functools

import jax
import jax.numpy as jnp
import numpy as np
from jax import lax
from jax.experimental import pallas as pl
from jax.experimental.pallas import tpu as pltpu
from jax.sharding import PartitionSpec as P

STEPS = 5
THETA = (1.25, 0.2, 2.3, 0.7)
MESH = pl.DeviceIdType.MESH
F32 = jnp.float32
BF16 = jnp.bfloat16

gll_points = (
    -1.0,
    -0.8717401485096066,
    -0.5917001814331423,
    -0.2092992179024789,
    0.2092992179024789,
    0.5917001814331423,
    0.8717401485096066,
    1.0,
)


def gll_table():
    points = np.array(gll_points)
    values = (429.0 * points**7 - 693.0 * points**5 + 315.0 * points**3 - 35.0 * points) / 16.0
    table = np.zeros((8, 8))
    for row in range(8):
        for column in range(8):
            if row != column:
                table[row, column] = values[row] / (values[column] * (points[row] - points[column]))
    table[0, 0] = -14.0
    table[7, 7] = 14.0
    return table


TABLE = gll_table()
SQUARES = TABLE * TABLE


def halves(matrix):
    full = np.asarray(matrix, np.float32)
    high = full.astype(jnp.bfloat16)
    low = (full - high.astype(np.float32)).astype(jnp.bfloat16)
    return high, low


def right_matrices(depth):
    eye = np.eye(depth // 8)
    out = []
    for m in (TABLE.T, TABLE, SQUARES):
        high, low = halves(np.kron(eye, m))
        out.append(np.block([[high, low], [high, np.zeros_like(low)]]))
    return np.stack(out)


def mix_lines(matrix, lines, even_matrix=False):
    even = [lines[j] + lines[7 - j] for j in range(4)]
    odd = [lines[j] - lines[7 - j] for j in range(4)]
    out = [None] * 8
    for i in range(4):
        p = q = None
        for j in range(4):
            a = float(np.float32(0.5 * (matrix[i, j] + matrix[i, 7 - j])))
            b = float(np.float32(0.5 * (matrix[i, j] - matrix[i, 7 - j])))
            p = a * even[j] if p is None else p + a * even[j]
            q = b * odd[j] if q is None else q + b * odd[j]
        out[i] = q + p
        out[7 - i] = p - q if even_matrix else q - p
    return out


def right_apply(lz, kind, v):
    high = v.astype(BF16)
    low = (v - high.astype(F32)).astype(BF16)
    depth = v.shape[1]
    both = jnp.dot(
        jnp.concatenate([high, low], axis=1), lz[kind], preferred_element_type=F32
    )
    return both[:, :depth] + both[:, depth:]


def kernel(
    dims, counts,
    metric, mass, shift, loads, inputs, lz,
    rf, fb,
    stage, ostage, met, inp, vecs, w, pre, mts, rhs, sm, s2, s3, f2, rr, acc, rows,
    xs, xr, ys, yr, er, zs, zr, asend, arecv,
    insem, outsem, ssem, rsem, sendr, recvr,
):
    C, X, Y, Z = dims
    nx, ny, nz = counts
    N = nx * ny * nz
    E, F = X // 8, Y // 8
    LOADS, MASS, METRIC, INPUTS = 0, C, C + 1, C + 7
    gx, gy, gz = lax.axis_index("gx"), lax.axis_index("gy"), lax.axis_index("gz")
    me = (gx * ny + gy) * nz + gz
    sh = shift[0]

    def block(n):
        return pl.ds(8 * n, 8)

    sources = (
        (loads, LOADS, C), (mass, MASS, 1), (metric, METRIC, 6), (inputs, INPUTS, C),
    )

    def fetch(q, e):
        ref, first, count = sources[q]
        if q == 1:
            src = ref.at[pl.ds(8 * e, 8)]
            dst = stage.at[first, :, pl.ds(Y * e, Y)]
        else:
            src = ref.at[:, pl.ds(8 * e, 8)]
            dst = stage.at[pl.ds(first, count), :, pl.ds(Y * e, Y)]
        return pltpu.make_async_copy(src, dst, insem.at[q, e])

    for q in range(4):
        for e in range(E):
            fetch(q, e).start()

    def coords(number):
        rest = lax.div(number, nz)
        return (lax.div(rest, ny), lax.rem(rest, ny), lax.rem(number, nz))

    for ref in (xr, yr, er, zr):
        ref[...] = jnp.zeros(ref.shape, F32)
    def raw(f, ix, iy):
        return stage[f, ix, pl.ds(iy, 8, stride=8), :]

    lane = lax.broadcasted_iota(jnp.int32, (8, Z), 1)
    sub = lax.broadcasted_iota(jnp.int32, (8, Z), 0)
    ye = sub % F
    inner0 = (lane % 8 == 0) & (lane > 0)
    inner7 = (lane % 8 == 7) & (lane < Z - 1)
    rim = (lane == 0) | (lane == Z - 1)
    slot_of_lane = ((lane + 1) % Z) // 2
    ix_of_lane, iy_of_lane = slot_of_lane // 8, slot_of_lane % 8

    def corner(hx, hy):
        return hx * (8 - F) + hy * (F - 1)

    directions = [
        (dx, dy, dz)
        for dx in (-1, 0, 1) for dy in (-1, 0, 1) for dz in (-1, 0, 1)
        if (dx, dy, dz) != (0, 0, 0)
    ]

    def there(d):
        ok = None
        for place, step, count in zip((gx, gy, gz), d, (nx, ny, nz)):
            if step:
                one = place > 0 if step < 0 else place < count - 1
                ok = one if ok is None else ok & one
        return ok

    barrier = pltpu.get_barrier_semaphore()
    if max(counts) - 1 <= STEPS:
        greeted = jnp.int32(0)
        for d in directions:
            greeted = greeted + there(d).astype(jnp.int32)

            @pl.when(there(d))
            def _():
                pl.semaphore_signal(
                    barrier, inc=1, device_id=(gx + d[0], gy + d[1], gz + d[2]),
                    device_id_type=MESH,
                )
    else:
        greeted = N - 1

        def greet(i, carry):
            pl.semaphore_signal(
                barrier, inc=1, device_id=coords(lax.rem(me + i, N)), device_id_type=MESH
            )
            return carry

        lax.fori_loop(1, N, greet, 0)

    def message(i, d, sslot, rslot):
        dx, dy, dz = d
        hx, hy, hz = (dx + 1) // 2, (dy + 1) // 2, (dz + 1) // 2
        if dz == 0:
            if dy == 0:
                src, dst = xs.at[sslot, hx], xr.at[rslot, 1 - hx]
            elif dx == 0:
                src, dst = ys.at[sslot, hy], yr.at[rslot, 1 - hy]
            else:
                row = 8 * (56 * hx + 7 * hy) + corner(hx, hy)
                src = w.at[sslot, pl.ds(row, 1)]
                dst = er.at[rslot, 2 * (1 - hx) + (1 - hy), pl.ds(corner(1 - hx, 1 - hy), 1)]
        else:
            if dx and dy:
                a, b, count = corner(hx, hy), corner(1 - hx, 1 - hy), 1
            elif dx:
                a, b, count = hx * (8 - F), (1 - hx) * (8 - F), F
            else:
                a, b, count = 0, 0, 8
            src = zs.at[sslot, pl.ds(a, count)]
            dst = zr.at[rslot, 1 - hz, 3 * (1 - dx) + (1 - dy), pl.ds(b, count)]
        return pltpu.make_async_remote_copy(
            src_ref=src,
            dst_ref=dst,
            send_sem=ssem.at[sslot, i],
            recv_sem=rsem.at[rslot, i],
            device_id=(gx + dx, gy + dy, gz + dz),
            device_id_type=MESH,
        )

    def fold(a, line_of):
        def along_y(line):
            v0, v7 = line[0], line[7]
            line = list(line)
            line[0] = v0 + jnp.where(ye > 0, pltpu.roll(v7, 1, 0), 0.0)
            line[7] = v7 + jnp.where(ye < F - 1, pltpu.roll(v0, 7, 0), 0.0)
            return line

        first, last = along_y(line_of(0)), along_y(line_of(7))
        lines = {
            0: [
                v + jnp.where(sub >= F, pltpu.roll(t, F, 0), 0.0) for v, t in zip(first, last)
            ],
            7: [
                t + jnp.where(sub < 8 - F, pltpu.roll(v, 8 - F, 0), 0.0)
                for v, t in zip(first, last)
            ],
        }
        packed = jnp.zeros((8, Z), F32)
        faces = [[None] * (8 // F) for _ in range(2)]
        for ix in (0, 7, 1, 2, 3, 4, 5, 6):
            line = lines[ix] if ix in lines else along_y(line_of(ix))
            ups = [pltpu.roll(v, 1, 1) for v in line]
            downs = [pltpu.roll(v, Z - 1, 1) for v in line]
            line = [
                v + jnp.where(inner0, p, jnp.where(inner7, q, 0.0))
                for v, p, q in zip(line, ups, downs)
            ]
            for iy in range(8):
                n = 8 * ix + iy
                w[a, block(n), :] = line[iy]
                moved = pltpu.roll(line[iy], 2 * n, 1) if n else line[iy]
                packed = jnp.where(slot_of_lane == n, moved, packed)
            if ix in (0, 7):
                h = ix // 7
                for j in range(8 // E):
                    out = None
                    for g in range(E):
                        v = line[j * E + g]
                        q = (g * F + h * F) % 8
                        v = pltpu.roll(v, q, 0) if q else v
                        out = v if out is None else jnp.where(sub // F == g, v, out)
                    xs[a, h, 8 * j : 8 * j + 8, :] = out
            for h in range(2):
                j, g = ix // F, ix % F
                v = line[7 * h]
                q = (g - h * (F - 1)) % 8
                v = pltpu.roll(v, q, 0) if q else v
                old = faces[h][j]
                faces[h][j] = v if old is None else jnp.where(ye == g, v, old)
        zs[a] = packed
        for h in range(2):
            for j in range(8 // F):
                ys[a, h, 8 * j : 8 * j + 8, :] = faces[h][j]

    def send(a, rslot):
        for i, d in enumerate(directions):
            @pl.when(there(d))
            def _():
                message(i, d, a, rslot).start()

    def collect(a, rslot):
        for i, d in enumerate(directions):
            @pl.when(there(tuple(-q for q in d)))
            def _():
                message(i, d, a, rslot).wait_recv()
        for i, d in enumerate(directions):
            @pl.when(there(d))
            def _():
                message(i, d, a, rslot).wait_send()
        sides = []
        for h in range(2):
            total = zr[rslot, h, 4]
            for dx in (-1, 0, 1):
                for dy in (-1, 0, 1):
                    if dx == 0 and dy == 0:
                        continue
                    v = zr[rslot, h, 3 * (dx + 1) + dy + 1]
                    if dx == 0:
                        v = pltpu.roll(v, (dy * (F - 1)) % 8, 0)
                    v = pltpu.roll(v, (2 * (56 * dx + 7 * dy)) % Z, 1)
                    mask = None
                    if dx:
                        mask = ix_of_lane == (7 if dx > 0 else 0)
                    if dy:
                        more = iy_of_lane == (7 if dy > 0 else 0)
                        mask = more if mask is None else mask & more
                    if dx == 0:
                        mask = mask & (ye == (F - 1 if dy > 0 else 0))
                    total = total + jnp.where(mask, v, 0.0)
            sides.append(total)
        both = jnp.where(
            lane % 2 == 0, pltpu.roll(sides[0], 1, 1), pltpu.roll(sides[1], Z - 1, 1)
        )

        def line_of(ix):
            line = []
            for iy in range(8):
                n = 8 * ix + iy
                v = pltpu.roll(both, (Z - 2 * n) % Z, 1) if n else both
                line.append(w[a, block(n), :] + jnp.where(rim, v, 0.0))
            if ix in (0, 7):
                h = ix // 7
                for iy in range(8):
                    j, g = iy // E, iy % E
                    v = xr[rslot, h, 8 * j : 8 * j + 8, :]
                    q = (h * (8 - F) - g * F) % 8
                    v = pltpu.roll(v, q, 0) if q else v
                    mask = sub >= 8 - F if h else sub < F
                    line[iy] = line[iy] + jnp.where(mask, v, 0.0)
                for hy in range(2):
                    line[7 * hy] = line[7 * hy] + er[rslot, 2 * h + hy]
            for h in range(2):
                j, g = ix // F, ix % F
                v = yr[rslot, h, 8 * j : 8 * j + 8, :]
                q = (h * (F - 1) - g) % 8
                v = pltpu.roll(v, q, 0) if q else v
                line[7 * h] = line[7 * h] + jnp.where(ye == h * (F - 1), v, 0.0)
            return line

        return line_of

    for e in range(E):
        fetch(0, e).wait()
    def fold_load(c, carry):
        fold(c, lambda ix: [raw(LOADS + c, ix, iy) for iy in range(8)])
        return carry

    lax.fori_loop(0, C, fold_load, 0)
    for q in (1, 2):
        for e in range(E):
            fetch(q, e).wait()
    for ix in range(8):
        for iy in range(8):
            at = block(8 * ix + iy)
            sm[at, :] = sh * raw(MASS, ix, iy)
            for f in range(6):
                met[f, at, :] = raw(METRIC + f, ix, iy)
    for part in range(2):
        at = pl.ds(256 * part, 256)
        s3[at, :] = right_apply(lz, 2, met[2, at, :])
    for ix in range(8):
        line = mix_lines(SQUARES.T, [met[1, block(8 * ix + iy), :] for iy in range(8)], True)
        for iy in range(8):
            s2[block(8 * ix + iy), :] = line[iy]
    ends = (-14.0,) + (0.0,) * 6 + (14.0,)
    ends_z = jnp.where(lane % 8 == 0, -14.0, jnp.where(lane % 8 == 7, 14.0, 0.0))
    for iy in range(8):
        line = mix_lines(SQUARES.T, [met[0, block(8 * ix + iy), :] for ix in range(8)], True)
        for ix in range(8):
            at = block(8 * ix + iy)
            total = line[ix] + s2[at, :] + s3[at, :] + sm[at, :]
            if ends[ix] and ends[iy]:
                total = total + (2.0 * ends[ix] * ends[iy]) * met[3, at, :]
            if ends[ix]:
                total = total + (2.0 * ends[ix]) * (ends_z * met[4, at, :])
            if ends[iy]:
                total = total + (2.0 * ends[iy]) * (ends_z * met[5, at, :])
            rr[at, :] = total

    def lines_in(ref):
        return lambda ix: [ref[block(8 * ix + iy), :] for iy in range(8)]

    fold(C, lines_in(rr))
    fold(C + 1, lines_in(sm))
    for c in range(C):
        vecs[c] = jnp.zeros((512, Z), F32)
    acc[...] = jnp.zeros(acc.shape, F32)
    rows[...] = jnp.zeros(rows.shape, F32)

    pl.semaphore_wait(barrier, greeted)
    for a in (C,) + tuple(range(C)) + (C + 1,):
        send(a, C + a)

    for e in range(E):
        fetch(3, e).wait()
    for j in range(C):
        for ix in range(8):
            for iy in range(8):
                inp[j, block(8 * ix + iy), :] = raw(INPUTS + j, ix, iy)

    line_of = collect(C, 2 * C)
    for ix in range(8):
        for iy, v in enumerate(line_of(ix)):
            pre[block(8 * ix + iy), :] = 1.0 / v

    def unit(final, u, carry):
        k = u // C
        c = u % C
        theta = jnp.where(
            k == 0, 0.0,
            jnp.where(k == 1, THETA[0], jnp.where(k == 2, THETA[1], jnp.where(k == 3, THETA[2], THETA[3]))),
        ).astype(F32)
        line_of = collect(c, ((k + 1) % 2) * C + c)
        keep = ((k + STEPS - 1) // STEPS) * (C - c) + c
        for ix in range(8):
            line = line_of(ix)
            before = [vecs[u, block(8 * ix + iy), :] for iy in range(8)]
            scale = [pre[block(8 * ix + iy), :] for iy in range(8)]
            fresh = [p * t - theta * b for p, t, b in zip(scale, line, before)]
            for iy in range(8):
                at = block(8 * ix + iy)
                vecs[u + C, at, :] = fresh[iy]
                if not final:
                    rhs[keep, at, :] = line[iy]

        for part in range(2):
            at = pl.ds(256 * part, 256)
            s3[at, :] = right_apply(lz, 0, vecs[u + C, at, :])
        for ix in range(8):
            line = mix_lines(TABLE, [vecs[u + C, block(8 * ix + iy), :] for iy in range(8)])
            for iy in range(8):
                s2[block(8 * ix + iy), :] = line[iy]
        for iy in range(8):
            va = [vecs[u + C, block(8 * ix + iy), :] for ix in range(8)]
            s1 = mix_lines(TABLE, va)
            f1 = []
            for ix in range(8):
                at = block(8 * ix + iy)
                a, b, g = s1[ix], s2[at, :], s3[at, :]
                m12, m13, m23 = met[3, at, :], met[4, at, :], met[5, at, :]
                f1.append(met[0, at, :] * a + m12 * b + m13 * g)
                f2[at, :] = m12 * a + met[1, at, :] * b + m23 * g
                s3[at, :] = m13 * a + m23 * b + met[2, at, :] * g
            r1 = mix_lines(TABLE.T, f1)
            for ix in range(8):
                at = block(8 * ix + iy)
                rr[at, :] = r1[ix] + sm[at, :] * va[ix]
        for part in range(2):
            at = pl.ds(256 * part, 256)
            rr[at, :] = rr[at, :] + right_apply(lz, 1, s3[at, :])
        sums = [None] * (C + 2)

        def result(ix):
            r2 = mix_lines(TABLE.T, [f2[block(8 * ix + iy), :] for iy in range(8)])
            out = []
            for iy in range(8):
                at = block(8 * ix + iy)
                out.append(r2[iy] + rr[at, :])
                v = vecs[u + C, at, :]
                terms = [v * out[iy], vecs[u, at, :] * out[iy]]
                terms += [v * inp[j, at, :] for j in range(C)]
                for m, t in enumerate(terms):
                    sums[m] = t if sums[m] is None else sums[m] + t
            return out

        if final:
            for ix in range(8):
                result(ix)
        else:
            fold(c, result)
        for m in range(C + 2):
            acc[(k * (C + 2) + m) * C + c] = sums[m]
        if not final:
            send(c, (k % 2) * C + c)

            @pl.when(k == 0)
            def _():
                g = None
                for ix in range(8):
                    for iy in range(8):
                        t = vecs[u + C, block(8 * ix + iy), :] * raw(LOADS + c, ix, iy)
                        g = t if g is None else g + t
                acc[C + c] = g

        return carry

    lax.fori_loop(0, (STEPS - 1) * C, functools.partial(unit, False), 0)
    lax.fori_loop((STEPS - 1) * C, STEPS * C, functools.partial(unit, True), 0)

    for q in range(STEPS * (C + 2) * C):
        rows[q : q + 1, :] = jnp.sum(acc[q], axis=0, keepdims=True)
    part = jnp.sum(rows[...].T, axis=0, keepdims=True)
    asend[...] = part
    arecv[me] = part

    def reduce_copy(i, slot):
        return pltpu.make_async_remote_copy(
            src_ref=asend,
            dst_ref=arecv.at[slot],
            send_sem=sendr.at[i],
            recv_sem=recvr.at[slot],
            device_id=coords(lax.rem(me + i, N)),
            device_id_type=MESH,
        )

    def push(i, carry):
        reduce_copy(i, me).start()
        return carry

    lax.fori_loop(1, N, push, 0)
    line_of = collect(C + 1, 2 * C + 1)
    for ix in range(8):
        for iy, v in enumerate(line_of(ix)):
            mts[block(8 * ix + iy), :] = v

    def arrive(i, carry):
        reduce_copy(i, lax.rem(me + i, N)).wait_recv()
        return carry

    lax.fori_loop(1, N, arrive, 0)
    total = jnp.sum(arecv[...], axis=0)

    def entry(k, m):
        q = (128 - (k * (C + 2) + m) * C) % 128
        return pltpu.roll(total, q, 1) if q else total

    G = [[None] * STEPS for _ in range(STEPS)]
    for k in range(STEPS):
        G[k][k] = entry(k, 0)
        if k:
            G[k - 1][k] = entry(k, 1)
    g = [entry(0, 1)]
    for gap in range(2, STEPS):
        for i in range(STEPS - gap):
            j = i + gap - 1
            G[i][j + 1] = G[i + 1][j] + float(THETA[i] - THETA[j]) * G[i][j]
    for i in range(1, STEPS):
        g.append(G[0][i - 1] - float(THETA[i - 1]) * g[i - 1])
    L = [[None] * STEPS for _ in range(STEPS)]
    inv = []
    for j in range(STEPS):
        lines = []
        for i in range(j, STEPS):
            t = G[j][i]
            for q in range(j):
                t = t - L[i][q] * lower[q][j]
            lines.append(t)
        if j == 0:
            lower = []
        lower.append([None] * j + lines)
        inv.append(1.0 / lines[0])
        for i in range(j + 1, STEPS):
            L[i][j] = lines[i - j] * inv[j]
    y = list(g)
    for i in range(STEPS):
        for q in range(i):
            y[i] = y[i] - L[i][q] * y[q]
    y = [t * d for t, d in zip(y, inv)]
    for i in reversed(range(STEPS)):
        for q in range(i + 1, STEPS):
            y[i] = y[i] - L[q][i] * y[q]
    couple = []
    for j in range(C):
        t = y[0] * entry(0, 2 + j)
        for k in range(1, STEPS):
            t = t + y[k] * entry(k, 2 + j)
        couple.append(t)

    def spread(line, c):
        return jnp.broadcast_to(line[:, c : c + 1], (8, Z))

    kk = [[spread(couple[j], c) for j in range(C)] for c in range(C)]
    ymat = [[None] * C for _ in range(C)]
    for a in range(C):
        for b in range(C):
            if b < a:
                ymat[a][b] = ymat[b][a]
                continue
            t = kk[a][0] * kk[b][0]
            for j in range(1, C):
                t = t + kk[a][j] * kk[b][j]
            ymat[a][b] = t + 1.0 if a == b else t
    one = jnp.ones((8, Z), F32)
    nil = jnp.zeros((8, Z), F32)
    right = [[one if a == b else nil for b in range(C)] + kk[a] for a in range(C)]
    for a in range(C):
        scale = 1.0 / ymat[a][a]
        ymat[a] = [t * scale for t in ymat[a]]
        right[a] = [t * scale for t in right[a]]
        for b in range(C):
            if b != a:
                q = ymat[b][a]
                ymat[b] = [t - q * s for t, s in zip(ymat[b], ymat[a])]
                right[b] = [t - q * s for t, s in zip(right[b], right[a])]
    coef = [[2.0 * right[c][j] for j in range(2 * C)] for c in range(C)]
    mixing = [[spread(y[k], c) for k in range(STEPS)] for c in range(C)]

    for ix in range(8):
        for iy in range(8):
            at = block(8 * ix + iy)
            m = mts[at, :]
            heat = []
            for c in range(C):
                t = mixing[c][0] * vecs[C + c, at, :]
                for k in range(1, STEPS):
                    t = t + mixing[c][k] * vecs[(k + 1) * C + c, at, :]
                heat.append(m * t)
            for j in range(C):
                t = heat[0] * coef[0][j]
                s = heat[0] * coef[0][C + j]
                for c in range(1, C):
                    t = t + heat[c] * coef[c][j]
                    s = s + heat[c] * coef[c][C + j]
                to = pl.ds(iy, 8, stride=8)
                ostage[j, ix, to, :] = rhs[j, at, :] - t
                ostage[C + j, ix, to, :] = s

    def store(q, e):
        return pltpu.make_async_copy(
            ostage.at[pl.ds(C * q, C), :, pl.ds(Y * e, Y)],
            (rf, fb)[q].at[:, pl.ds(8 * e, 8)],
            outsem.at[q, e],
        )

    for q in range(2):
        for e in range(E):
            store(q, e).start()

    def depart(i, carry):
        reduce_copy(i, me).wait_send()
        return carry

    lax.fori_loop(1, N, depart, 0)
    for q in range(2):
        for e in range(E):
            store(q, e).wait()


def local(counts, metric, mass, shift, loads, inputs):
    C, X, Y, Z = loads.shape
    E, F = X // 8, Y // 8
    assert E * F == 8 and Z >= 128 and STEPS * (C + 2) * C <= 128
    N = counts[0] * counts[1] * counts[2]
    lz = jnp.asarray(right_matrices(Z))
    vm = lambda *shape: pltpu.VMEM(shape, F32)
    dma = pltpu.SemaphoreType.DMA
    anywhere = pl.BlockSpec(memory_space=pl.ANY)
    return pl.pallas_call(
        functools.partial(kernel, (C, X, Y, Z), counts),
        out_shape=[jax.ShapeDtypeStruct(loads.shape, F32)] * 2,
        in_specs=[anywhere, anywhere, pl.BlockSpec(memory_space=pltpu.SMEM), anywhere, anywhere,
                  pl.BlockSpec(memory_space=pltpu.VMEM)],
        out_specs=[anywhere, anywhere],
        scratch_shapes=[
            vm(2 * C + 7, 8, 64, Z), vm(2 * C, 8, 64, Z), vm(6, 512, Z), vm(C, 512, Z),
            vm((STEPS + 1) * C, 512, Z), vm(C + 2, 512, Z), vm(512, Z), vm(512, Z),
            vm(C + 1, 512, Z), vm(512, Z), vm(512, Z), vm(512, Z), vm(512, Z), vm(512, Z),
            vm(128, 8, Z), vm(128, Z),
            vm(C + 2, 2, 64 // E, Z), vm(2 * C + 2, 2, 64 // E, Z),
            vm(C + 2, 2, 64 // F, Z), vm(2 * C + 2, 2, 64 // F, Z),
            vm(2 * C + 2, 4, 8, Z), vm(C + 2, 8, Z), vm(2 * C + 2, 2, 9, 8, Z),
            vm(1, 128), vm(N, 1, 128),
            dma((4, E)), dma((2, E)), dma((C + 2, 26)), dma((2 * C + 2, 26)), dma((N,)), dma((N,)),
        ],
        compiler_params=pltpu.CompilerParams(
            collective_id=0, has_side_effects=True, vmem_limit_bytes=56 << 20
        ),
    )(metric, mass, shift, loads, inputs, lz)


def solution(mesh):
    counts = tuple(mesh.shape[a] for a in ("gx", "gy", "gz"))
    return jax.shard_map(
        functools.partial(local, counts),
        mesh=mesh,
        in_specs=(
            P(None, "gx", "gy", "gz"),
            P("gx", "gy", "gz"),
            P(),
            P(None, "gx", "gy", "gz"),
            P(None, "gx", "gy", "gz"),
        ),
        out_specs=(P(None, "gx", "gy", "gz"), P(None, "gx", "gy", "gz")),
        check_vma=False,
    )
```

```python
import functools

import jax
import jax.numpy as jnp
import numpy as np
from jax import lax
from jax.experimental import pallas as pl
from jax.experimental.pallas import tpu as pltpu
from jax.sharding import PartitionSpec as P

STEPS = 5
THETA = (1.25, 0.2, 2.3, 0.7)
MESH = pl.DeviceIdType.MESH
F32 = jnp.float32
BF16 = jnp.bfloat16

gll_points = (
    -1.0,
    -0.8717401485096066,
    -0.5917001814331423,
    -0.2092992179024789,
    0.2092992179024789,
    0.5917001814331423,
    0.8717401485096066,
    1.0,
)


def gll_table():
    points = np.array(gll_points)
    values = (429.0 * points**7 - 693.0 * points**5 + 315.0 * points**3 - 35.0 * points) / 16.0
    table = np.zeros((8, 8))
    for row in range(8):
        for column in range(8):
            if row != column:
                table[row, column] = values[row] / (values[column] * (points[row] - points[column]))
    table[0, 0] = -14.0
    table[7, 7] = 14.0
    return table


TABLE = gll_table()
SQUARES = TABLE * TABLE


def halves(matrix):
    full = np.asarray(matrix, np.float32)
    high = full.astype(jnp.bfloat16)
    low = (full - high.astype(np.float32)).astype(jnp.bfloat16)
    return high, low


def right_matrices(depth):
    eye = np.eye(depth // 8)
    out = []
    for m in (TABLE.T, TABLE, SQUARES):
        high, low = halves(np.kron(eye, m))
        out.append(np.block([[high, low], [high, np.zeros_like(low)]]))
    return np.stack(out)


def mix_lines(matrix, lines, even_matrix=False):
    even = [lines[j] + lines[7 - j] for j in range(4)]
    odd = [lines[j] - lines[7 - j] for j in range(4)]
    out = [None] * 8
    for i in range(4):
        p = q = None
        for j in range(4):
            a = float(np.float32(0.5 * (matrix[i, j] + matrix[i, 7 - j])))
            b = float(np.float32(0.5 * (matrix[i, j] - matrix[i, 7 - j])))
            p = a * even[j] if p is None else p + a * even[j]
            q = b * odd[j] if q is None else q + b * odd[j]
        out[i] = q + p
        out[7 - i] = p - q if even_matrix else q - p
    return out


def right_apply(lz, kind, v):
    high = v.astype(BF16)
    low = (v - high.astype(F32)).astype(BF16)
    depth = v.shape[1]
    both = jnp.dot(
        jnp.concatenate([high, low], axis=1), lz[kind], preferred_element_type=F32
    )
    return both[:, :depth] + both[:, depth:]


def kernel(
    dims, counts,
    metric, mass, shift, loads, inputs, lz,
    rf, fb,
    stage, ostage, met, inp, vecs, w, pre, mts, rhs, sm, s2, s3, f2, rr, acc, rows,
    xs, xr, ys, yr, er, zs, zr, asend, arecv,
    insem, outsem, ssem, rsem, sendr, recvr,
):
    C, X, Y, Z = dims
    nx, ny, nz = counts
    N = nx * ny * nz
    E, F = X // 8, Y // 8
    LOADS, MASS, METRIC, INPUTS = 0, C, C + 1, C + 7
    gx, gy, gz = lax.axis_index("gx"), lax.axis_index("gy"), lax.axis_index("gz")
    me = (gx * ny + gy) * nz + gz
    sh = shift[0]

    def block(n):
        return pl.ds(8 * n, 8)

    sources = (
        (loads, LOADS, C), (mass, MASS, 1), (metric, METRIC, 6), (inputs, INPUTS, C),
    )

    def fetch(q, e):
        ref, first, count = sources[q]
        if q == 1:
            src = ref.at[pl.ds(8 * e, 8)]
            dst = stage.at[first, :, pl.ds(Y * e, Y)]
        else:
            src = ref.at[:, pl.ds(8 * e, 8)]
            dst = stage.at[pl.ds(first, count), :, pl.ds(Y * e, Y)]
        return pltpu.make_async_copy(src, dst, insem.at[q, e])

    for q in range(4):
        for e in range(E):
            fetch(q, e).start()

    def coords(number):
        rest = lax.div(number, nz)
        return (lax.div(rest, ny), lax.rem(rest, ny), lax.rem(number, nz))

    for ref in (xr, yr, er, zr):
        ref[...] = jnp.zeros(ref.shape, F32)
    def raw(f, ix, iy):
        return stage[f, ix, pl.ds(iy, 8, stride=8), :]

    lane = lax.broadcasted_iota(jnp.int32, (8, Z), 1)
    sub = lax.broadcasted_iota(jnp.int32, (8, Z), 0)
    ye = sub % F
    inner0 = (lane % 8 == 0) & (lane > 0)
    inner7 = (lane % 8 == 7) & (lane < Z - 1)
    rim = (lane == 0) | (lane == Z - 1)
    slot_of_lane = ((lane + 1) % Z) // 2
    ix_of_lane, iy_of_lane = slot_of_lane // 8, slot_of_lane % 8

    xe = sub // F
    weight_x = [
        jnp.where((xe > 0) | (gx > 0), 0.5, 1.0), jnp.where((xe < E - 1) | (gx < nx - 1), 0.5, 1.0)
    ]
    weight_y = [
        jnp.where((ye > 0) | (gy > 0), 0.5, 1.0), jnp.where((ye < F - 1) | (gy < ny - 1), 0.5, 1.0)
    ]
    weight_z = jnp.where(
        ((lane % 8 == 0) & ((lane > 0) | (gz > 0)))
        | ((lane % 8 == 7) & ((lane < Z - 1) | (gz < nz - 1))),
        0.5, 1.0,
    )

    def corner(hx, hy):
        return hx * (8 - F) + hy * (F - 1)

    if nz == 2:
        z_steps = [(1 - 2 * gz, None, None, 0)]
    else:
        z_steps = [(-1, gz > 0, gz < nz - 1, 1), (1, gz < nz - 1, gz > 0, 0)]
    columns = [(dx, dy) for dx in (-1, 0, 1) for dy in (-1, 0, 1)]

    def there(dx, dy):
        ok = None
        for place, step, count in zip((gx, gy), (dx, dy), (nx, ny)):
            if step:
                one = place > 0 if step < 0 else place < count - 1
                ok = one if ok is None else ok & one
        return ok

    def under(test, act):
        if test is None:
            act()
        else:
            pl.when(test)(act)

    def both_tests(a, b):
        return b if a is None else a if b is None else a & b

    def towards(act):
        for dx, dy in columns:
            def group(dx=dx, dy=dy):
                if dx or dy:
                    act(dx, dy, None)
                for q, step in enumerate(z_steps):
                    under(step[1], functools.partial(act, dx, dy, q))
            under(there(dx, dy), group)

    def backwards(act):
        for dx, dy in columns:
            def group(dx=dx, dy=dy):
                if dx or dy:
                    act(dx, dy, None)
                for q, step in enumerate(z_steps):
                    under(step[2], functools.partial(act, dx, dy, q))
            under(there(-dx, -dy), group)

    barrier = pltpu.get_barrier_semaphore()
    if max(counts) - 1 <= STEPS:
        greeted = jnp.int32(0)
        for dx, dy in columns:
            for step in [None] + z_steps:
                test = there(dx, dy)
                if step is None and test is None:
                    continue
                if step is not None:
                    test = both_tests(test, step[1])
                greeted = greeted + (1 if test is None else test.astype(jnp.int32))

        def signal(dx, dy, q):
            dz = 0 if q is None else z_steps[q][0]
            pl.semaphore_signal(
                barrier, inc=1, device_id=(gx + dx, gy + dy, gz + dz), device_id_type=MESH
            )

        towards(signal)
    else:
        greeted = N - 1

        def greet(i, carry):
            pl.semaphore_signal(
                barrier, inc=1, device_id=coords(lax.rem(me + i, N)), device_id_type=MESH
            )
            return carry

        lax.fori_loop(1, N, greet, 0)

    def message(dx, dy, q, sslot, rslot):
        hx, hy = (dx + 1) // 2, (dy + 1) // 2
        i = 3 * (dx + 1) + dy + 1
        if q is None:
            dz = 0
            if dy == 0:
                src, dst = xs.at[sslot, hx], xr.at[rslot, 1 - hx]
            elif dx == 0:
                src, dst = ys.at[sslot, hy], yr.at[rslot, 1 - hy]
            else:
                row = 8 * (56 * hx + 7 * hy) + corner(hx, hy)
                src = w.at[sslot, pl.ds(row, 1)]
                dst = er.at[rslot, 2 * (1 - hx) + (1 - hy), pl.ds(corner(1 - hx, 1 - hy), 1)]
        else:
            dz, _, _, side = z_steps[q]
            if dx and dy:
                a, b, count = corner(hx, hy), corner(1 - hx, 1 - hy), 1
            elif dx:
                a, b, count = hx * (8 - F), (1 - hx) * (8 - F), F
            else:
                a, b, count = 0, 0, 8
            src = zs.at[sslot, pl.ds(a, count)]
            dst = zr.at[rslot, side, 8 - i, pl.ds(b, count)]
            i = 9 * (q + 1) + i
        return pltpu.make_async_remote_copy(
            src_ref=src,
            dst_ref=dst,
            send_sem=ssem.at[sslot, i],
            recv_sem=rsem.at[rslot, i],
            device_id=(gx + dx, gy + dy, gz + dz),
            device_id_type=MESH,
        )

    def fold(a, line_of):
        def along_y(line):
            v0, v7 = line[0], line[7]
            line = list(line)
            line[0] = v0 + jnp.where(ye > 0, pltpu.roll(v7, 1, 0), 0.0)
            line[7] = v7 + jnp.where(ye < F - 1, pltpu.roll(v0, 7, 0), 0.0)
            return line

        first, last = along_y(line_of(0)), along_y(line_of(7))
        lines = {
            0: [
                v + jnp.where(sub >= F, pltpu.roll(t, F, 0), 0.0) for v, t in zip(first, last)
            ],
            7: [
                t + jnp.where(sub < 8 - F, pltpu.roll(v, 8 - F, 0), 0.0)
                for v, t in zip(first, last)
            ],
        }
        packed = jnp.zeros((8, Z), F32)
        faces = [[None] * (8 // F) for _ in range(2)]
        for ix in (0, 7, 1, 2, 3, 4, 5, 6):
            line = lines[ix] if ix in lines else along_y(line_of(ix))
            ups = [pltpu.roll(v, 1, 1) for v in line]
            downs = [pltpu.roll(v, Z - 1, 1) for v in line]
            line = [
                v + jnp.where(inner0, p, jnp.where(inner7, q, 0.0))
                for v, p, q in zip(line, ups, downs)
            ]
            for iy in range(8):
                n = 8 * ix + iy
                w[a, block(n), :] = line[iy]
                moved = pltpu.roll(line[iy], 2 * n, 1) if n else line[iy]
                packed = jnp.where(slot_of_lane == n, moved, packed)
            if ix in (0, 7):
                h = ix // 7
                for j in range(8 // E):
                    out = None
                    for g in range(E):
                        v = line[j * E + g]
                        q = (g * F + h * F) % 8
                        v = pltpu.roll(v, q, 0) if q else v
                        out = v if out is None else jnp.where(sub // F == g, v, out)
                    xs[a, h, 8 * j : 8 * j + 8, :] = out
            for h in range(2):
                j, g = ix // F, ix % F
                v = line[7 * h]
                q = (g - h * (F - 1)) % 8
                v = pltpu.roll(v, q, 0) if q else v
                old = faces[h][j]
                faces[h][j] = v if old is None else jnp.where(ye == g, v, old)
        zs[a] = packed
        for h in range(2):
            for j in range(8 // F):
                ys[a, h, 8 * j : 8 * j + 8, :] = faces[h][j]

    def send(a, rslot):
        towards(lambda dx, dy, q: message(dx, dy, q, a, rslot).start())

    def collect(a, rslot):
        backwards(lambda dx, dy, q: message(dx, dy, q, a, rslot).wait_recv())
        towards(lambda dx, dy, q: message(dx, dy, q, a, rslot).wait_send())
        sides = []
        for h in range(len(z_steps)):
            total = zr[rslot, h, 4]
            for dx in (-1, 0, 1):
                for dy in (-1, 0, 1):
                    if dx == 0 and dy == 0:
                        continue
                    v = zr[rslot, h, 3 * (dx + 1) + dy + 1]
                    if dx == 0:
                        v = pltpu.roll(v, (dy * (F - 1)) % 8, 0)
                    v = pltpu.roll(v, (2 * (56 * dx + 7 * dy)) % Z, 1)
                    mask = None
                    if dx:
                        mask = ix_of_lane == (7 if dx > 0 else 0)
                    if dy:
                        more = iy_of_lane == (7 if dy > 0 else 0)
                        mask = more if mask is None else mask & more
                    if dx == 0:
                        mask = mask & (ye == (F - 1 if dy > 0 else 0))
                    total = total + jnp.where(mask, v, 0.0)
            sides.append(total)
        if nz == 2:
            sides = [jnp.where(gz > 0, sides[0], 0.0), jnp.where(gz > 0, 0.0, sides[0])]
        both = jnp.where(
            lane % 2 == 0, pltpu.roll(sides[0], 1, 1), pltpu.roll(sides[1], Z - 1, 1)
        )

        def line_of(ix):
            line = []
            for iy in range(8):
                n = 8 * ix + iy
                v = pltpu.roll(both, (Z - 2 * n) % Z, 1) if n else both
                line.append(w[a, block(n), :] + jnp.where(rim, v, 0.0))
            if ix in (0, 7):
                h = ix // 7
                for iy in range(8):
                    j, g = iy // E, iy % E
                    v = xr[rslot, h, 8 * j : 8 * j + 8, :]
                    q = (h * (8 - F) - g * F) % 8
                    v = pltpu.roll(v, q, 0) if q else v
                    mask = sub >= 8 - F if h else sub < F
                    line[iy] = line[iy] + jnp.where(mask, v, 0.0)
                for hy in range(2):
                    line[7 * hy] = line[7 * hy] + er[rslot, 2 * h + hy]
            for h in range(2):
                j, g = ix // F, ix % F
                v = yr[rslot, h, 8 * j : 8 * j + 8, :]
                q = (h * (F - 1) - g) % 8
                v = pltpu.roll(v, q, 0) if q else v
                line[7 * h] = line[7 * h] + jnp.where(ye == h * (F - 1), v, 0.0)
            return line

        return line_of

    for e in range(E):
        fetch(0, e).wait()
    def fold_load(c, carry):
        fold(c, lambda ix: [raw(LOADS + c, ix, iy) for iy in range(8)])
        return carry

    lax.fori_loop(0, C, fold_load, 0)
    for q in (1, 2):
        for e in range(E):
            fetch(q, e).wait()
    for ix in range(8):
        for iy in range(8):
            at = block(8 * ix + iy)
            sm[at, :] = sh * raw(MASS, ix, iy)
            for f in range(6):
                met[f, at, :] = raw(METRIC + f, ix, iy)
    for part in range(2):
        at = pl.ds(256 * part, 256)
        s3[at, :] = right_apply(lz, 2, met[2, at, :])
    for ix in range(8):
        line = mix_lines(SQUARES.T, [met[1, block(8 * ix + iy), :] for iy in range(8)], True)
        for iy in range(8):
            s2[block(8 * ix + iy), :] = line[iy]
    ends = (-14.0,) + (0.0,) * 6 + (14.0,)
    ends_z = jnp.where(lane % 8 == 0, -14.0, jnp.where(lane % 8 == 7, 14.0, 0.0))
    for iy in range(8):
        line = mix_lines(SQUARES.T, [met[0, block(8 * ix + iy), :] for ix in range(8)], True)
        for ix in range(8):
            at = block(8 * ix + iy)
            total = line[ix] + s2[at, :] + s3[at, :] + sm[at, :]
            if ends[ix] and ends[iy]:
                total = total + (2.0 * ends[ix] * ends[iy]) * met[3, at, :]
            if ends[ix]:
                total = total + (2.0 * ends[ix]) * (ends_z * met[4, at, :])
            if ends[iy]:
                total = total + (2.0 * ends[iy]) * (ends_z * met[5, at, :])
            rr[at, :] = total

    def lines_in(ref):
        return lambda ix: [ref[block(8 * ix + iy), :] for iy in range(8)]

    fold(C, lines_in(rr))
    fold(C + 1, lines_in(sm))
    for c in range(C):
        vecs[c] = jnp.zeros((512, Z), F32)
    acc[...] = jnp.zeros(acc.shape, F32)
    rows[...] = jnp.zeros(rows.shape, F32)

    pl.semaphore_wait(barrier, greeted)
    for a in (C,) + tuple(range(C)) + (C + 1,):
        send(a, C + a)

    for e in range(E):
        fetch(3, e).wait()
    for j in range(C):
        for ix in range(8):
            for iy in range(8):
                inp[j, block(8 * ix + iy), :] = raw(INPUTS + j, ix, iy)

    line_of = collect(C, 2 * C)
    for ix in range(8):
        for iy, v in enumerate(line_of(ix)):
            pre[block(8 * ix + iy), :] = 1.0 / v

    def unit(final, u, carry):
        k = u // C
        c = u % C
        theta = jnp.where(
            k == 0, 0.0,
            jnp.where(k == 1, THETA[0], jnp.where(k == 2, THETA[1], jnp.where(k == 3, THETA[2], THETA[3]))),
        ).astype(F32)
        line_of = collect(c, ((k + 1) % 2) * C + c)
        keep = ((k + STEPS - 1) // STEPS) * (C - c) + c
        shared = [[None] * 3 for _ in range(3)]
        sums = [None] * (C + 2)

        def add(old, t):
            return t if old is None else old + t

        for ix in range(8):
            line = line_of(ix)
            before = [vecs[u, block(8 * ix + iy), :] for iy in range(8)]
            scale = [pre[block(8 * ix + iy), :] for iy in range(8)]
            fresh = [p * t - theta * b for p, t, b in zip(scale, line, before)]
            for iy in range(8):
                at = block(8 * ix + iy)
                v = fresh[iy]
                vecs[u + C, at, :] = v
                if not final:
                    rhs[keep, at, :] = line[iy]
                p, q = (ix > 0) + (ix == 7), (iy > 0) + (iy == 7)
                shared[p][q] = add(shared[p][q], v * line[iy])
                for j in range(C):
                    sums[2 + j] = add(sums[2 + j], v * inp[j, at, :])
        for p in range(3):
            for q in range(3):
                t = shared[p][q]
                if p != 1:
                    t = t * weight_x[p // 2]
                if q != 1:
                    t = t * weight_y[q // 2]
                sums[1] = add(sums[1], t)
        sums[1] = sums[1] * weight_z

        for part in range(2):
            at = pl.ds(256 * part, 256)
            s3[at, :] = right_apply(lz, 0, vecs[u + C, at, :])
        for ix in range(8):
            line = mix_lines(TABLE, [vecs[u + C, block(8 * ix + iy), :] for iy in range(8)])
            for iy in range(8):
                s2[block(8 * ix + iy), :] = line[iy]
        for iy in range(8):
            va = [vecs[u + C, block(8 * ix + iy), :] for ix in range(8)]
            s1 = mix_lines(TABLE, va)
            f1 = []
            for ix in range(8):
                at = block(8 * ix + iy)
                a, b, g = s1[ix], s2[at, :], s3[at, :]
                m12, m13, m23 = met[3, at, :], met[4, at, :], met[5, at, :]
                if final:
                    t = m12 * b + m13 * g
                    q = m23 * g
                    t = a * (met[0, at, :] * a + (t + t)) + b * (met[1, at, :] * b + (q + q))
                    t = t + g * (met[2, at, :] * g) + va[ix] * (sm[at, :] * va[ix])
                    sums[0] = add(sums[0], t)
                    continue
                f1.append(met[0, at, :] * a + m12 * b + m13 * g)
                f2[at, :] = m12 * a + met[1, at, :] * b + m23 * g
                s3[at, :] = m13 * a + m23 * b + met[2, at, :] * g
            if final:
                continue
            r1 = mix_lines(TABLE.T, f1)
            for ix in range(8):
                at = block(8 * ix + iy)
                rr[at, :] = r1[ix] + sm[at, :] * va[ix]
        def result(ix):
            r2 = mix_lines(TABLE.T, [f2[block(8 * ix + iy), :] for iy in range(8)])
            out = []
            for iy in range(8):
                at = block(8 * ix + iy)
                out.append(r2[iy] + rr[at, :])
                sums[0] = add(sums[0], vecs[u + C, at, :] * out[iy])
            return out

        if not final:
            for part in range(2):
                at = pl.ds(256 * part, 256)
                rr[at, :] = rr[at, :] + right_apply(lz, 1, s3[at, :])
            fold(c, result)
        for m in range(C + 2):
            acc[(k * (C + 2) + m) * C + c] = sums[m]
        if not final:
            send(c, (k % 2) * C + c)
        return carry

    lax.fori_loop(0, (STEPS - 1) * C, functools.partial(unit, False), 0)
    lax.fori_loop((STEPS - 1) * C, STEPS * C, functools.partial(unit, True), 0)

    for q in range(STEPS * (C + 2) * C):
        rows[q : q + 1, :] = jnp.sum(acc[q], axis=0, keepdims=True)
    part = jnp.sum(rows[...].T, axis=0, keepdims=True)
    asend[...] = part
    arecv[0] = part

    def around(place, step, count):
        moved = place + step
        return lax.select(moved >= count, moved - count, moved) if step else place

    for i in range(1, N):
        a, b, c = i // (ny * nz), i // nz % ny, i % nz
        pltpu.make_async_remote_copy(
            src_ref=asend,
            dst_ref=arecv.at[i],
            send_sem=sendr,
            recv_sem=recvr,
            device_id=(around(gx, a, nx), around(gy, b, ny), around(gz, c, nz)),
            device_id_type=MESH,
        ).start()
    line_of = collect(C + 1, 2 * C + 1)
    for ix in range(8):
        for iy, v in enumerate(line_of(ix)):
            mts[block(8 * ix + iy), :] = v

    others = arecv.at[pl.ds(1, N - 1)]
    pltpu.make_async_copy(others, others, recvr).wait()
    total = jnp.sum(arecv[...], axis=0)

    def entry(k, m):
        q = (128 - (k * (C + 2) + m) * C) % 128
        return pltpu.roll(total, q, 1) if q else total

    G = [[None] * STEPS for _ in range(STEPS)]
    for k in range(STEPS):
        G[k][k] = entry(k, 0)
        if k:
            G[k - 1][k] = entry(k, 1)
    g = [entry(0, 1)]
    for gap in range(2, STEPS):
        for i in range(STEPS - gap):
            j = i + gap - 1
            G[i][j + 1] = G[i + 1][j] + float(THETA[i] - THETA[j]) * G[i][j]
    for i in range(1, STEPS):
        g.append(G[0][i - 1] - float(THETA[i - 1]) * g[i - 1])
    L = [[None] * STEPS for _ in range(STEPS)]
    inv = []
    for j in range(STEPS):
        lines = []
        for i in range(j, STEPS):
            t = G[j][i]
            for q in range(j):
                t = t - L[i][q] * lower[q][j]
            lines.append(t)
        if j == 0:
            lower = []
        lower.append([None] * j + lines)
        inv.append(1.0 / lines[0])
        for i in range(j + 1, STEPS):
            L[i][j] = lines[i - j] * inv[j]
    y = list(g)
    for i in range(STEPS):
        for q in range(i):
            y[i] = y[i] - L[i][q] * y[q]
    y = [t * d for t, d in zip(y, inv)]
    for i in reversed(range(STEPS)):
        for q in range(i + 1, STEPS):
            y[i] = y[i] - L[q][i] * y[q]
    couple = []
    for j in range(C):
        t = y[0] * entry(0, 2 + j)
        for k in range(1, STEPS):
            t = t + y[k] * entry(k, 2 + j)
        couple.append(t)

    def spread(line, c):
        return jnp.broadcast_to(line[:, c : c + 1], (8, Z))

    kk = [[spread(couple[j], c) for j in range(C)] for c in range(C)]
    ymat = [[None] * C for _ in range(C)]
    for a in range(C):
        for b in range(C):
            if b < a:
                ymat[a][b] = ymat[b][a]
                continue
            t = kk[a][0] * kk[b][0]
            for j in range(1, C):
                t = t + kk[a][j] * kk[b][j]
            ymat[a][b] = t + 1.0 if a == b else t
    one = jnp.ones((8, Z), F32)
    nil = jnp.zeros((8, Z), F32)
    right = [[one if a == b else nil for b in range(C)] + kk[a] for a in range(C)]
    for a in range(C):
        scale = 1.0 / ymat[a][a]
        ymat[a] = [t * scale for t in ymat[a]]
        right[a] = [t * scale for t in right[a]]
        for b in range(C):
            if b != a:
                q = ymat[b][a]
                ymat[b] = [t - q * s for t, s in zip(ymat[b], ymat[a])]
                right[b] = [t - q * s for t, s in zip(right[b], right[a])]
    coef = [[2.0 * right[c][j] for j in range(2 * C)] for c in range(C)]
    mixing = [[spread(y[k], c) for k in range(STEPS)] for c in range(C)]

    for ix in range(8):
        for iy in range(8):
            at = block(8 * ix + iy)
            m = mts[at, :]
            heat = []
            for c in range(C):
                t = mixing[c][0] * vecs[C + c, at, :]
                for k in range(1, STEPS):
                    t = t + mixing[c][k] * vecs[(k + 1) * C + c, at, :]
                heat.append(m * t)
            for j in range(C):
                t = heat[0] * coef[0][j]
                s = heat[0] * coef[0][C + j]
                for c in range(1, C):
                    t = t + heat[c] * coef[c][j]
                    s = s + heat[c] * coef[c][C + j]
                to = pl.ds(iy, 8, stride=8)
                ostage[j, ix, to, :] = rhs[j, at, :] - t
                ostage[C + j, ix, to, :] = s

    def store(q, e):
        return pltpu.make_async_copy(
            ostage.at[pl.ds(C * q, C), :, pl.ds(Y * e, Y)],
            (rf, fb)[q].at[:, pl.ds(8 * e, 8)],
            outsem.at[q, e],
        )

    for q in range(2):
        for e in range(E):
            store(q, e).start()

    pltpu.make_async_copy(others, others, sendr).wait()
    for q in range(2):
        for e in range(E):
            store(q, e).wait()


def local(counts, metric, mass, shift, loads, inputs):
    C, X, Y, Z = loads.shape
    E, F = X // 8, Y // 8
    assert E * F == 8 and Z >= 128 and STEPS * (C + 2) * C <= 128
    N = counts[0] * counts[1] * counts[2]
    lz = jnp.asarray(right_matrices(Z))
    vm = lambda *shape: pltpu.VMEM(shape, F32)
    dma = pltpu.SemaphoreType.DMA
    anywhere = pl.BlockSpec(memory_space=pl.ANY)
    return pl.pallas_call(
        functools.partial(kernel, (C, X, Y, Z), counts),
        out_shape=[jax.ShapeDtypeStruct(loads.shape, F32)] * 2,
        in_specs=[anywhere, anywhere, pl.BlockSpec(memory_space=pltpu.SMEM), anywhere, anywhere,
                  pl.BlockSpec(memory_space=pltpu.VMEM)],
        out_specs=[anywhere, anywhere],
        scratch_shapes=[
            vm(2 * C + 7, 8, 64, Z), vm(2 * C, 8, 64, Z), vm(6, 512, Z), vm(C, 512, Z),
            vm((STEPS + 1) * C, 512, Z), vm(C + 2, 512, Z), vm(512, Z), vm(512, Z),
            vm(C + 1, 512, Z), vm(512, Z), vm(512, Z), vm(512, Z), vm(512, Z), vm(512, Z),
            vm(128, 8, Z), vm(128, Z),
            vm(C + 2, 2, 64 // E, Z), vm(2 * C + 2, 2, 64 // E, Z),
            vm(C + 2, 2, 64 // F, Z), vm(2 * C + 2, 2, 64 // F, Z),
            vm(2 * C + 2, 4, 8, Z), vm(C + 2, 8, Z), vm(2 * C + 2, 1 if counts[2] == 2 else 2, 9, 8, Z),
            vm(1, 128), vm(N, 1, 128),
            dma((4, E)), dma((2, E)), dma((C + 2, 27)), dma((2 * C + 2, 27)), dma, dma,
        ],
        compiler_params=pltpu.CompilerParams(
            collective_id=0, has_side_effects=True, vmem_limit_bytes=56 << 20
        ),
    )(metric, mass, shift, loads, inputs, lz)


def solution(mesh):
    counts = tuple(mesh.shape[a] for a in ("gx", "gy", "gz"))
    return jax.shard_map(
        functools.partial(local, counts),
        mesh=mesh,
        in_specs=(
            P(None, "gx", "gy", "gz"),
            P("gx", "gy", "gz"),
            P(),
            P(None, "gx", "gy", "gz"),
            P(None, "gx", "gy", "gz"),
        ),
        out_specs=(P(None, "gx", "gy", "gz"), P(None, "gx", "gy", "gz")),
        check_vma=False,
    )
```

```python
import functools

import jax
import jax.numpy as jnp
import numpy as np
from jax import lax
from jax.experimental import pallas as pl
from jax.experimental.pallas import tpu as pltpu
from jax.sharding import PartitionSpec as P

STEPS = 5
THETA = (1.25, 0.2, 2.3, 0.7)
MESH = pl.DeviceIdType.MESH
F32 = jnp.float32
BF16 = jnp.bfloat16

gll_points = (
    -1.0,
    -0.8717401485096066,
    -0.5917001814331423,
    -0.2092992179024789,
    0.2092992179024789,
    0.5917001814331423,
    0.8717401485096066,
    1.0,
)


def gll_table():
    points = np.array(gll_points)
    values = (429.0 * points**7 - 693.0 * points**5 + 315.0 * points**3 - 35.0 * points) / 16.0
    table = np.zeros((8, 8))
    for row in range(8):
        for column in range(8):
            if row != column:
                table[row, column] = values[row] / (values[column] * (points[row] - points[column]))
    table[0, 0] = -14.0
    table[7, 7] = 14.0
    return table


TABLE = gll_table()
SQUARES = TABLE * TABLE


def halves(matrix):
    full = np.asarray(matrix, np.float32)
    high = full.astype(jnp.bfloat16)
    low = (full - high.astype(np.float32)).astype(jnp.bfloat16)
    return high, low


def right_matrices(depth):
    eye = np.eye(depth // 8)
    out = []
    for m in (TABLE.T, TABLE, SQUARES):
        high, low = halves(np.kron(eye, m))
        out.append(np.block([[high, low], [high, np.zeros_like(low)]]))
    return np.stack(out)


def mix_lines(matrix, lines, even_matrix=False):
    even = [lines[j] + lines[7 - j] for j in range(4)]
    odd = [lines[j] - lines[7 - j] for j in range(4)]
    out = [None] * 8
    for i in range(4):
        p = q = None
        for j in range(4):
            a = float(np.float32(0.5 * (matrix[i, j] + matrix[i, 7 - j])))
            b = float(np.float32(0.5 * (matrix[i, j] - matrix[i, 7 - j])))
            p = a * even[j] if p is None else p + a * even[j]
            q = b * odd[j] if q is None else q + b * odd[j]
        out[i] = q + p
        out[7 - i] = p - q if even_matrix else q - p
    return out


def right_apply(lz, kind, v):
    high = v.astype(BF16)
    low = (v - high.astype(F32)).astype(BF16)
    depth = v.shape[1]
    both = jnp.dot(
        jnp.concatenate([high, low], axis=1), lz[kind], preferred_element_type=F32
    )
    return both[:, :depth] + both[:, depth:]


def kernel(
    dims, counts,
    metric, mass, shift, loads, inputs, lz,
    rf, fb,
    stage, ostage, met, inp, vecs, w, pre, mts, rhs, sm, s2, s3, f2, rr, acc, rows,
    xs, xr, ys, yr, er, zs, zr, asend, arecv,
    insem, outsem, ssem, rsem, sendr, recvr, besides,
):
    C, X, Y, Z = dims
    nx, ny, nz = counts
    N = nx * ny * nz
    E, F = X // 8, Y // 8
    LOADS, MASS, METRIC, INPUTS = 0, C, C + 1, C + 7
    gx, gy, gz = lax.axis_index("gx"), lax.axis_index("gy"), lax.axis_index("gz")
    me = (gx * ny + gy) * nz + gz
    sh = shift[0]

    def block(n):
        return pl.ds(8 * n, 8)

    sources = (
        (loads, LOADS, C), (mass, MASS, 1), (metric, METRIC, 6), (inputs, INPUTS, C),
    )

    def fetch(q, e):
        ref, first, count = sources[q]
        if q == 1:
            src = ref.at[pl.ds(8 * e, 8)]
            dst = stage.at[first, :, pl.ds(Y * e, Y)]
        else:
            src = ref.at[:, pl.ds(8 * e, 8)]
            dst = stage.at[pl.ds(first, count), :, pl.ds(Y * e, Y)]
        return pltpu.make_async_copy(src, dst, insem.at[q, e])

    for q in range(4):
        for e in range(E):
            fetch(q, e).start()

    def coords(number):
        rest = lax.div(number, nz)
        return (lax.div(rest, ny), lax.rem(rest, ny), lax.rem(number, nz))

    for ref in (xr, yr, er, zr):
        ref[...] = jnp.zeros(ref.shape, F32)
    def raw(f, ix, iy):
        return stage[f, ix, pl.ds(iy, 8, stride=8), :]

    lane = lax.broadcasted_iota(jnp.int32, (8, Z), 1)
    sub = lax.broadcasted_iota(jnp.int32, (8, Z), 0)
    ye = sub % F
    inner0 = (lane % 8 == 0) & (lane > 0)
    inner7 = (lane % 8 == 7) & (lane < Z - 1)
    inner = inner0 | inner7
    across = jnp.where(inner0, lane - 1, jnp.where(inner7, lane + 1, lane))
    across = jnp.where((lane == 0) | (lane == Z - 2), Z - 1, across)
    across = jnp.where((lane == 1) | (lane == Z - 1), 0, across)
    rim = (lane == 0) | (lane == Z - 1)
    slot_of_lane = lane // 2
    ix_of_lane, iy_of_lane = slot_of_lane // 8, slot_of_lane % 8

    xe = sub // F
    weight_x = [
        jnp.where((xe > 0) | (gx > 0), 0.5, 1.0), jnp.where((xe < E - 1) | (gx < nx - 1), 0.5, 1.0)
    ]
    weight_y = [
        jnp.where((ye > 0) | (gy > 0), 0.5, 1.0), jnp.where((ye < F - 1) | (gy < ny - 1), 0.5, 1.0)
    ]
    weight_z = jnp.where(
        ((lane % 8 == 0) & ((lane > 0) | (gz > 0)))
        | ((lane % 8 == 7) & ((lane < Z - 1) | (gz < nz - 1))),
        0.5, 1.0,
    )

    def corner(hx, hy):
        return hx * (8 - F) + hy * (F - 1)

    if nz == 2:
        z_steps = [(1 - 2 * gz, None, None, 0)]
    else:
        z_steps = [(-1, gz > 0, gz < nz - 1, 1), (1, gz < nz - 1, gz > 0, 0)]
    columns = [(dx, dy) for dx in (-1, 0, 1) for dy in (-1, 0, 1)]

    def there(dx, dy):
        ok = None
        for place, step, count in zip((gx, gy), (dx, dy), (nx, ny)):
            if step:
                one = place > 0 if step < 0 else place < count - 1
                ok = one if ok is None else ok & one
        return ok

    def under(test, act):
        if test is None:
            act()
        else:
            pl.when(test)(act)

    def both_tests(a, b):
        return b if a is None else a if b is None else a & b

    def towards(act):
        for dx, dy in columns:
            def group(dx=dx, dy=dy):
                if dx or dy:
                    act(dx, dy, None)
                for q, step in enumerate(z_steps):
                    under(step[1], functools.partial(act, dx, dy, q))
            under(there(dx, dy), group)

    def backwards(act):
        for dx, dy in columns:
            def group(dx=dx, dy=dy):
                if dx or dy:
                    act(dx, dy, None)
                for q, step in enumerate(z_steps):
                    under(step[2], functools.partial(act, dx, dy, q))
            under(there(-dx, -dy), group)

    barrier = pltpu.get_barrier_semaphore()
    if max(counts) - 1 <= STEPS:
        greeted = jnp.int32(0)
        for dx, dy in columns:
            test = there(dx, dy)
            if test is not None:
                greeted = greeted + test.astype(jnp.int32)
        for step in z_steps:
            greeted = greeted + (1 if step[1] is None else step[1].astype(jnp.int32))

        def signal(dx, dy, q, sem):
            dz = 0 if q is None else z_steps[q][0]
            pl.semaphore_signal(
                sem, inc=1, device_id=(gx + dx, gy + dy, gz + dz), device_id_type=MESH
            )

        for dx, dy in columns:
            if dx or dy:
                under(there(dx, dy), functools.partial(signal, dx, dy, None, barrier))
        for q, step in enumerate(z_steps):
            under(step[1], functools.partial(signal, 0, 0, q, barrier))
    else:
        greeted = N - 1

        def greet(i, carry):
            pl.semaphore_signal(
                barrier, inc=1, device_id=coords(lax.rem(me + i, N)), device_id_type=MESH
            )
            return carry

        lax.fori_loop(1, N, greet, 0)

    def message(dx, dy, q, sslot, rslot):
        hx, hy = (dx + 1) // 2, (dy + 1) // 2
        i = 3 * (dx + 1) + dy + 1
        if q is None:
            dz = 0
            if dy == 0:
                src, dst = xs.at[sslot, hx], xr.at[rslot, 1 - hx]
            elif dx == 0:
                src, dst = ys.at[sslot, hy], yr.at[rslot, 1 - hy]
            else:
                row = 8 * (56 * hx + 7 * hy) + corner(hx, hy)
                src = w.at[sslot, pl.ds(row, 1)]
                dst = er.at[rslot, 2 * (1 - hx) + (1 - hy), pl.ds(corner(1 - hx, 1 - hy), 1)]
        else:
            dz, _, _, side = z_steps[q]
            if dx and dy:
                a, b, count = corner(hx, hy), corner(1 - hx, 1 - hy), 1
            elif dx:
                a, b, count = hx * (8 - F), (1 - hx) * (8 - F), F
            else:
                a, b, count = 0, 0, 8
            src = zs.at[sslot, pl.ds(a, count)]
            dst = zr.at[rslot, side, 8 - i, pl.ds(b, count)]
            i = 9 * (q + 1) + i
        return pltpu.make_async_remote_copy(
            src_ref=src,
            dst_ref=dst,
            send_sem=ssem.at[sslot, i],
            recv_sem=rsem.at[rslot, i],
            device_id=(gx + dx, gy + dy, gz + dz),
            device_id_type=MESH,
        )

    def fold(a, line_of):
        def along_y(line):
            v0, v7 = line[0], line[7]
            line = list(line)
            line[0] = v0 + jnp.where(ye > 0, pltpu.roll(v7, 1, 0), 0.0)
            line[7] = v7 + jnp.where(ye < F - 1, pltpu.roll(v0, 7, 0), 0.0)
            return line

        first, last = along_y(line_of(0)), along_y(line_of(7))
        lines = {
            0: [
                v + jnp.where(sub >= F, pltpu.roll(t, F, 0), 0.0) for v, t in zip(first, last)
            ],
            7: [
                t + jnp.where(sub < 8 - F, pltpu.roll(v, 8 - F, 0), 0.0)
                for v, t in zip(first, last)
            ],
        }
        packed = jnp.zeros((8, Z), F32)
        faces = [[None] * (8 // F) for _ in range(2)]
        for ix in (0, 7, 1, 2, 3, 4, 5, 6):
            line = lines[ix] if ix in lines else along_y(line_of(ix))
            swapped = [jnp.take_along_axis(v, across, axis=1) for v in line]
            line = [v + jnp.where(inner, t, 0.0) for v, t in zip(line, swapped)]
            for iy in range(8):
                n = 8 * ix + iy
                w[a, block(n), :] = line[iy]
                if iy % 2 == 0:
                    moved = jnp.where(lane < Z // 2, swapped[iy + 1], swapped[iy])
                    moved = pltpu.roll(moved, (2 * n + 2) % Z, 1)
                    packed = jnp.where(slot_of_lane // 2 == n // 2, moved, packed)
            if ix in (0, 7):
                h = ix // 7
                for j in range(8 // E):
                    out = None
                    for g in range(E):
                        v = line[j * E + g]
                        q = (g * F + h * F) % 8
                        v = pltpu.roll(v, q, 0) if q else v
                        out = v if out is None else jnp.where(sub // F == g, v, out)
                    xs[a, h, 8 * j : 8 * j + 8, :] = out
            for h in range(2):
                j, g = ix // F, ix % F
                v = line[7 * h]
                q = (g - h * (F - 1)) % 8
                v = pltpu.roll(v, q, 0) if q else v
                old = faces[h][j]
                faces[h][j] = v if old is None else jnp.where(ye == g, v, old)
        zs[a] = packed
        for h in range(2):
            for j in range(8 // F):
                ys[a, h, 8 * j : 8 * j + 8, :] = faces[h][j]

    def send(a, rslot):
        towards(lambda dx, dy, q: message(dx, dy, q, a, rslot).start())

    def collect(a, rslot):
        backwards(lambda dx, dy, q: message(dx, dy, q, a, rslot).wait_recv())
        towards(lambda dx, dy, q: message(dx, dy, q, a, rslot).wait_send())
        sides = []
        for h in range(len(z_steps)):
            total = zr[rslot, h, 4]
            for dx in (-1, 0, 1):
                for dy in (-1, 0, 1):
                    if dx == 0 and dy == 0:
                        continue
                    v = zr[rslot, h, 3 * (dx + 1) + dy + 1]
                    if dx == 0:
                        v = pltpu.roll(v, (dy * (F - 1)) % 8, 0)
                    v = pltpu.roll(v, (2 * (56 * dx + 7 * dy)) % Z, 1)
                    mask = None
                    if dx:
                        mask = ix_of_lane == (7 if dx > 0 else 0)
                    if dy:
                        more = iy_of_lane == (7 if dy > 0 else 0)
                        mask = more if mask is None else mask & more
                    if dx == 0:
                        mask = mask & (ye == (F - 1 if dy > 0 else 0))
                    total = total + jnp.where(mask, v, 0.0)
            sides.append(total)
        if nz == 2:
            sides = [jnp.where(gz > 0, sides[0], 0.0), jnp.where(gz > 0, 0.0, sides[0])]
        both = jnp.where(
            lane % 2 == 0, sides[0], pltpu.roll(sides[1], Z - 2, 1)
        )

        def line_of(ix):
            line = []
            for iy in range(8):
                n = 8 * ix + iy
                v = pltpu.roll(both, (Z - 2 * n) % Z, 1) if n else both
                line.append(w[a, block(n), :] + jnp.where(rim, v, 0.0))
            if ix in (0, 7):
                h = ix // 7
                for iy in range(8):
                    j, g = iy // E, iy % E
                    v = xr[rslot, h, 8 * j : 8 * j + 8, :]
                    q = (h * (8 - F) - g * F) % 8
                    v = pltpu.roll(v, q, 0) if q else v
                    mask = sub >= 8 - F if h else sub < F
                    line[iy] = line[iy] + jnp.where(mask, v, 0.0)
                for hy in range(2):
                    line[7 * hy] = line[7 * hy] + er[rslot, 2 * h + hy]
            for h in range(2):
                j, g = ix // F, ix % F
                v = yr[rslot, h, 8 * j : 8 * j + 8, :]
                q = (h * (F - 1) - g) % 8
                v = pltpu.roll(v, q, 0) if q else v
                line[7 * h] = line[7 * h] + jnp.where(ye == h * (F - 1), v, 0.0)
            return line

        return line_of

    for e in range(E):
        fetch(0, e).wait()
    def fold_load(c, carry):
        fold(c, lambda ix: [raw(LOADS + c, ix, iy) for iy in range(8)])
        return carry

    lax.fori_loop(0, C, fold_load, 0)
    for q in (1, 2):
        for e in range(E):
            fetch(q, e).wait()
    for ix in range(8):
        for iy in range(8):
            at = block(8 * ix + iy)
            sm[at, :] = sh * raw(MASS, ix, iy)
            for f in range(6):
                met[f, at, :] = raw(METRIC + f, ix, iy)
    for part in range(2):
        at = pl.ds(256 * part, 256)
        s3[at, :] = right_apply(lz, 2, met[2, at, :])
    for ix in range(8):
        line = mix_lines(SQUARES.T, [met[1, block(8 * ix + iy), :] for iy in range(8)], True)
        for iy in range(8):
            s2[block(8 * ix + iy), :] = line[iy]
    ends = (-14.0,) + (0.0,) * 6 + (14.0,)
    ends_z = jnp.where(lane % 8 == 0, -14.0, jnp.where(lane % 8 == 7, 14.0, 0.0))
    for iy in range(8):
        line = mix_lines(SQUARES.T, [met[0, block(8 * ix + iy), :] for ix in range(8)], True)
        for ix in range(8):
            at = block(8 * ix + iy)
            total = line[ix] + s2[at, :] + s3[at, :] + sm[at, :]
            if ends[ix] and ends[iy]:
                total = total + (2.0 * ends[ix] * ends[iy]) * met[3, at, :]
            if ends[ix]:
                total = total + (2.0 * ends[ix]) * (ends_z * met[4, at, :])
            if ends[iy]:
                total = total + (2.0 * ends[iy]) * (ends_z * met[5, at, :])
            rr[at, :] = total

    def lines_in(ref):
        return lambda ix: [ref[block(8 * ix + iy), :] for iy in range(8)]

    fold(C, lines_in(rr))
    for c in range(C):
        vecs[c] = jnp.zeros((512, Z), F32)
    acc[...] = jnp.zeros(acc.shape, F32)
    rows[...] = jnp.zeros(rows.shape, F32)

    pl.semaphore_wait(barrier, greeted)
    if max(counts) - 1 <= STEPS:
        beside = jnp.int32(0)
        for q, step in enumerate(z_steps):
            under(step[1], functools.partial(signal, 0, 0, q, besides))
            beside = beside + (1 if step[1] is None else step[1].astype(jnp.int32))
        pl.semaphore_wait(besides, beside)
    for a in (C,) + tuple(range(C)):
        send(a, C + a)
    fold(C + 1, lines_in(sm))
    send(C + 1, 2 * C + 1)

    for e in range(E):
        fetch(3, e).wait()
    for j in range(C):
        for ix in range(8):
            for iy in range(8):
                inp[j, block(8 * ix + iy), :] = raw(INPUTS + j, ix, iy)

    line_of = collect(C, 2 * C)
    for ix in range(8):
        for iy, v in enumerate(line_of(ix)):
            pre[block(8 * ix + iy), :] = 1.0 / v

    def unit(final, u, carry):
        k = u // C
        c = u % C
        theta = jnp.where(
            k == 0, 0.0,
            jnp.where(k == 1, THETA[0], jnp.where(k == 2, THETA[1], jnp.where(k == 3, THETA[2], THETA[3]))),
        ).astype(F32)
        line_of = collect(c, ((k + 1) % 2) * C + c)
        keep = ((k + STEPS - 1) // STEPS) * (C - c) + c
        shared = [[None] * 3 for _ in range(3)]
        sums = [None] * (C + 2)

        def add(old, t):
            return t if old is None else old + t

        for ix in range(8):
            line = line_of(ix)
            before = [vecs[u, block(8 * ix + iy), :] for iy in range(8)]
            scale = [pre[block(8 * ix + iy), :] for iy in range(8)]
            fresh = [p * t - theta * b for p, t, b in zip(scale, line, before)]
            for iy in range(8):
                at = block(8 * ix + iy)
                v = fresh[iy]
                vecs[u + C, at, :] = v
                if not final:
                    rhs[keep, at, :] = line[iy]
                p, q = (ix > 0) + (ix == 7), (iy > 0) + (iy == 7)
                shared[p][q] = add(shared[p][q], v * line[iy])
                for j in range(C):
                    sums[2 + j] = add(sums[2 + j], v * inp[j, at, :])
        for p in range(3):
            for q in range(3):
                t = shared[p][q]
                if p != 1:
                    t = t * weight_x[p // 2]
                if q != 1:
                    t = t * weight_y[q // 2]
                sums[1] = add(sums[1], t)
        sums[1] = sums[1] * weight_z

        for part in range(2):
            at = pl.ds(256 * part, 256)
            s3[at, :] = right_apply(lz, 0, vecs[u + C, at, :])
        for ix in range(8):
            line = mix_lines(TABLE, [vecs[u + C, block(8 * ix + iy), :] for iy in range(8)])
            for iy in range(8):
                s2[block(8 * ix + iy), :] = line[iy]
        for iy in range(8):
            va = [vecs[u + C, block(8 * ix + iy), :] for ix in range(8)]
            s1 = mix_lines(TABLE, va)
            f1 = []
            for ix in range(8):
                at = block(8 * ix + iy)
                a, b, g = s1[ix], s2[at, :], s3[at, :]
                m12, m13, m23 = met[3, at, :], met[4, at, :], met[5, at, :]
                if final:
                    t = m12 * b + m13 * g
                    q = m23 * g
                    t = a * (met[0, at, :] * a + (t + t)) + b * (met[1, at, :] * b + (q + q))
                    t = t + g * (met[2, at, :] * g) + va[ix] * (sm[at, :] * va[ix])
                    sums[0] = add(sums[0], t)
                    continue
                f1.append(met[0, at, :] * a + m12 * b + m13 * g)
                f2[at, :] = m12 * a + met[1, at, :] * b + m23 * g
                s3[at, :] = m13 * a + m23 * b + met[2, at, :] * g
            if final:
                continue
            r1 = mix_lines(TABLE.T, f1)
            for ix in range(8):
                at = block(8 * ix + iy)
                rr[at, :] = r1[ix] + sm[at, :] * va[ix]
        def result(ix):
            r2 = mix_lines(TABLE.T, [f2[block(8 * ix + iy), :] for iy in range(8)])
            out = []
            for iy in range(8):
                at = block(8 * ix + iy)
                out.append(r2[iy] + rr[at, :])
                sums[0] = add(sums[0], vecs[u + C, at, :] * out[iy])
            return out

        if not final:
            for part in range(2):
                at = pl.ds(256 * part, 256)
                rr[at, :] = rr[at, :] + right_apply(lz, 1, s3[at, :])
            fold(c, result)
        for m in range(C + 2):
            acc[(k * (C + 2) + m) * C + c] = sums[m]
        if not final:
            send(c, (k % 2) * C + c)
        return carry

    lax.fori_loop(0, (STEPS - 1) * C, functools.partial(unit, False), 0)
    lax.fori_loop((STEPS - 1) * C, STEPS * C, functools.partial(unit, True), 0)

    for q in range(STEPS * (C + 2) * C):
        rows[q : q + 1, :] = jnp.sum(acc[q], axis=0, keepdims=True)
    part = jnp.sum(rows[...].T, axis=0, keepdims=True)
    asend[...] = part
    arecv[0] = part

    def around(place, step, count):
        moved = place + step
        return lax.select(moved >= count, moved - count, moved) if step else place

    for i in range(1, N):
        a, b, c = i // (ny * nz), i // nz % ny, i % nz
        pltpu.make_async_remote_copy(
            src_ref=asend,
            dst_ref=arecv.at[i],
            send_sem=sendr,
            recv_sem=recvr,
            device_id=(around(gx, a, nx), around(gy, b, ny), around(gz, c, nz)),
            device_id_type=MESH,
        ).start()
    line_of = collect(C + 1, 2 * C + 1)
    for ix in range(8):
        for iy, v in enumerate(line_of(ix)):
            mts[block(8 * ix + iy), :] = v

    others = arecv.at[pl.ds(1, N - 1)]
    pltpu.make_async_copy(others, others, recvr).wait()
    total = jnp.sum(arecv[...], axis=0)

    def entry(k, m):
        q = (128 - (k * (C + 2) + m) * C) % 128
        return pltpu.roll(total, q, 1) if q else total

    G = [[None] * STEPS for _ in range(STEPS)]
    for k in range(STEPS):
        G[k][k] = entry(k, 0)
        if k:
            G[k - 1][k] = entry(k, 1)
    g = [entry(0, 1)]
    for gap in range(2, STEPS):
        for i in range(STEPS - gap):
            j = i + gap - 1
            G[i][j + 1] = G[i + 1][j] + float(THETA[i] - THETA[j]) * G[i][j]
    for i in range(1, STEPS):
        g.append(G[0][i - 1] - float(THETA[i - 1]) * g[i - 1])
    L = [[None] * STEPS for _ in range(STEPS)]
    inv = []
    for j in range(STEPS):
        lines = []
        for i in range(j, STEPS):
            t = G[j][i]
            for q in range(j):
                t = t - L[i][q] * lower[q][j]
            lines.append(t)
        if j == 0:
            lower = []
        lower.append([None] * j + lines)
        inv.append(1.0 / lines[0])
        for i in range(j + 1, STEPS):
            L[i][j] = lines[i - j] * inv[j]
    y = list(g)
    for i in range(STEPS):
        for q in range(i):
            y[i] = y[i] - L[i][q] * y[q]
    y = [t * d for t, d in zip(y, inv)]
    for i in reversed(range(STEPS)):
        for q in range(i + 1, STEPS):
            y[i] = y[i] - L[q][i] * y[q]
    couple = []
    for j in range(C):
        t = y[0] * entry(0, 2 + j)
        for k in range(1, STEPS):
            t = t + y[k] * entry(k, 2 + j)
        couple.append(t)

    def spread(line, c):
        return jnp.broadcast_to(line[:, c : c + 1], (8, Z))

    kk = [[spread(couple[j], c) for j in range(C)] for c in range(C)]
    ymat = [[None] * C for _ in range(C)]
    for a in range(C):
        for b in range(C):
            if b < a:
                ymat[a][b] = ymat[b][a]
                continue
            t = kk[a][0] * kk[b][0]
            for j in range(1, C):
                t = t + kk[a][j] * kk[b][j]
            ymat[a][b] = t + 1.0 if a == b else t
    one = jnp.ones((8, Z), F32)
    nil = jnp.zeros((8, Z), F32)
    right = [[one if a == b else nil for b in range(C)] + kk[a] for a in range(C)]
    for a in range(C):
        scale = 1.0 / ymat[a][a]
        ymat[a] = [t * scale for t in ymat[a]]
        right[a] = [t * scale for t in right[a]]
        for b in range(C):
            if b != a:
                q = ymat[b][a]
                ymat[b] = [t - q * s for t, s in zip(ymat[b], ymat[a])]
                right[b] = [t - q * s for t, s in zip(right[b], right[a])]
    coef = [[2.0 * right[c][j] for j in range(2 * C)] for c in range(C)]
    mixing = [[spread(y[k], c) for k in range(STEPS)] for c in range(C)]

    for ix in range(8):
        for iy in range(8):
            at = block(8 * ix + iy)
            m = mts[at, :]
            heat = []
            for c in range(C):
                t = mixing[c][0] * vecs[C + c, at, :]
                for k in range(1, STEPS):
                    t = t + mixing[c][k] * vecs[(k + 1) * C + c, at, :]
                heat.append(m * t)
            for j in range(C):
                t = heat[0] * coef[0][j]
                s = heat[0] * coef[0][C + j]
                for c in range(1, C):
                    t = t + heat[c] * coef[c][j]
                    s = s + heat[c] * coef[c][C + j]
                to = pl.ds(iy, 8, stride=8)
                ostage[j, ix, to, :] = rhs[j, at, :] - t
                ostage[C + j, ix, to, :] = s

    def store(q, e):
        return pltpu.make_async_copy(
            ostage.at[pl.ds(C * q, C), :, pl.ds(Y * e, Y)],
            (rf, fb)[q].at[:, pl.ds(8 * e, 8)],
            outsem.at[q, e],
        )

    for q in range(2):
        for e in range(E):
            store(q, e).start()

    pltpu.make_async_copy(others, others, sendr).wait()
    for q in range(2):
        for e in range(E):
            store(q, e).wait()


def local(counts, metric, mass, shift, loads, inputs):
    C, X, Y, Z = loads.shape
    E, F = X // 8, Y // 8
    assert E * F == 8 and Z >= 128 and STEPS * (C + 2) * C <= 128
    N = counts[0] * counts[1] * counts[2]
    lz = jnp.asarray(right_matrices(Z))
    vm = lambda *shape: pltpu.VMEM(shape, F32)
    dma = pltpu.SemaphoreType.DMA
    anywhere = pl.BlockSpec(memory_space=pl.ANY)
    return pl.pallas_call(
        functools.partial(kernel, (C, X, Y, Z), counts),
        out_shape=[jax.ShapeDtypeStruct(loads.shape, F32)] * 2,
        in_specs=[anywhere, anywhere, pl.BlockSpec(memory_space=pltpu.SMEM), anywhere, anywhere,
                  pl.BlockSpec(memory_space=pltpu.VMEM)],
        out_specs=[anywhere, anywhere],
        scratch_shapes=[
            vm(2 * C + 7, 8, 64, Z), vm(2 * C, 8, 64, Z), vm(6, 512, Z), vm(C, 512, Z),
            vm((STEPS + 1) * C, 512, Z), vm(C + 2, 512, Z), vm(512, Z), vm(512, Z),
            vm(C + 1, 512, Z), vm(512, Z), vm(512, Z), vm(512, Z), vm(512, Z), vm(512, Z),
            vm(128, 8, Z), vm(128, Z),
            vm(C + 2, 2, 64 // E, Z), vm(2 * C + 2, 2, 64 // E, Z),
            vm(C + 2, 2, 64 // F, Z), vm(2 * C + 2, 2, 64 // F, Z),
            vm(2 * C + 2, 4, 8, Z), vm(C + 2, 8, Z), vm(2 * C + 2, 1 if counts[2] == 2 else 2, 9, 8, Z),
            vm(1, 128), vm(N, 1, 128),
            dma((4, E)), dma((2, E)), dma((C + 2, 27)), dma((2 * C + 2, 27)), dma, dma,
            pltpu.SemaphoreType.REGULAR,
        ],
        compiler_params=pltpu.CompilerParams(
            collective_id=0, has_side_effects=True, vmem_limit_bytes=56 << 20
        ),
    )(metric, mass, shift, loads, inputs, lz)


def solution(mesh):
    counts = tuple(mesh.shape[a] for a in ("gx", "gy", "gz"))
    return jax.shard_map(
        functools.partial(local, counts),
        mesh=mesh,
        in_specs=(
            P(None, "gx", "gy", "gz"),
            P("gx", "gy", "gz"),
            P(),
            P(None, "gx", "gy", "gz"),
            P(None, "gx", "gy", "gz"),
        ),
        out_specs=(P(None, "gx", "gy", "gz"), P(None, "gx", "gy", "gz")),
        check_vma=False,
    )
```

```python
import functools

import jax
import jax.numpy as jnp
import numpy as np
from jax import lax
from jax.experimental import pallas as pl
from jax.experimental.pallas import tpu as pltpu
from jax.sharding import PartitionSpec as P

STEPS = 5
THETA = (1.25, 0.2, 2.3, 0.7)
MESH = pl.DeviceIdType.MESH
F32 = jnp.float32
BF16 = jnp.bfloat16

gll_points = (
    -1.0,
    -0.8717401485096066,
    -0.5917001814331423,
    -0.2092992179024789,
    0.2092992179024789,
    0.5917001814331423,
    0.8717401485096066,
    1.0,
)


def gll_table():
    points = np.array(gll_points)
    values = (429.0 * points**7 - 693.0 * points**5 + 315.0 * points**3 - 35.0 * points) / 16.0
    table = np.zeros((8, 8))
    for row in range(8):
        for column in range(8):
            if row != column:
                table[row, column] = values[row] / (values[column] * (points[row] - points[column]))
    table[0, 0] = -14.0
    table[7, 7] = 14.0
    return table


TABLE = gll_table()
SQUARES = TABLE * TABLE


def halves(matrix):
    full = np.asarray(matrix, np.float32)
    high = full.astype(jnp.bfloat16)
    low = (full - high.astype(np.float32)).astype(jnp.bfloat16)
    return high, low


def right_matrices(depth):
    eye = np.eye(depth // 8)
    out = []
    for m in (TABLE.T, TABLE, SQUARES):
        high, low = halves(np.kron(eye, m))
        out.append(np.block([[high, low], [high, np.zeros_like(low)]]))
    return np.stack(out)


def mix_lines(matrix, lines, even_matrix=False):
    even = [lines[j] + lines[7 - j] for j in range(4)]
    odd = [lines[j] - lines[7 - j] for j in range(4)]
    out = [None] * 8
    for i in range(4):
        p = q = None
        for j in range(4):
            a = float(np.float32(0.5 * (matrix[i, j] + matrix[i, 7 - j])))
            b = float(np.float32(0.5 * (matrix[i, j] - matrix[i, 7 - j])))
            p = a * even[j] if p is None else p + a * even[j]
            q = b * odd[j] if q is None else q + b * odd[j]
        out[i] = q + p
        out[7 - i] = p - q if even_matrix else q - p
    return out


def right_apply(lz, kind, v):
    high = v.astype(BF16)
    low = (v - high.astype(F32)).astype(BF16)
    depth = v.shape[1]
    both = jnp.dot(
        jnp.concatenate([high, low], axis=1), lz[kind], preferred_element_type=F32
    )
    return both[:, :depth] + both[:, depth:]


def kernel(
    dims, counts,
    metric, mass, shift, loads, inputs, lz,
    heat_out, rhs_out, coef_out,
    stage, warm, table, met, inp, vecs, w, pre, mts, rhs, sm, s2, s3, f2, rr, acc, rows,
    xs, xr, ys, yr, er, zs, zr, asend, arecv,
    insem, outsem, ssem, rsem, sendr, recvr, besides,
):
    C, X, Y, Z = dims
    nx, ny, nz = counts
    N = nx * ny * nz
    E, F = X // 8, Y // 8
    LOADS, MASS, METRIC, INPUTS = 0, C, C + 1, C + 7
    gx, gy, gz = lax.axis_index("gx"), lax.axis_index("gy"), lax.axis_index("gz")
    me = (gx * ny + gy) * nz + gz
    sh = shift[0]

    def block(n):
        return pl.ds(8 * n, 8)

    sources = (
        (loads, LOADS, C), (mass, MASS, 1), (metric, METRIC, 6), (inputs, INPUTS, C),
    )

    def fetch(q, e):
        ref, first, count = sources[q]
        if q == 1:
            src = ref.at[pl.ds(8 * e, 8)]
            dst = stage.at[first, :, pl.ds(Y * e, Y)]
        else:
            src = ref.at[:, pl.ds(8 * e, 8)]
            dst = stage.at[pl.ds(first, count), :, pl.ds(Y * e, Y)]
        return pltpu.make_async_copy(src, dst, insem.at[q, e])

    for q in range(4):
        for e in range(E):
            fetch(q, e).start()

    def coords(number):
        rest = lax.div(number, nz)
        return (lax.div(rest, ny), lax.rem(rest, ny), lax.rem(number, nz))

    for ref in (xr, yr, er, zr):
        ref[...] = jnp.zeros(ref.shape, F32)
    def raw(f, ix, iy):
        return stage[f, ix, pl.ds(iy, 8, stride=8), :]

    lane = lax.broadcasted_iota(jnp.int32, (8, Z), 1)
    sub = lax.broadcasted_iota(jnp.int32, (8, Z), 0)
    ye = sub % F
    inner0 = (lane % 8 == 0) & (lane > 0)
    inner7 = (lane % 8 == 7) & (lane < Z - 1)
    inner = inner0 | inner7
    across = jnp.where(inner0, lane - 1, jnp.where(inner7, lane + 1, lane))
    across = jnp.where((lane == 0) | (lane == Z - 2), Z - 1, across)
    across = jnp.where((lane == 1) | (lane == Z - 1), 0, across)
    rim = (lane == 0) | (lane == Z - 1)
    slot_of_lane = lane // 2
    ix_of_lane, iy_of_lane = slot_of_lane // 8, slot_of_lane % 8

    xe = sub // F
    weight_x = [
        jnp.where((xe > 0) | (gx > 0), 0.5, 1.0), jnp.where((xe < E - 1) | (gx < nx - 1), 0.5, 1.0)
    ]
    weight_y = [
        jnp.where((ye > 0) | (gy > 0), 0.5, 1.0), jnp.where((ye < F - 1) | (gy < ny - 1), 0.5, 1.0)
    ]
    weight_z = jnp.where(
        ((lane % 8 == 0) & ((lane > 0) | (gz > 0)))
        | ((lane % 8 == 7) & ((lane < Z - 1) | (gz < nz - 1))),
        0.5, 1.0,
    )

    def corner(hx, hy):
        return hx * (8 - F) + hy * (F - 1)

    if nz == 2:
        z_steps = [(1 - 2 * gz, None, None, 0)]
    else:
        z_steps = [(-1, gz > 0, gz < nz - 1, 1), (1, gz < nz - 1, gz > 0, 0)]
    columns = [(dx, dy) for dx in (-1, 0, 1) for dy in (-1, 0, 1)]

    def there(dx, dy):
        ok = None
        for place, step, count in zip((gx, gy), (dx, dy), (nx, ny)):
            if step:
                one = place > 0 if step < 0 else place < count - 1
                ok = one if ok is None else ok & one
        return ok

    def under(test, act):
        if test is None:
            act()
        else:
            pl.when(test)(act)

    def both_tests(a, b):
        return b if a is None else a if b is None else a & b

    def towards(act):
        for dx, dy in columns:
            def group(dx=dx, dy=dy):
                if dx or dy:
                    act(dx, dy, None)
                for q, step in enumerate(z_steps):
                    under(step[1], functools.partial(act, dx, dy, q))
            under(there(dx, dy), group)

    def backwards(act):
        for dx, dy in columns:
            def group(dx=dx, dy=dy):
                if dx or dy:
                    act(dx, dy, None)
                for q, step in enumerate(z_steps):
                    under(step[2], functools.partial(act, dx, dy, q))
            under(there(-dx, -dy), group)

    barrier = pltpu.get_barrier_semaphore()
    if max(counts) - 1 <= STEPS:
        greeted = jnp.int32(0)
        for dx, dy in columns:
            test = there(dx, dy)
            if test is not None:
                greeted = greeted + test.astype(jnp.int32)
        for step in z_steps:
            greeted = greeted + (1 if step[1] is None else step[1].astype(jnp.int32))

        def signal(dx, dy, q, sem):
            dz = 0 if q is None else z_steps[q][0]
            pl.semaphore_signal(
                sem, inc=1, device_id=(gx + dx, gy + dy, gz + dz), device_id_type=MESH
            )

        for dx, dy in columns:
            if dx or dy:
                under(there(dx, dy), functools.partial(signal, dx, dy, None, barrier))
        for q, step in enumerate(z_steps):
            under(step[1], functools.partial(signal, 0, 0, q, barrier))
    else:
        greeted = N - 1

        def greet(i, carry):
            pl.semaphore_signal(
                barrier, inc=1, device_id=coords(lax.rem(me + i, N)), device_id_type=MESH
            )
            return carry

        lax.fori_loop(1, N, greet, 0)

    def message(dx, dy, q, sslot, rslot):
        hx, hy = (dx + 1) // 2, (dy + 1) // 2
        i = 3 * (dx + 1) + dy + 1
        if q is None:
            dz = 0
            if dy == 0:
                src, dst = xs.at[sslot, hx], xr.at[rslot, 1 - hx]
            elif dx == 0:
                src, dst = ys.at[sslot, hy], yr.at[rslot, 1 - hy]
            else:
                row = 8 * (56 * hx + 7 * hy) + corner(hx, hy)
                src = w.at[sslot, pl.ds(row, 1)]
                dst = er.at[rslot, 2 * (1 - hx) + (1 - hy), pl.ds(corner(1 - hx, 1 - hy), 1)]
        else:
            dz, _, _, side = z_steps[q]
            if dx and dy:
                a, b, count = corner(hx, hy), corner(1 - hx, 1 - hy), 1
            elif dx:
                a, b, count = hx * (8 - F), (1 - hx) * (8 - F), F
            else:
                a, b, count = 0, 0, 8
            src = zs.at[sslot, pl.ds(a, count)]
            dst = zr.at[rslot, side, 8 - i, pl.ds(b, count)]
            i = 9 * (q + 1) + i
        return pltpu.make_async_remote_copy(
            src_ref=src,
            dst_ref=dst,
            send_sem=ssem.at[sslot, i],
            recv_sem=rsem.at[rslot, i],
            device_id=(gx + dx, gy + dy, gz + dz),
            device_id_type=MESH,
        )

    def fold(a, line_of):
        def along_y(line):
            v0, v7 = line[0], line[7]
            line = list(line)
            line[0] = v0 + jnp.where(ye > 0, pltpu.roll(v7, 1, 0), 0.0)
            line[7] = v7 + jnp.where(ye < F - 1, pltpu.roll(v0, 7, 0), 0.0)
            return line

        first, last = along_y(line_of(0)), along_y(line_of(7))
        lines = {
            0: [
                v + jnp.where(sub >= F, pltpu.roll(t, F, 0), 0.0) for v, t in zip(first, last)
            ],
            7: [
                t + jnp.where(sub < 8 - F, pltpu.roll(v, 8 - F, 0), 0.0)
                for v, t in zip(first, last)
            ],
        }
        packed = jnp.zeros((8, Z), F32)
        faces = [[None] * (8 // F) for _ in range(2)]
        for ix in (0, 7, 1, 2, 3, 4, 5, 6):
            line = lines[ix] if ix in lines else along_y(line_of(ix))
            swapped = [jnp.take_along_axis(v, across, axis=1) for v in line]
            line = [v + jnp.where(inner, t, 0.0) for v, t in zip(line, swapped)]
            for iy in range(8):
                n = 8 * ix + iy
                w[a, block(n), :] = line[iy]
                if iy % 2 == 0:
                    moved = jnp.where(lane < Z // 2, swapped[iy + 1], swapped[iy])
                    moved = pltpu.roll(moved, (2 * n + 2) % Z, 1)
                    packed = jnp.where(slot_of_lane // 2 == n // 2, moved, packed)
            if ix in (0, 7):
                h = ix // 7
                for j in range(8 // E):
                    out = None
                    for g in range(E):
                        v = line[j * E + g]
                        q = (g * F + h * F) % 8
                        v = pltpu.roll(v, q, 0) if q else v
                        out = v if out is None else jnp.where(sub // F == g, v, out)
                    xs[a, h, 8 * j : 8 * j + 8, :] = out
            for h in range(2):
                j, g = ix // F, ix % F
                v = line[7 * h]
                q = (g - h * (F - 1)) % 8
                v = pltpu.roll(v, q, 0) if q else v
                old = faces[h][j]
                faces[h][j] = v if old is None else jnp.where(ye == g, v, old)
        zs[a] = packed
        for h in range(2):
            for j in range(8 // F):
                ys[a, h, 8 * j : 8 * j + 8, :] = faces[h][j]

    def send(a, rslot):
        towards(lambda dx, dy, q: message(dx, dy, q, a, rslot).start())

    def collect(a, rslot):
        backwards(lambda dx, dy, q: message(dx, dy, q, a, rslot).wait_recv())
        towards(lambda dx, dy, q: message(dx, dy, q, a, rslot).wait_send())
        sides = []
        for h in range(len(z_steps)):
            total = zr[rslot, h, 4]
            for dx in (-1, 0, 1):
                for dy in (-1, 0, 1):
                    if dx == 0 and dy == 0:
                        continue
                    v = zr[rslot, h, 3 * (dx + 1) + dy + 1]
                    if dx == 0:
                        v = pltpu.roll(v, (dy * (F - 1)) % 8, 0)
                    v = pltpu.roll(v, (2 * (56 * dx + 7 * dy)) % Z, 1)
                    mask = None
                    if dx:
                        mask = ix_of_lane == (7 if dx > 0 else 0)
                    if dy:
                        more = iy_of_lane == (7 if dy > 0 else 0)
                        mask = more if mask is None else mask & more
                    if dx == 0:
                        mask = mask & (ye == (F - 1 if dy > 0 else 0))
                    total = total + jnp.where(mask, v, 0.0)
            sides.append(total)
        if nz == 2:
            sides = [jnp.where(gz > 0, sides[0], 0.0), jnp.where(gz > 0, 0.0, sides[0])]
        both = jnp.where(
            lane % 2 == 0, sides[0], pltpu.roll(sides[1], Z - 2, 1)
        )

        def line_of(ix):
            line = []
            for iy in range(8):
                n = 8 * ix + iy
                v = pltpu.roll(both, (Z - 2 * n) % Z, 1) if n else both
                line.append(w[a, block(n), :] + jnp.where(rim, v, 0.0))
            if ix in (0, 7):
                h = ix // 7
                for iy in range(8):
                    j, g = iy // E, iy % E
                    v = xr[rslot, h, 8 * j : 8 * j + 8, :]
                    q = (h * (8 - F) - g * F) % 8
                    v = pltpu.roll(v, q, 0) if q else v
                    mask = sub >= 8 - F if h else sub < F
                    line[iy] = line[iy] + jnp.where(mask, v, 0.0)
                for hy in range(2):
                    line[7 * hy] = line[7 * hy] + er[rslot, 2 * h + hy]
            for h in range(2):
                j, g = ix // F, ix % F
                v = yr[rslot, h, 8 * j : 8 * j + 8, :]
                q = (h * (F - 1) - g) % 8
                v = pltpu.roll(v, q, 0) if q else v
                line[7 * h] = line[7 * h] + jnp.where(ye == h * (F - 1), v, 0.0)
            return line

        return line_of

    for e in range(E):
        fetch(0, e).wait()
    def fold_load(c, carry):
        fold(c, lambda ix: [raw(LOADS + c, ix, iy) for iy in range(8)])
        return carry

    lax.fori_loop(0, C, fold_load, 0)
    for q in (1, 2):
        for e in range(E):
            fetch(q, e).wait()
    for ix in range(8):
        for iy in range(8):
            at = block(8 * ix + iy)
            sm[at, :] = sh * raw(MASS, ix, iy)
            for f in range(6):
                met[f, at, :] = raw(METRIC + f, ix, iy)
    for part in range(2):
        at = pl.ds(256 * part, 256)
        s3[at, :] = right_apply(lz, 2, met[2, at, :])
    for ix in range(8):
        line = mix_lines(SQUARES.T, [met[1, block(8 * ix + iy), :] for iy in range(8)], True)
        for iy in range(8):
            s2[block(8 * ix + iy), :] = line[iy]
    ends = (-14.0,) + (0.0,) * 6 + (14.0,)
    ends_z = jnp.where(lane % 8 == 0, -14.0, jnp.where(lane % 8 == 7, 14.0, 0.0))
    for iy in range(8):
        line = mix_lines(SQUARES.T, [met[0, block(8 * ix + iy), :] for ix in range(8)], True)
        for ix in range(8):
            at = block(8 * ix + iy)
            total = line[ix] + s2[at, :] + s3[at, :] + sm[at, :]
            if ends[ix] and ends[iy]:
                total = total + (2.0 * ends[ix] * ends[iy]) * met[3, at, :]
            if ends[ix]:
                total = total + (2.0 * ends[ix]) * (ends_z * met[4, at, :])
            if ends[iy]:
                total = total + (2.0 * ends[iy]) * (ends_z * met[5, at, :])
            rr[at, :] = total

    def lines_in(ref):
        return lambda ix: [ref[block(8 * ix + iy), :] for iy in range(8)]

    fold(C, lines_in(rr))
    for c in range(C):
        vecs[c] = jnp.zeros((512, Z), F32)
    acc[...] = jnp.zeros(acc.shape, F32)
    rows[...] = jnp.zeros(rows.shape, F32)

    pl.semaphore_wait(barrier, greeted)
    if max(counts) - 1 <= STEPS:
        beside = jnp.int32(0)
        for q, step in enumerate(z_steps):
            under(step[1], functools.partial(signal, 0, 0, q, besides))
            beside = beside + (1 if step[1] is None else step[1].astype(jnp.int32))
        pl.semaphore_wait(besides, beside)
    for a in (C,) + tuple(range(C)):
        send(a, C + a)
    fold(C + 1, lines_in(sm))
    send(C + 1, 2 * C + 1)

    for e in range(E):
        fetch(3, e).wait()
    for j in range(C):
        for ix in range(8):
            for iy in range(8):
                inp[j, block(8 * ix + iy), :] = raw(INPUTS + j, ix, iy)

    line_of = collect(C, 2 * C)
    for ix in range(8):
        for iy, v in enumerate(line_of(ix)):
            pre[block(8 * ix + iy), :] = 1.0 / v

    def unit(final, u, carry):
        k = u // C
        c = u % C
        theta = jnp.where(
            k == 0, 0.0,
            jnp.where(k == 1, THETA[0], jnp.where(k == 2, THETA[1], jnp.where(k == 3, THETA[2], THETA[3]))),
        ).astype(F32)
        line_of = collect(c, ((k + 1) % 2) * C + c)
        keep = ((k + STEPS - 1) // STEPS) * (C - c) + c
        shared = [[None] * 3 for _ in range(3)]
        sums = [None] * (C + 2)

        def add(old, t):
            return t if old is None else old + t

        for ix in range(8):
            line = line_of(ix)
            before = [vecs[u, block(8 * ix + iy), :] for iy in range(8)]
            scale = [pre[block(8 * ix + iy), :] for iy in range(8)]
            fresh = [p * t - theta * b for p, t, b in zip(scale, line, before)]
            for iy in range(8):
                at = block(8 * ix + iy)
                v = fresh[iy]
                vecs[u + C, at, :] = v
                if not final:
                    rhs[keep, at, :] = line[iy]
                p, q = (ix > 0) + (ix == 7), (iy > 0) + (iy == 7)
                shared[p][q] = add(shared[p][q], v * line[iy])
                for j in range(C):
                    sums[2 + j] = add(sums[2 + j], v * inp[j, at, :])
        for p in range(3):
            for q in range(3):
                t = shared[p][q]
                if p != 1:
                    t = t * weight_x[p // 2]
                if q != 1:
                    t = t * weight_y[q // 2]
                sums[1] = add(sums[1], t)
        sums[1] = sums[1] * weight_z

        for part in range(2):
            at = pl.ds(256 * part, 256)
            s3[at, :] = right_apply(lz, 0, vecs[u + C, at, :])
        for ix in range(8):
            line = mix_lines(TABLE, [vecs[u + C, block(8 * ix + iy), :] for iy in range(8)])
            for iy in range(8):
                s2[block(8 * ix + iy), :] = line[iy]
        for iy in range(8):
            va = [vecs[u + C, block(8 * ix + iy), :] for ix in range(8)]
            s1 = mix_lines(TABLE, va)
            f1 = []
            for ix in range(8):
                at = block(8 * ix + iy)
                a, b, g = s1[ix], s2[at, :], s3[at, :]
                m12, m13, m23 = met[3, at, :], met[4, at, :], met[5, at, :]
                if final:
                    t = m12 * b + m13 * g
                    q = m23 * g
                    t = a * (met[0, at, :] * a + (t + t)) + b * (met[1, at, :] * b + (q + q))
                    t = t + g * (met[2, at, :] * g) + va[ix] * (sm[at, :] * va[ix])
                    sums[0] = add(sums[0], t)
                    continue
                f1.append(met[0, at, :] * a + m12 * b + m13 * g)
                f2[at, :] = m12 * a + met[1, at, :] * b + m23 * g
                s3[at, :] = m13 * a + m23 * b + met[2, at, :] * g
            if final:
                continue
            r1 = mix_lines(TABLE.T, f1)
            for ix in range(8):
                at = block(8 * ix + iy)
                rr[at, :] = r1[ix] + sm[at, :] * va[ix]
        def result(ix):
            r2 = mix_lines(TABLE.T, [f2[block(8 * ix + iy), :] for iy in range(8)])
            out = []
            for iy in range(8):
                at = block(8 * ix + iy)
                out.append(r2[iy] + rr[at, :])
                sums[0] = add(sums[0], vecs[u + C, at, :] * out[iy])
            return out

        if not final:
            for part in range(2):
                at = pl.ds(256 * part, 256)
                rr[at, :] = rr[at, :] + right_apply(lz, 1, s3[at, :])
            fold(c, result)
        for m in range(C + 2):
            acc[(k * (C + 2) + m) * C + c] = sums[m]
        if not final:
            send(c, (k % 2) * C + c)
        return carry

    lax.fori_loop(0, (STEPS - 1) * C, functools.partial(unit, False), 0)
    leaving = [pltpu.make_async_copy(rhs.at[pl.ds(0, C)], rhs_out, outsem.at[0])]
    leaving[0].start()
    lax.fori_loop((STEPS - 1) * C, STEPS * C, functools.partial(unit, True), 0)

    for q in range(STEPS * (C + 2) * C):
        rows[q : q + 1, :] = jnp.sum(acc[q], axis=0, keepdims=True)
    part = jnp.sum(rows[...].T, axis=0, keepdims=True)
    asend[...] = part
    arecv[0] = part

    def around(place, step, count):
        moved = place + step
        return lax.select(moved >= count, moved - count, moved) if step else place

    for i in range(1, N):
        a, b, c = i // (ny * nz), i // nz % ny, i % nz
        pltpu.make_async_remote_copy(
            src_ref=asend,
            dst_ref=arecv.at[i],
            send_sem=sendr,
            recv_sem=recvr,
            device_id=(around(gx, a, nx), around(gy, b, ny), around(gz, c, nz)),
            device_id_type=MESH,
        ).start()
    line_of = collect(C + 1, 2 * C + 1)
    for ix in range(8):
        for iy, v in enumerate(line_of(ix)):
            mts[block(8 * ix + iy), :] = v

    others = arecv.at[pl.ds(1, N - 1)]
    pltpu.make_async_copy(others, others, recvr).wait()
    total = jnp.sum(arecv[...], axis=0)

    def entry(k, m):
        q = (128 - (k * (C + 2) + m) * C) % 128
        return pltpu.roll(total, q, 1) if q else total

    G = [[None] * STEPS for _ in range(STEPS)]
    for k in range(STEPS):
        G[k][k] = entry(k, 0)
        if k:
            G[k - 1][k] = entry(k, 1)
    g = [entry(0, 1)]
    for gap in range(2, STEPS):
        for i in range(STEPS - gap):
            j = i + gap - 1
            G[i][j + 1] = G[i + 1][j] + float(THETA[i] - THETA[j]) * G[i][j]
    for i in range(1, STEPS):
        g.append(G[0][i - 1] - float(THETA[i - 1]) * g[i - 1])
    L = [[None] * STEPS for _ in range(STEPS)]
    inv = []
    for j in range(STEPS):
        lines = []
        for i in range(j, STEPS):
            t = G[j][i]
            for q in range(j):
                t = t - L[i][q] * lower[q][j]
            lines.append(t)
        if j == 0:
            lower = []
        lower.append([None] * j + lines)
        inv.append(1.0 / lines[0])
        for i in range(j + 1, STEPS):
            L[i][j] = lines[i - j] * inv[j]
    y = list(g)
    for i in range(STEPS):
        for q in range(i):
            y[i] = y[i] - L[i][q] * y[q]
    y = [t * d for t, d in zip(y, inv)]
    for i in reversed(range(STEPS)):
        for q in range(i + 1, STEPS):
            y[i] = y[i] - L[q][i] * y[q]
    couple = []
    for j in range(C):
        t = y[0] * entry(0, 2 + j)
        for k in range(1, STEPS):
            t = t + y[k] * entry(k, 2 + j)
        couple.append(t)

    def spread(line, c):
        return jnp.broadcast_to(line[:, c : c + 1], (8, Z))

    kk = [[spread(couple[j], c) for j in range(C)] for c in range(C)]
    ymat = [[None] * C for _ in range(C)]
    for a in range(C):
        for b in range(C):
            if b < a:
                ymat[a][b] = ymat[b][a]
                continue
            t = kk[a][0] * kk[b][0]
            for j in range(1, C):
                t = t + kk[a][j] * kk[b][j]
            ymat[a][b] = t + 1.0 if a == b else t
    one = jnp.ones((8, Z), F32)
    nil = jnp.zeros((8, Z), F32)
    right = [[one if a == b else nil for b in range(C)] + kk[a] for a in range(C)]
    for a in range(C):
        scale = 1.0 / ymat[a][a]
        ymat[a] = [t * scale for t in ymat[a]]
        right[a] = [t * scale for t in right[a]]
        for b in range(C):
            if b != a:
                q = ymat[b][a]
                ymat[b] = [t - q * s for t, s in zip(ymat[b], ymat[a])]
                right[b] = [t - q * s for t, s in zip(right[b], right[a])]
    for c in range(C):
        for j in range(2 * C):
            q = 2 * C * c + j
            table[q : q + 1, :] = 2.0 * right[c][j][0:1, :]
    leaving.append(pltpu.make_async_copy(table, coef_out, outsem.at[1]))
    leaving[1].start()
    mixing = [[spread(y[k], c) for k in range(STEPS)] for c in range(C)]
    for half in range(2):
        for n in range(32 * half, 32 * half + 32):
            at = block(n)
            m = mts[at, :]
            for c in range(C):
                t = mixing[c][0] * vecs[C + c, at, :]
                for k in range(1, STEPS):
                    t = t + mixing[c][k] * vecs[(k + 1) * C + c, at, :]
                warm[c, at, :] = m * t
        rows_of = pl.ds(256 * half, 256)
        leaving.append(
            pltpu.make_async_copy(
                warm.at[:, rows_of], heat_out.at[:, rows_of], outsem.at[2 + half]
            )
        )
        leaving[-1].start()

    pltpu.make_async_copy(others, others, sendr).wait()
    for copy in leaving:
        copy.wait()


def finish(C, E, F, lines, heat, rhs, coef, rf, fb):
    def weight(q):
        return jnp.broadcast_to(coef[q : q + 1, :], (8, coef.shape[1]))

    weights = [[weight(2 * C * c + j) for j in range(2 * C)] for c in range(C)]
    for ix in range(lines):
        for iy in range(8):
            at = pl.ds(64 * ix + 8 * iy, 8)
            hs = [heat[c, at, :] for c in range(C)]
            for j in range(2 * C):
                t = hs[0] * weights[0][j]
                for c in range(1, C):
                    t = t + hs[c] * weights[c][j]
                if j < C:
                    t = rhs[j, at, :] - t
                out = rf if j < C else fb
                for e in range(E):
                    out[j % C, e, ix, pl.ds(iy, F, stride=8), :] = t[e * F : (e + 1) * F]


def local(counts, metric, mass, shift, loads, inputs):
    C, X, Y, Z = loads.shape
    E, F = X // 8, Y // 8
    assert E * F == 8 and Z >= 128 and STEPS * (C + 2) * C <= 128
    N = counts[0] * counts[1] * counts[2]
    lz = jnp.asarray(right_matrices(Z))
    vm = lambda *shape: pltpu.VMEM(shape, F32)
    dma = pltpu.SemaphoreType.DMA
    anywhere = pl.BlockSpec(memory_space=pl.ANY)
    field = jax.ShapeDtypeStruct((C, 512, Z), F32)
    heat, rhs, coef = pl.pallas_call(
        functools.partial(kernel, (C, X, Y, Z), counts),
        out_shape=[field, field, jax.ShapeDtypeStruct((2 * C * C, Z), F32)],
        in_specs=[anywhere, anywhere, pl.BlockSpec(memory_space=pltpu.SMEM), anywhere, anywhere,
                  pl.BlockSpec(memory_space=pltpu.VMEM)],
        out_specs=[anywhere] * 3,
        scratch_shapes=[
            vm(2 * C + 7, 8, 64, Z), vm(C, 512, Z), vm(2 * C * C, Z), vm(6, 512, Z), vm(C, 512, Z),
            vm((STEPS + 1) * C, 512, Z), vm(C + 2, 512, Z), vm(512, Z), vm(512, Z),
            vm(C + 1, 512, Z), vm(512, Z), vm(512, Z), vm(512, Z), vm(512, Z), vm(512, Z),
            vm(128, 8, Z), vm(128, Z),
            vm(C + 2, 2, 64 // E, Z), vm(2 * C + 2, 2, 64 // E, Z),
            vm(C + 2, 2, 64 // F, Z), vm(2 * C + 2, 2, 64 // F, Z),
            vm(2 * C + 2, 4, 8, Z), vm(C + 2, 8, Z), vm(2 * C + 2, 1 if counts[2] == 2 else 2, 9, 8, Z),
            vm(1, 128), vm(N, 1, 128),
            dma((4, E)), dma((4,)), dma((C + 2, 27)), dma((2 * C + 2, 27)), dma, dma,
            pltpu.SemaphoreType.REGULAR,
        ],
        compiler_params=pltpu.CompilerParams(
            collective_id=0, has_side_effects=True, vmem_limit_bytes=56 << 20
        ),
    )(metric, mass, shift, loads, inputs, lz)
    lines = 4
    part = pl.BlockSpec((C, 64 * lines, Z), lambda i: (0, i, 0))
    whole = pl.BlockSpec((C, E, lines, Y, Z), lambda i: (0, 0, i, 0, 0))
    rf, fb = pl.pallas_call(
        functools.partial(finish, C, E, F, lines),
        grid=(8 // lines,),
        out_shape=[jax.ShapeDtypeStruct((C, E, 8, Y, Z), F32)] * 2,
        in_specs=[part, part, pl.BlockSpec((2 * C * C, Z), lambda i: (0, 0))],
        out_specs=[whole, whole],
    )(heat, rhs, coef)
    return rf.reshape(loads.shape), fb.reshape(loads.shape)


def solution(mesh):
    counts = tuple(mesh.shape[a] for a in ("gx", "gy", "gz"))
    return jax.shard_map(
        functools.partial(local, counts),
        mesh=mesh,
        in_specs=(
            P(None, "gx", "gy", "gz"),
            P("gx", "gy", "gz"),
            P(),
            P(None, "gx", "gy", "gz"),
            P(None, "gx", "gy", "gz"),
        ),
        out_specs=(P(None, "gx", "gy", "gz"), P(None, "gx", "gy", "gz")),
        check_vma=False,
    )
```

```python
import functools

import jax
import jax.numpy as jnp
import numpy as np
from jax import lax
from jax.experimental import pallas as pl
from jax.experimental.pallas import tpu as pltpu
from jax.sharding import PartitionSpec as P

STEPS = 5
THETA = (1.25, 0.2, 2.3, 0.7)
MESH = pl.DeviceIdType.MESH
F32 = jnp.float32
BF16 = jnp.bfloat16

gll_points = (
    -1.0,
    -0.8717401485096066,
    -0.5917001814331423,
    -0.2092992179024789,
    0.2092992179024789,
    0.5917001814331423,
    0.8717401485096066,
    1.0,
)


def gll_table():
    points = np.array(gll_points)
    values = (429.0 * points**7 - 693.0 * points**5 + 315.0 * points**3 - 35.0 * points) / 16.0
    table = np.zeros((8, 8))
    for row in range(8):
        for column in range(8):
            if row != column:
                table[row, column] = values[row] / (values[column] * (points[row] - points[column]))
    table[0, 0] = -14.0
    table[7, 7] = 14.0
    return table


TABLE = gll_table()
SQUARES = TABLE * TABLE


def halves(matrix):
    full = np.asarray(matrix, np.float32)
    high = full.astype(jnp.bfloat16)
    low = (full - high.astype(np.float32)).astype(jnp.bfloat16)
    return high, low


def right_matrices(depth):
    eye = np.eye(depth // 8)
    out = []
    for m in (TABLE.T, TABLE, SQUARES):
        high, low = halves(np.kron(eye, m))
        out.append(np.block([[high, low], [high, np.zeros_like(low)]]))
    return np.stack(out)


def mix_lines(matrix, lines, even_matrix=False):
    even = [lines[j] + lines[7 - j] for j in range(4)]
    odd = [lines[j] - lines[7 - j] for j in range(4)]
    out = [None] * 8
    for i in range(4):
        p = q = None
        for j in range(4):
            a = float(np.float32(0.5 * (matrix[i, j] + matrix[i, 7 - j])))
            b = float(np.float32(0.5 * (matrix[i, j] - matrix[i, 7 - j])))
            p = a * even[j] if p is None else p + a * even[j]
            q = b * odd[j] if q is None else q + b * odd[j]
        out[i] = q + p
        out[7 - i] = p - q if even_matrix else q - p
    return out


def right_apply(lz, kind, v):
    high = v.astype(BF16)
    low = (v - high.astype(F32)).astype(BF16)
    depth = v.shape[1]
    both = jnp.dot(
        jnp.concatenate([high, low], axis=1), lz[kind], preferred_element_type=F32
    )
    return both[:, :depth] + both[:, depth:]


def kernel(
    dims, counts,
    metric, mass, shift, loads, inputs, lz,
    heat_out, rhs_out, coef_out,
    stage, table, met, inp, vecs, w, pre, mts, rhs, sm, s2, s3, f2, rr, acc, rows,
    xs, xr, ys, yr, er, zs, zr, asend, arecv,
    insem, outsem, ssem, rsem, sendr, recvr, besides,
):
    C, X, Y, Z = dims
    nx, ny, nz = counts
    N = nx * ny * nz
    E, F = X // 8, Y // 8
    LOADS, MASS, METRIC, INPUTS = 0, C, C + 1, C + 7
    gx, gy, gz = lax.axis_index("gx"), lax.axis_index("gy"), lax.axis_index("gz")
    me = (gx * ny + gy) * nz + gz
    sh = shift[0]

    def block(n):
        return pl.ds(8 * n, 8)

    sources = (
        (loads, LOADS, C), (mass, MASS, 1), (metric, METRIC, 6), (inputs, INPUTS, C),
    )

    def fetch(q, e):
        ref, first, count = sources[q]
        if q == 1:
            src = ref.at[pl.ds(8 * e, 8)]
            dst = stage.at[first, :, pl.ds(Y * e, Y)]
        else:
            src = ref.at[:, pl.ds(8 * e, 8)]
            dst = stage.at[pl.ds(first, count), :, pl.ds(Y * e, Y)]
        return pltpu.make_async_copy(src, dst, insem.at[q, e])

    for q in range(4):
        for e in range(E):
            fetch(q, e).start()

    def coords(number):
        rest = lax.div(number, nz)
        return (lax.div(rest, ny), lax.rem(rest, ny), lax.rem(number, nz))

    for ref in (xr, yr, er, zr):
        ref[...] = jnp.zeros(ref.shape, F32)
    def raw(f, ix, iy):
        return stage[f, ix, pl.ds(iy, 8, stride=8), :]

    lane = lax.broadcasted_iota(jnp.int32, (8, Z), 1)
    sub = lax.broadcasted_iota(jnp.int32, (8, Z), 0)
    ye = sub % F
    inner0 = (lane % 8 == 0) & (lane > 0)
    inner7 = (lane % 8 == 7) & (lane < Z - 1)
    inner = inner0 | inner7
    across = jnp.where(inner0, lane - 1, jnp.where(inner7, lane + 1, lane))
    across = jnp.where((lane == 0) | (lane == Z - 2), Z - 1, across)
    across = jnp.where((lane == 1) | (lane == Z - 1), 0, across)
    rim = (lane == 0) | (lane == Z - 1)
    slot_of_lane = lane // 2
    ix_of_lane, iy_of_lane = slot_of_lane // 8, slot_of_lane % 8

    xe = sub // F
    weight_x = [
        jnp.where((xe > 0) | (gx > 0), 0.5, 1.0), jnp.where((xe < E - 1) | (gx < nx - 1), 0.5, 1.0)
    ]
    weight_y = [
        jnp.where((ye > 0) | (gy > 0), 0.5, 1.0), jnp.where((ye < F - 1) | (gy < ny - 1), 0.5, 1.0)
    ]
    weight_z = jnp.where(
        ((lane % 8 == 0) & ((lane > 0) | (gz > 0)))
        | ((lane % 8 == 7) & ((lane < Z - 1) | (gz < nz - 1))),
        0.5, 1.0,
    )

    def corner(hx, hy):
        return hx * (8 - F) + hy * (F - 1)

    if nz == 2:
        z_steps = [(1 - 2 * gz, None, None, 0)]
    else:
        z_steps = [(-1, gz > 0, gz < nz - 1, 1), (1, gz < nz - 1, gz > 0, 0)]
    columns = [(dx, dy) for dx in (-1, 0, 1) for dy in (-1, 0, 1)]

    def there(dx, dy):
        ok = None
        for place, step, count in zip((gx, gy), (dx, dy), (nx, ny)):
            if step:
                one = place > 0 if step < 0 else place < count - 1
                ok = one if ok is None else ok & one
        return ok

    def under(test, act):
        if test is None:
            act()
        else:
            pl.when(test)(act)

    def both_tests(a, b):
        return b if a is None else a if b is None else a & b

    def towards(act):
        for dx, dy in columns:
            def group(dx=dx, dy=dy):
                if dx or dy:
                    act(dx, dy, None)
                for q, step in enumerate(z_steps):
                    under(step[1], functools.partial(act, dx, dy, q))
            under(there(dx, dy), group)

    def backwards(act):
        for dx, dy in columns:
            def group(dx=dx, dy=dy):
                if dx or dy:
                    act(dx, dy, None)
                for q, step in enumerate(z_steps):
                    under(step[2], functools.partial(act, dx, dy, q))
            under(there(-dx, -dy), group)

    barrier = pltpu.get_barrier_semaphore()
    if max(counts) - 1 <= STEPS:
        greeted = jnp.int32(0)
        for dx, dy in columns:
            test = there(dx, dy)
            if test is not None:
                greeted = greeted + test.astype(jnp.int32)
        for step in z_steps:
            greeted = greeted + (1 if step[1] is None else step[1].astype(jnp.int32))

        def signal(dx, dy, q, sem):
            dz = 0 if q is None else z_steps[q][0]
            pl.semaphore_signal(
                sem, inc=1, device_id=(gx + dx, gy + dy, gz + dz), device_id_type=MESH
            )

        for dx, dy in columns:
            if dx or dy:
                under(there(dx, dy), functools.partial(signal, dx, dy, None, barrier))
        for q, step in enumerate(z_steps):
            under(step[1], functools.partial(signal, 0, 0, q, barrier))
    else:
        greeted = N - 1

        def greet(i, carry):
            pl.semaphore_signal(
                barrier, inc=1, device_id=coords(lax.rem(me + i, N)), device_id_type=MESH
            )
            return carry

        lax.fori_loop(1, N, greet, 0)

    def message(dx, dy, q, sslot, rslot):
        hx, hy = (dx + 1) // 2, (dy + 1) // 2
        i = 3 * (dx + 1) + dy + 1
        if q is None:
            dz = 0
            if dy == 0:
                src, dst = xs.at[sslot, hx], xr.at[rslot, 1 - hx]
            elif dx == 0:
                src, dst = ys.at[sslot, hy], yr.at[rslot, 1 - hy]
            else:
                row = 8 * (56 * hx + 7 * hy) + corner(hx, hy)
                src = w.at[sslot, pl.ds(row, 1)]
                dst = er.at[rslot, 2 * (1 - hx) + (1 - hy), pl.ds(corner(1 - hx, 1 - hy), 1)]
        else:
            dz, _, _, side = z_steps[q]
            if dx and dy:
                a, b, count = corner(hx, hy), corner(1 - hx, 1 - hy), 1
            elif dx:
                a, b, count = hx * (8 - F), (1 - hx) * (8 - F), F
            else:
                a, b, count = 0, 0, 8
            src = zs.at[sslot, pl.ds(a, count)]
            dst = zr.at[rslot, side, 8 - i, pl.ds(b, count)]
            i = 9 * (q + 1) + i
        return pltpu.make_async_remote_copy(
            src_ref=src,
            dst_ref=dst,
            send_sem=ssem.at[sslot, i],
            recv_sem=rsem.at[rslot, i],
            device_id=(gx + dx, gy + dy, gz + dz),
            device_id_type=MESH,
        )

    def fold(a, line_of):
        def along_y(line):
            v0, v7 = line[0], line[7]
            line = list(line)
            line[0] = v0 + jnp.where(ye > 0, pltpu.roll(v7, 1, 0), 0.0)
            line[7] = v7 + jnp.where(ye < F - 1, pltpu.roll(v0, 7, 0), 0.0)
            return line

        first, last = along_y(line_of(0)), along_y(line_of(7))
        lines = {
            0: [
                v + jnp.where(sub >= F, pltpu.roll(t, F, 0), 0.0) for v, t in zip(first, last)
            ],
            7: [
                t + jnp.where(sub < 8 - F, pltpu.roll(v, 8 - F, 0), 0.0)
                for v, t in zip(first, last)
            ],
        }
        packed = jnp.zeros((8, Z), F32)
        faces = [[None] * (8 // F) for _ in range(2)]
        for ix in (0, 7, 1, 2, 3, 4, 5, 6):
            line = lines[ix] if ix in lines else along_y(line_of(ix))
            swapped = [jnp.take_along_axis(v, across, axis=1) for v in line]
            line = [v + jnp.where(inner, t, 0.0) for v, t in zip(line, swapped)]
            for iy in range(8):
                n = 8 * ix + iy
                w[a, block(n), :] = line[iy]
                if iy % 2 == 0:
                    moved = jnp.where(lane < Z // 2, swapped[iy + 1], swapped[iy])
                    moved = pltpu.roll(moved, (2 * n + 2) % Z, 1)
                    packed = jnp.where(slot_of_lane // 2 == n // 2, moved, packed)
            if ix in (0, 7):
                h = ix // 7
                for j in range(8 // E):
                    out = None
                    for g in range(E):
                        v = line[j * E + g]
                        q = (g * F + h * F) % 8
                        v = pltpu.roll(v, q, 0) if q else v
                        out = v if out is None else jnp.where(sub // F == g, v, out)
                    xs[a, h, 8 * j : 8 * j + 8, :] = out
            for h in range(2):
                j, g = ix // F, ix % F
                v = line[7 * h]
                q = (g - h * (F - 1)) % 8
                v = pltpu.roll(v, q, 0) if q else v
                old = faces[h][j]
                faces[h][j] = v if old is None else jnp.where(ye == g, v, old)
        zs[a] = packed
        for h in range(2):
            for j in range(8 // F):
                ys[a, h, 8 * j : 8 * j + 8, :] = faces[h][j]

    def send(a, rslot):
        towards(lambda dx, dy, q: message(dx, dy, q, a, rslot).start())

    def collect(a, rslot):
        backwards(lambda dx, dy, q: message(dx, dy, q, a, rslot).wait_recv())
        towards(lambda dx, dy, q: message(dx, dy, q, a, rslot).wait_send())
        sides = []
        for h in range(len(z_steps)):
            total = zr[rslot, h, 4]
            for dx in (-1, 0, 1):
                for dy in (-1, 0, 1):
                    if dx == 0 and dy == 0:
                        continue
                    v = zr[rslot, h, 3 * (dx + 1) + dy + 1]
                    if dx == 0:
                        v = pltpu.roll(v, (dy * (F - 1)) % 8, 0)
                    v = pltpu.roll(v, (2 * (56 * dx + 7 * dy)) % Z, 1)
                    mask = None
                    if dx:
                        mask = ix_of_lane == (7 if dx > 0 else 0)
                    if dy:
                        more = iy_of_lane == (7 if dy > 0 else 0)
                        mask = more if mask is None else mask & more
                    if dx == 0:
                        mask = mask & (ye == (F - 1 if dy > 0 else 0))
                    total = total + jnp.where(mask, v, 0.0)
            sides.append(total)
        if nz == 2:
            sides = [jnp.where(gz > 0, sides[0], 0.0), jnp.where(gz > 0, 0.0, sides[0])]
        both = jnp.where(
            lane % 2 == 0, sides[0], pltpu.roll(sides[1], Z - 2, 1)
        )

        def line_of(ix):
            line = []
            for iy in range(8):
                n = 8 * ix + iy
                v = pltpu.roll(both, (Z - 2 * n) % Z, 1) if n else both
                line.append(w[a, block(n), :] + jnp.where(rim, v, 0.0))
            if ix in (0, 7):
                h = ix // 7
                for iy in range(8):
                    j, g = iy // E, iy % E
                    v = xr[rslot, h, 8 * j : 8 * j + 8, :]
                    q = (h * (8 - F) - g * F) % 8
                    v = pltpu.roll(v, q, 0) if q else v
                    mask = sub >= 8 - F if h else sub < F
                    line[iy] = line[iy] + jnp.where(mask, v, 0.0)
                for hy in range(2):
                    line[7 * hy] = line[7 * hy] + er[rslot, 2 * h + hy]
            for h in range(2):
                j, g = ix // F, ix % F
                v = yr[rslot, h, 8 * j : 8 * j + 8, :]
                q = (h * (F - 1) - g) % 8
                v = pltpu.roll(v, q, 0) if q else v
                line[7 * h] = line[7 * h] + jnp.where(ye == h * (F - 1), v, 0.0)
            return line

        return line_of

    for e in range(E):
        fetch(0, e).wait()
    def fold_load(c, carry):
        fold(c, lambda ix: [raw(LOADS + c, ix, iy) for iy in range(8)])
        return carry

    lax.fori_loop(0, C, fold_load, 0)
    for q in (1, 2):
        for e in range(E):
            fetch(q, e).wait()
    for ix in range(8):
        for iy in range(8):
            at = block(8 * ix + iy)
            sm[at, :] = sh * raw(MASS, ix, iy)
            for f in range(6):
                met[f, at, :] = raw(METRIC + f, ix, iy)
    for part in range(2):
        at = pl.ds(256 * part, 256)
        s3[at, :] = right_apply(lz, 2, met[2, at, :])
    for ix in range(8):
        line = mix_lines(SQUARES.T, [met[1, block(8 * ix + iy), :] for iy in range(8)], True)
        for iy in range(8):
            s2[block(8 * ix + iy), :] = line[iy]
    ends = (-14.0,) + (0.0,) * 6 + (14.0,)
    ends_z = jnp.where(lane % 8 == 0, -14.0, jnp.where(lane % 8 == 7, 14.0, 0.0))
    for iy in range(8):
        line = mix_lines(SQUARES.T, [met[0, block(8 * ix + iy), :] for ix in range(8)], True)
        for ix in range(8):
            at = block(8 * ix + iy)
            total = line[ix] + s2[at, :] + s3[at, :] + sm[at, :]
            if ends[ix] and ends[iy]:
                total = total + (2.0 * ends[ix] * ends[iy]) * met[3, at, :]
            if ends[ix]:
                total = total + (2.0 * ends[ix]) * (ends_z * met[4, at, :])
            if ends[iy]:
                total = total + (2.0 * ends[iy]) * (ends_z * met[5, at, :])
            rr[at, :] = total

    def lines_in(ref):
        return lambda ix: [ref[block(8 * ix + iy), :] for iy in range(8)]

    fold(C, lines_in(rr))
    for c in range(C):
        vecs[c] = jnp.zeros((512, Z), F32)
    acc[...] = jnp.zeros(acc.shape, F32)
    rows[...] = jnp.zeros(rows.shape, F32)

    pl.semaphore_wait(barrier, greeted)
    if max(counts) - 1 <= STEPS:
        beside = jnp.int32(0)
        for q, step in enumerate(z_steps):
            under(step[1], functools.partial(signal, 0, 0, q, besides))
            beside = beside + (1 if step[1] is None else step[1].astype(jnp.int32))
        pl.semaphore_wait(besides, beside)
    for a in (C,) + tuple(range(C)):
        send(a, C + a)
    fold(C + 1, lines_in(sm))
    send(C + 1, 2 * C + 1)

    for e in range(E):
        fetch(3, e).wait()
    for j in range(C):
        for ix in range(8):
            for iy in range(8):
                inp[j, block(8 * ix + iy), :] = raw(INPUTS + j, ix, iy)

    line_of = collect(C, 2 * C)
    for ix in range(8):
        for iy, v in enumerate(line_of(ix)):
            pre[block(8 * ix + iy), :] = 1.0 / v

    def unit(final, u, carry):
        k = u // C
        c = u % C
        theta = jnp.where(
            k == 0, 0.0,
            jnp.where(k == 1, THETA[0], jnp.where(k == 2, THETA[1], jnp.where(k == 3, THETA[2], THETA[3]))),
        ).astype(F32)
        line_of = collect(c, ((k + 1) % 2) * C + c)
        keep = ((k + STEPS - 1) // STEPS) * (C - c) + c
        shared = [[None] * 3 for _ in range(3)]
        sums = [None] * (C + 2)

        def add(old, t):
            return t if old is None else old + t

        for ix in range(8):
            line = line_of(ix)
            before = [vecs[u, block(8 * ix + iy), :] for iy in range(8)]
            scale = [pre[block(8 * ix + iy), :] for iy in range(8)]
            fresh = [p * t - theta * b for p, t, b in zip(scale, line, before)]
            for iy in range(8):
                at = block(8 * ix + iy)
                v = fresh[iy]
                vecs[u + C, at, :] = v
                if not final:
                    rhs[keep, at, :] = line[iy]
                p, q = (ix > 0) + (ix == 7), (iy > 0) + (iy == 7)
                shared[p][q] = add(shared[p][q], v * line[iy])
                for j in range(C):
                    sums[2 + j] = add(sums[2 + j], v * inp[j, at, :])
        for p in range(3):
            for q in range(3):
                t = shared[p][q]
                if p != 1:
                    t = t * weight_x[p // 2]
                if q != 1:
                    t = t * weight_y[q // 2]
                sums[1] = add(sums[1], t)
        sums[1] = sums[1] * weight_z

        for part in range(2):
            at = pl.ds(256 * part, 256)
            s3[at, :] = right_apply(lz, 0, vecs[u + C, at, :])
        for ix in range(8):
            line = mix_lines(TABLE, [vecs[u + C, block(8 * ix + iy), :] for iy in range(8)])
            for iy in range(8):
                s2[block(8 * ix + iy), :] = line[iy]
        for iy in range(8):
            va = [vecs[u + C, block(8 * ix + iy), :] for ix in range(8)]
            s1 = mix_lines(TABLE, va)
            f1 = []
            for ix in range(8):
                at = block(8 * ix + iy)
                a, b, g = s1[ix], s2[at, :], s3[at, :]
                m12, m13, m23 = met[3, at, :], met[4, at, :], met[5, at, :]
                if final:
                    t = m12 * b + m13 * g
                    q = m23 * g
                    t = a * (met[0, at, :] * a + (t + t)) + b * (met[1, at, :] * b + (q + q))
                    t = t + g * (met[2, at, :] * g) + va[ix] * (sm[at, :] * va[ix])
                    sums[0] = add(sums[0], t)
                    continue
                f1.append(met[0, at, :] * a + m12 * b + m13 * g)
                f2[at, :] = m12 * a + met[1, at, :] * b + m23 * g
                s3[at, :] = m13 * a + m23 * b + met[2, at, :] * g
            if final:
                continue
            r1 = mix_lines(TABLE.T, f1)
            for ix in range(8):
                at = block(8 * ix + iy)
                rr[at, :] = r1[ix] + sm[at, :] * va[ix]
        def result(ix):
            r2 = mix_lines(TABLE.T, [f2[block(8 * ix + iy), :] for iy in range(8)])
            out = []
            for iy in range(8):
                at = block(8 * ix + iy)
                out.append(r2[iy] + rr[at, :])
                sums[0] = add(sums[0], vecs[u + C, at, :] * out[iy])
            return out

        if not final:
            for part in range(2):
                at = pl.ds(256 * part, 256)
                rr[at, :] = rr[at, :] + right_apply(lz, 1, s3[at, :])
            fold(c, result)
        for m in range(C + 2):
            acc[(k * (C + 2) + m) * C + c] = sums[m]
        if not final:
            send(c, (k % 2) * C + c)
        return carry

    lax.fori_loop(0, (STEPS - 1) * C, functools.partial(unit, False), 0)
    def add_up(start, stop):
        for q in range(start, stop):
            rows[q : q + 1, :] = jnp.sum(acc[q], axis=0, keepdims=True)

    add_up(0, (STEPS - 1) * (C + 2) * C)
    leaving = [pltpu.make_async_copy(rhs.at[pl.ds(0, C)], rhs_out, outsem.at[0])]
    leaving[0].start()
    lax.fori_loop((STEPS - 1) * C, STEPS * C, functools.partial(unit, True), 0)

    add_up((STEPS - 1) * (C + 2) * C, STEPS * (C + 2) * C)
    part = jnp.sum(rows[...].T, axis=0, keepdims=True)
    asend[...] = part
    arecv[0] = part

    def around(place, step, count):
        moved = place + step
        return lax.select(moved >= count, moved - count, moved) if step else place

    for i in range(1, N):
        a, b, c = i // (ny * nz), i // nz % ny, i % nz
        pltpu.make_async_remote_copy(
            src_ref=asend,
            dst_ref=arecv.at[i],
            send_sem=sendr,
            recv_sem=recvr,
            device_id=(around(gx, a, nx), around(gy, b, ny), around(gz, c, nz)),
            device_id_type=MESH,
        ).start()
    line_of = collect(C + 1, 2 * C + 1)
    for ix in range(8):
        for iy, v in enumerate(line_of(ix)):
            mts[block(8 * ix + iy), :] = v

    others = arecv.at[pl.ds(1, N - 1)]
    pltpu.make_async_copy(others, others, recvr).wait()
    total = jnp.sum(arecv[...], axis=0)

    def entry(k, m):
        q = (128 - (k * (C + 2) + m) * C) % 128
        return pltpu.roll(total, q, 1) if q else total

    G = [[None] * STEPS for _ in range(STEPS)]
    for k in range(STEPS):
        G[k][k] = entry(k, 0)
        if k:
            G[k - 1][k] = entry(k, 1)
    g = [entry(0, 1)]
    for gap in range(2, STEPS):
        for i in range(STEPS - gap):
            j = i + gap - 1
            G[i][j + 1] = G[i + 1][j] + float(THETA[i] - THETA[j]) * G[i][j]
    for i in range(1, STEPS):
        g.append(G[0][i - 1] - float(THETA[i - 1]) * g[i - 1])
    L = [[None] * STEPS for _ in range(STEPS)]
    inv = []
    for j in range(STEPS):
        lines = []
        for i in range(j, STEPS):
            t = G[j][i]
            for q in range(j):
                t = t - L[i][q] * lower[q][j]
            lines.append(t)
        if j == 0:
            lower = []
        lower.append([None] * j + lines)
        inv.append(1.0 / lines[0])
        for i in range(j + 1, STEPS):
            L[i][j] = lines[i - j] * inv[j]
    y = list(g)
    for i in range(STEPS):
        for q in range(i):
            y[i] = y[i] - L[i][q] * y[q]
    y = [t * d for t, d in zip(y, inv)]
    for i in reversed(range(STEPS)):
        for q in range(i + 1, STEPS):
            y[i] = y[i] - L[q][i] * y[q]
    couple = []
    for j in range(C):
        t = y[0] * entry(0, 2 + j)
        for k in range(1, STEPS):
            t = t + y[k] * entry(k, 2 + j)
        couple.append(t)

    def spread(line, c):
        return jnp.broadcast_to(line[:, c : c + 1], (8, Z))

    mixing = [[spread(y[k], c) for k in range(STEPS)] for c in range(C)]
    for n in range(64):
        at = block(n)
        m = mts[at, :]
        for c in range(C):
            t = mixing[c][0] * vecs[C + c, at, :]
            for k in range(1, STEPS):
                t = t + mixing[c][k] * vecs[(k + 1) * C + c, at, :]
            heat_out[c, at, :] = m * t
    kk = [[spread(couple[j], c) for j in range(C)] for c in range(C)]
    ymat = [[None] * C for _ in range(C)]
    for a in range(C):
        for b in range(C):
            if b < a:
                ymat[a][b] = ymat[b][a]
                continue
            t = kk[a][0] * kk[b][0]
            for j in range(1, C):
                t = t + kk[a][j] * kk[b][j]
            ymat[a][b] = t + 1.0 if a == b else t
    one = jnp.ones((8, Z), F32)
    nil = jnp.zeros((8, Z), F32)
    right = [[one if a == b else nil for b in range(C)] + kk[a] for a in range(C)]
    for a in range(C):
        scale = 1.0 / ymat[a][a]
        ymat[a] = [t * scale for t in ymat[a]]
        right[a] = [t * scale for t in right[a]]
        for b in range(C):
            if b != a:
                q = ymat[b][a]
                ymat[b] = [t - q * s for t, s in zip(ymat[b], ymat[a])]
                right[b] = [t - q * s for t, s in zip(right[b], right[a])]
    for c in range(C):
        for j in range(2 * C):
            q = 2 * C * c + j
            table[q : q + 1, :] = 2.0 * right[c][j][0:1, :]
    leaving.append(pltpu.make_async_copy(table, coef_out, outsem.at[1]))
    leaving[-1].start()
    pltpu.make_async_copy(others, others, sendr).wait()
    for copy in leaving:
        copy.wait()


def finish(C, E, F, lines, heat, rhs, coef, rf, fb):
    first = pl.program_id(0) * (64 * lines)

    def weight(q):
        return jnp.broadcast_to(coef[q : q + 1, :], (8, coef.shape[1]))

    weights = [[weight(2 * C * c + j) for j in range(2 * C)] for c in range(C)]
    for ix in range(lines):
        for iy in range(8):
            at = pl.ds(pl.multiple_of(first + 64 * ix + 8 * iy, 8), 8)
            hs = [heat[c, at, :] for c in range(C)]
            for j in range(2 * C):
                t = hs[0] * weights[0][j]
                for c in range(1, C):
                    t = t + hs[c] * weights[c][j]
                if j < C:
                    t = rhs[j, at, :] - t
                out = rf if j < C else fb
                for e in range(E):
                    out[j % C, e, ix, pl.ds(iy, F, stride=8), :] = t[e * F : (e + 1) * F]


def local(counts, metric, mass, shift, loads, inputs):
    C, X, Y, Z = loads.shape
    E, F = X // 8, Y // 8
    assert E * F == 8 and Z >= 128 and STEPS * (C + 2) * C <= 128
    N = counts[0] * counts[1] * counts[2]
    lz = jnp.asarray(right_matrices(Z))
    vm = lambda *shape: pltpu.VMEM(shape, F32)
    dma = pltpu.SemaphoreType.DMA
    anywhere = pl.BlockSpec(memory_space=pl.ANY)
    field = jax.ShapeDtypeStruct((C, 512, Z), F32)
    heat, rhs, coef = pl.pallas_call(
        functools.partial(kernel, (C, X, Y, Z), counts),
        out_shape=[pltpu.VMEM((C, 512, Z), F32), pltpu.VMEM((C, 512, Z), F32), jax.ShapeDtypeStruct((2 * C * C, Z), F32)],
        in_specs=[anywhere, anywhere, pl.BlockSpec(memory_space=pltpu.SMEM), anywhere, anywhere,
                  pl.BlockSpec(memory_space=pltpu.VMEM)],
        out_specs=[pl.BlockSpec(memory_space=pltpu.VMEM)] * 2 + [anywhere],
        scratch_shapes=[
            vm(2 * C + 7, 8, 64, Z), vm(2 * C * C, Z), vm(6, 512, Z), vm(C, 512, Z),
            vm((STEPS + 1) * C, 512, Z), vm(C + 2, 512, Z), vm(512, Z), vm(512, Z),
            vm(C + 1, 512, Z), vm(512, Z), vm(512, Z), vm(512, Z), vm(512, Z), vm(512, Z),
            vm(128, 8, Z), vm(128, Z),
            vm(C + 2, 2, 64 // E, Z), vm(2 * C + 2, 2, 64 // E, Z),
            vm(C + 2, 2, 64 // F, Z), vm(2 * C + 2, 2, 64 // F, Z),
            vm(2 * C + 2, 4, 8, Z), vm(C + 2, 8, Z), vm(2 * C + 2, 1 if counts[2] == 2 else 2, 9, 8, Z),
            vm(1, 128), vm(N, 1, 128),
            dma((4, E)), dma((2,)), dma((C + 2, 27)), dma((2 * C + 2, 27)), dma, dma,
            pltpu.SemaphoreType.REGULAR,
        ],
        compiler_params=pltpu.CompilerParams(
            collective_id=0, has_side_effects=True, vmem_limit_bytes=56 << 20
        ),
    )(metric, mass, shift, loads, inputs, lz)
    lines = 4
    whole = pl.BlockSpec((C, E, lines, Y, Z), lambda i: (0, 0, i, 0, 0))
    rf, fb = pl.pallas_call(
        functools.partial(finish, C, E, F, lines),
        grid=(8 // lines,),
        out_shape=[jax.ShapeDtypeStruct((C, E, 8, Y, Z), F32)] * 2,
        in_specs=[pl.BlockSpec(memory_space=pltpu.VMEM)] * 3,
        out_specs=[whole, whole],
        compiler_params=pltpu.CompilerParams(vmem_limit_bytes=24 << 20),
    )(heat, rhs, coef)
    return rf.reshape(loads.shape), fb.reshape(loads.shape)


def solution(mesh):
    counts = tuple(mesh.shape[a] for a in ("gx", "gy", "gz"))
    return jax.shard_map(
        functools.partial(local, counts),
        mesh=mesh,
        in_specs=(
            P(None, "gx", "gy", "gz"),
            P("gx", "gy", "gz"),
            P(),
            P(None, "gx", "gy", "gz"),
            P(None, "gx", "gy", "gz"),
        ),
        out_specs=(P(None, "gx", "gy", "gz"), P(None, "gx", "gy", "gz")),
        check_vma=False,
    )
```

```python
import functools

import jax
import jax.numpy as jnp
import numpy as np
from jax import lax
from jax.experimental import pallas as pl
from jax.experimental.pallas import tpu as pltpu
from jax.sharding import PartitionSpec as P

STEPS = 5
THETA = (1.25, 0.2, 2.3, 0.7)
MESH = pl.DeviceIdType.MESH
F32 = jnp.float32
BF16 = jnp.bfloat16

gll_points = (
    -1.0,
    -0.8717401485096066,
    -0.5917001814331423,
    -0.2092992179024789,
    0.2092992179024789,
    0.5917001814331423,
    0.8717401485096066,
    1.0,
)


def gll_table():
    points = np.array(gll_points)
    values = (429.0 * points**7 - 693.0 * points**5 + 315.0 * points**3 - 35.0 * points) / 16.0
    table = np.zeros((8, 8))
    for row in range(8):
        for column in range(8):
            if row != column:
                table[row, column] = values[row] / (values[column] * (points[row] - points[column]))
    table[0, 0] = -14.0
    table[7, 7] = 14.0
    return table


TABLE = gll_table()
SQUARES = TABLE * TABLE


def halves(matrix):
    full = np.asarray(matrix, np.float32)
    high = full.astype(jnp.bfloat16)
    low = (full - high.astype(np.float32)).astype(jnp.bfloat16)
    return high, low


def right_matrices(depth):
    eye = np.eye(depth // 8)
    out = []
    for m in (TABLE.T, TABLE, SQUARES):
        high, low = halves(np.kron(eye, m))
        out.append(np.block([[high, low], [high, np.zeros_like(low)]]))
    return np.stack(out)


def mix_lines(matrix, lines, even_matrix=False):
    even = [lines[j] + lines[7 - j] for j in range(4)]
    odd = [lines[j] - lines[7 - j] for j in range(4)]
    out = [None] * 8
    for i in range(4):
        p = q = None
        for j in range(4):
            a = float(np.float32(0.5 * (matrix[i, j] + matrix[i, 7 - j])))
            b = float(np.float32(0.5 * (matrix[i, j] - matrix[i, 7 - j])))
            p = a * even[j] if p is None else p + a * even[j]
            q = b * odd[j] if q is None else q + b * odd[j]
        out[i] = q + p
        out[7 - i] = p - q if even_matrix else q - p
    return out


def right_apply(lz, kind, v):
    high = v.astype(BF16)
    low = (v - high.astype(F32)).astype(BF16)
    depth = v.shape[1]
    both = jnp.dot(
        jnp.concatenate([high, low], axis=1), lz[kind], preferred_element_type=F32
    )
    return both[:, :depth] + both[:, depth:]


def kernel(
    dims, counts,
    metric, mass, shift, loads, inputs, lz,
    heat_out, rhs_out, coef_out,
    stage, table, met, inp, vecs, w, pre, mts, rhs, sm, s2, s3, f2, rr, acc, rows,
    xs, xr, ys, yr, er, zs, zr, asend, arecv,
    insem, outsem, ssem, rsem, sendr, recvr, besides,
):
    C, X, Y, Z = dims
    nx, ny, nz = counts
    N = nx * ny * nz
    E, F = X // 8, Y // 8
    LOADS, MASS, METRIC, INPUTS = 0, C, C + 1, C + 7
    gx, gy, gz = lax.axis_index("gx"), lax.axis_index("gy"), lax.axis_index("gz")
    me = (gx * ny + gy) * nz + gz
    sh = shift[0]

    def block(n):
        return pl.ds(8 * n, 8)

    sources = (
        (loads, LOADS, C), (mass, MASS, 1), (metric, METRIC, 6), (inputs, INPUTS, C),
    )

    def fetch(q, e):
        ref, first, count = sources[q]
        if q == 1:
            src = ref.at[pl.ds(8 * e, 8)]
            dst = stage.at[first, :, pl.ds(Y * e, Y)]
        else:
            src = ref.at[:, pl.ds(8 * e, 8)]
            dst = stage.at[pl.ds(first, count), :, pl.ds(Y * e, Y)]
        return pltpu.make_async_copy(src, dst, insem.at[q, e])

    for q in range(4):
        for e in range(E):
            fetch(q, e).start()

    def coords(number):
        rest = lax.div(number, nz)
        return (lax.div(rest, ny), lax.rem(rest, ny), lax.rem(number, nz))

    for ref in (xr, yr, er, zr):
        ref[...] = jnp.zeros(ref.shape, F32)
    def raw(f, ix, iy):
        return stage[f, ix, pl.ds(iy, 8, stride=8), :]

    lane = lax.broadcasted_iota(jnp.int32, (8, Z), 1)
    sub = lax.broadcasted_iota(jnp.int32, (8, Z), 0)
    ye = sub % F
    inner0 = (lane % 8 == 0) & (lane > 0)
    inner7 = (lane % 8 == 7) & (lane < Z - 1)
    inner = inner0 | inner7
    across = jnp.where(inner0, lane - 1, jnp.where(inner7, lane + 1, lane))
    across = jnp.where((lane == 0) | (lane == Z - 2), Z - 1, across)
    across = jnp.where((lane == 1) | (lane == Z - 1), 0, across)
    rim = (lane == 0) | (lane == Z - 1)
    slot_of_lane = lane // 2
    ix_of_lane, iy_of_lane = slot_of_lane // 8, slot_of_lane % 8

    xe = sub // F
    weight_x = [
        jnp.where((xe > 0) | (gx > 0), 0.5, 1.0), jnp.where((xe < E - 1) | (gx < nx - 1), 0.5, 1.0)
    ]
    weight_y = [
        jnp.where((ye > 0) | (gy > 0), 0.5, 1.0), jnp.where((ye < F - 1) | (gy < ny - 1), 0.5, 1.0)
    ]
    weight_z = jnp.where(
        ((lane % 8 == 0) & ((lane > 0) | (gz > 0)))
        | ((lane % 8 == 7) & ((lane < Z - 1) | (gz < nz - 1))),
        0.5, 1.0,
    )

    def corner(hx, hy):
        return hx * (8 - F) + hy * (F - 1)

    if nz == 2:
        z_steps = [(1 - 2 * gz, None, None, 0)]
    else:
        z_steps = [(-1, gz > 0, gz < nz - 1, 1), (1, gz < nz - 1, gz > 0, 0)]
    columns = [(dx, dy) for dx in (-1, 0, 1) for dy in (-1, 0, 1)]

    def there(dx, dy):
        ok = None
        for place, step, count in zip((gx, gy), (dx, dy), (nx, ny)):
            if step:
                one = place > 0 if step < 0 else place < count - 1
                ok = one if ok is None else ok & one
        return ok

    def under(test, act):
        if test is None:
            act()
        else:
            pl.when(test)(act)

    def both_tests(a, b):
        return b if a is None else a if b is None else a & b

    def towards(act):
        for dx, dy in columns:
            def group(dx=dx, dy=dy):
                if dx or dy:
                    act(dx, dy, None)
                for q, step in enumerate(z_steps):
                    under(step[1], functools.partial(act, dx, dy, q))
            under(there(dx, dy), group)

    def backwards(act):
        for dx, dy in columns:
            def group(dx=dx, dy=dy):
                if dx or dy:
                    act(dx, dy, None)
                for q, step in enumerate(z_steps):
                    under(step[2], functools.partial(act, dx, dy, q))
            under(there(-dx, -dy), group)

    barrier = pltpu.get_barrier_semaphore()
    if max(counts) - 1 <= STEPS:
        greeted = jnp.int32(0)
        for dx, dy in columns:
            test = there(dx, dy)
            if test is not None:
                greeted = greeted + test.astype(jnp.int32)
        for step in z_steps:
            greeted = greeted + (1 if step[1] is None else step[1].astype(jnp.int32))

        def signal(dx, dy, q, sem):
            dz = 0 if q is None else z_steps[q][0]
            pl.semaphore_signal(
                sem, inc=1, device_id=(gx + dx, gy + dy, gz + dz), device_id_type=MESH
            )

        for dx, dy in columns:
            if dx or dy:
                under(there(dx, dy), functools.partial(signal, dx, dy, None, barrier))
        for q, step in enumerate(z_steps):
            under(step[1], functools.partial(signal, 0, 0, q, barrier))
    else:
        greeted = N - 1

        def greet(i, carry):
            pl.semaphore_signal(
                barrier, inc=1, device_id=coords(lax.rem(me + i, N)), device_id_type=MESH
            )
            return carry

        lax.fori_loop(1, N, greet, 0)

    def message(dx, dy, q, sslot, rslot):
        hx, hy = (dx + 1) // 2, (dy + 1) // 2
        i = 3 * (dx + 1) + dy + 1
        if q is None:
            dz = 0
            if dy == 0:
                src, dst = xs.at[sslot, hx], xr.at[rslot, 1 - hx]
            elif dx == 0:
                src, dst = ys.at[sslot, hy], yr.at[rslot, 1 - hy]
            else:
                row = 8 * (56 * hx + 7 * hy) + corner(hx, hy)
                src = w.at[sslot, pl.ds(row, 1)]
                dst = er.at[rslot, 2 * (1 - hx) + (1 - hy), pl.ds(corner(1 - hx, 1 - hy), 1)]
        else:
            dz, _, _, side = z_steps[q]
            if dx and dy:
                a, b, count = corner(hx, hy), corner(1 - hx, 1 - hy), 1
            elif dx:
                a, b, count = hx * (8 - F), (1 - hx) * (8 - F), F
            else:
                a, b, count = 0, 0, 8
            src = zs.at[sslot, pl.ds(a, count)]
            dst = zr.at[rslot, side, 8 - i, pl.ds(b, count)]
            i = 9 * (q + 1) + i
        return pltpu.make_async_remote_copy(
            src_ref=src,
            dst_ref=dst,
            send_sem=ssem.at[sslot, i],
            recv_sem=rsem.at[rslot, i],
            device_id=(gx + dx, gy + dy, gz + dz),
            device_id_type=MESH,
        )

    def fold(a, line_of):
        def along_y(line):
            v0, v7 = line[0], line[7]
            line = list(line)
            line[0] = v0 + jnp.where(ye > 0, pltpu.roll(v7, 1, 0), 0.0)
            line[7] = v7 + jnp.where(ye < F - 1, pltpu.roll(v0, 7, 0), 0.0)
            return line

        first, last = along_y(line_of(0)), along_y(line_of(7))
        lines = {
            0: [
                v + jnp.where(sub >= F, pltpu.roll(t, F, 0), 0.0) for v, t in zip(first, last)
            ],
            7: [
                t + jnp.where(sub < 8 - F, pltpu.roll(v, 8 - F, 0), 0.0)
                for v, t in zip(first, last)
            ],
        }
        packed = jnp.zeros((8, Z), F32)
        faces = [[None] * (8 // F) for _ in range(2)]
        for ix in (0, 7, 1, 2, 3, 4, 5, 6):
            line = lines[ix] if ix in lines else along_y(line_of(ix))
            swapped = [jnp.take_along_axis(v, across, axis=1) for v in line]
            line = [v + jnp.where(inner, t, 0.0) for v, t in zip(line, swapped)]
            for iy in range(8):
                n = 8 * ix + iy
                w[a, block(n), :] = line[iy]
                if iy % 2 == 0:
                    moved = jnp.where(lane < Z // 2, swapped[iy + 1], swapped[iy])
                    moved = pltpu.roll(moved, (2 * n + 2) % Z, 1)
                    packed = jnp.where(slot_of_lane // 2 == n // 2, moved, packed)
            if ix in (0, 7):
                h = ix // 7
                for j in range(8 // E):
                    out = None
                    for g in range(E):
                        v = line[j * E + g]
                        q = (g * F + h * F) % 8
                        v = pltpu.roll(v, q, 0) if q else v
                        out = v if out is None else jnp.where(sub // F == g, v, out)
                    xs[a, h, 8 * j : 8 * j + 8, :] = out
            for h in range(2):
                j, g = ix // F, ix % F
                v = line[7 * h]
                q = (g - h * (F - 1)) % 8
                v = pltpu.roll(v, q, 0) if q else v
                old = faces[h][j]
                faces[h][j] = v if old is None else jnp.where(ye == g, v, old)
        zs[a] = packed
        for h in range(2):
            for j in range(8 // F):
                ys[a, h, 8 * j : 8 * j + 8, :] = faces[h][j]

    def send(a, rslot):
        towards(lambda dx, dy, q: message(dx, dy, q, a, rslot).start())

    def collect(a, rslot):
        backwards(lambda dx, dy, q: message(dx, dy, q, a, rslot).wait_recv())
        towards(lambda dx, dy, q: message(dx, dy, q, a, rslot).wait_send())
        sides = []
        for h in range(len(z_steps)):
            total = zr[rslot, h, 4]
            for dx in (-1, 0, 1):
                for dy in (-1, 0, 1):
                    if dx == 0 and dy == 0:
                        continue
                    v = zr[rslot, h, 3 * (dx + 1) + dy + 1]
                    if dx == 0:
                        v = pltpu.roll(v, (dy * (F - 1)) % 8, 0)
                    v = pltpu.roll(v, (2 * (56 * dx + 7 * dy)) % Z, 1)
                    mask = None
                    if dx:
                        mask = ix_of_lane == (7 if dx > 0 else 0)
                    if dy:
                        more = iy_of_lane == (7 if dy > 0 else 0)
                        mask = more if mask is None else mask & more
                    if dx == 0:
                        mask = mask & (ye == (F - 1 if dy > 0 else 0))
                    total = total + jnp.where(mask, v, 0.0)
            sides.append(total)
        if nz == 2:
            sides = [jnp.where(gz > 0, sides[0], 0.0), jnp.where(gz > 0, 0.0, sides[0])]
        both = jnp.where(
            lane % 2 == 0, sides[0], pltpu.roll(sides[1], Z - 2, 1)
        )

        def line_of(ix):
            line = []
            for iy in range(8):
                n = 8 * ix + iy
                v = pltpu.roll(both, (Z - 2 * n) % Z, 1) if n else both
                line.append(w[a, block(n), :] + jnp.where(rim, v, 0.0))
            if ix in (0, 7):
                h = ix // 7
                for iy in range(8):
                    j, g = iy // E, iy % E
                    v = xr[rslot, h, 8 * j : 8 * j + 8, :]
                    q = (h * (8 - F) - g * F) % 8
                    v = pltpu.roll(v, q, 0) if q else v
                    mask = sub >= 8 - F if h else sub < F
                    line[iy] = line[iy] + jnp.where(mask, v, 0.0)
                for hy in range(2):
                    line[7 * hy] = line[7 * hy] + er[rslot, 2 * h + hy]
            for h in range(2):
                j, g = ix // F, ix % F
                v = yr[rslot, h, 8 * j : 8 * j + 8, :]
                q = (h * (F - 1) - g) % 8
                v = pltpu.roll(v, q, 0) if q else v
                line[7 * h] = line[7 * h] + jnp.where(ye == h * (F - 1), v, 0.0)
            return line

        return line_of

    for e in range(E):
        fetch(0, e).wait()
    def fold_load(c, carry):
        fold(c, lambda ix: [raw(LOADS + c, ix, iy) for iy in range(8)])
        return carry

    lax.fori_loop(0, C, fold_load, 0)
    for q in (1, 2):
        for e in range(E):
            fetch(q, e).wait()
    for ix in range(8):
        for iy in range(8):
            at = block(8 * ix + iy)
            sm[at, :] = sh * raw(MASS, ix, iy)
            for f in range(6):
                met[f, at, :] = raw(METRIC + f, ix, iy)
    for part in range(2):
        at = pl.ds(256 * part, 256)
        s3[at, :] = right_apply(lz, 2, met[2, at, :])
    for ix in range(8):
        line = mix_lines(SQUARES.T, [met[1, block(8 * ix + iy), :] for iy in range(8)], True)
        for iy in range(8):
            s2[block(8 * ix + iy), :] = line[iy]
    ends = (-14.0,) + (0.0,) * 6 + (14.0,)
    ends_z = jnp.where(lane % 8 == 0, -14.0, jnp.where(lane % 8 == 7, 14.0, 0.0))
    for iy in range(8):
        line = mix_lines(SQUARES.T, [met[0, block(8 * ix + iy), :] for ix in range(8)], True)
        for ix in range(8):
            at = block(8 * ix + iy)
            total = line[ix] + s2[at, :] + s3[at, :] + sm[at, :]
            if ends[ix] and ends[iy]:
                total = total + (2.0 * ends[ix] * ends[iy]) * met[3, at, :]
            if ends[ix]:
                total = total + (2.0 * ends[ix]) * (ends_z * met[4, at, :])
            if ends[iy]:
                total = total + (2.0 * ends[iy]) * (ends_z * met[5, at, :])
            rr[at, :] = total

    def lines_in(ref):
        return lambda ix: [ref[block(8 * ix + iy), :] for iy in range(8)]

    fold(C, lines_in(rr))
    for c in range(C):
        vecs[c] = jnp.zeros((512, Z), F32)
    acc[...] = jnp.zeros(acc.shape, F32)
    rows[...] = jnp.zeros(rows.shape, F32)

    pl.semaphore_wait(barrier, greeted)
    if max(counts) - 1 <= STEPS:
        beside = jnp.int32(0)
        for q, step in enumerate(z_steps):
            under(step[1], functools.partial(signal, 0, 0, q, besides))
            beside = beside + (1 if step[1] is None else step[1].astype(jnp.int32))
        pl.semaphore_wait(besides, beside)
    for a in (C,) + tuple(range(C)):
        send(a, C + a)
    fold(C + 1, lines_in(sm))
    send(C + 1, 2 * C + 1)

    for e in range(E):
        fetch(3, e).wait()
    for j in range(C):
        for ix in range(8):
            for iy in range(8):
                inp[j, block(8 * ix + iy), :] = raw(INPUTS + j, ix, iy)

    line_of = collect(C, 2 * C)
    for ix in range(8):
        for iy, v in enumerate(line_of(ix)):
            pre[block(8 * ix + iy), :] = 1.0 / v

    def unit(final, u, carry):
        k = u // C
        c = u % C
        theta = jnp.where(
            k == 0, 0.0,
            jnp.where(k == 1, THETA[0], jnp.where(k == 2, THETA[1], jnp.where(k == 3, THETA[2], THETA[3]))),
        ).astype(F32)
        line_of = collect(c, ((k + 1) % 2) * C + c)
        keep = ((k + STEPS - 1) // STEPS) * (C - c) + c
        shared = [[None] * 3 for _ in range(3)]
        sums = [None] * (C + 2)

        def add(old, t):
            return t if old is None else old + t

        for ix in range(8):
            line = line_of(ix)
            before = [vecs[u, block(8 * ix + iy), :] for iy in range(8)]
            scale = [pre[block(8 * ix + iy), :] for iy in range(8)]
            fresh = [p * t - theta * b for p, t, b in zip(scale, line, before)]
            for iy in range(8):
                at = block(8 * ix + iy)
                v = fresh[iy]
                vecs[u + C, at, :] = v
                if not final:
                    rhs[keep, at, :] = line[iy]
                p, q = (ix > 0) + (ix == 7), (iy > 0) + (iy == 7)
                shared[p][q] = add(shared[p][q], v * line[iy])
                if final:
                    for j in range(C):
                        sums[2 + j] = add(sums[2 + j], v * inp[j, at, :])
        for p in range(3):
            for q in range(3):
                t = shared[p][q]
                if p != 1:
                    t = t * weight_x[p // 2]
                if q != 1:
                    t = t * weight_y[q // 2]
                sums[1] = add(sums[1], t)
        sums[1] = sums[1] * weight_z

        for part in range(2):
            at = pl.ds(256 * part, 256)
            s3[at, :] = right_apply(lz, 0, vecs[u + C, at, :])
        for ix in range(8):
            line = mix_lines(TABLE, [vecs[u + C, block(8 * ix + iy), :] for iy in range(8)])
            for iy in range(8):
                s2[block(8 * ix + iy), :] = line[iy]
        for iy in range(8):
            va = [vecs[u + C, block(8 * ix + iy), :] for ix in range(8)]
            s1 = mix_lines(TABLE, va)
            f1 = []
            for ix in range(8):
                at = block(8 * ix + iy)
                a, b, g = s1[ix], s2[at, :], s3[at, :]
                m12, m13, m23 = met[3, at, :], met[4, at, :], met[5, at, :]
                if final:
                    t = m12 * b + m13 * g
                    q = m23 * g
                    t = a * (met[0, at, :] * a + (t + t)) + b * (met[1, at, :] * b + (q + q))
                    t = t + g * (met[2, at, :] * g) + va[ix] * (sm[at, :] * va[ix])
                    sums[0] = add(sums[0], t)
                    continue
                f1.append(met[0, at, :] * a + m12 * b + m13 * g)
                f2[at, :] = m12 * a + met[1, at, :] * b + m23 * g
                s3[at, :] = m13 * a + m23 * b + met[2, at, :] * g
            if final:
                continue
            r1 = mix_lines(TABLE.T, f1)
            for ix in range(8):
                at = block(8 * ix + iy)
                rr[at, :] = r1[ix] + sm[at, :] * va[ix]
        def result(ix):
            r2 = mix_lines(TABLE.T, [f2[block(8 * ix + iy), :] for iy in range(8)])
            out = []
            for iy in range(8):
                at = block(8 * ix + iy)
                out.append(r2[iy] + rr[at, :])
                sums[0] = add(sums[0], vecs[u + C, at, :] * out[iy])
            return out

        if not final:
            for part in range(2):
                at = pl.ds(256 * part, 256)
                rr[at, :] = rr[at, :] + right_apply(lz, 1, s3[at, :])
            fold(c, result)
        if not final:
            send(c, (k % 2) * C + c)
            for n in range(64):
                at = block(n)
                v = vecs[u + C, at, :]
                for j in range(C):
                    sums[2 + j] = add(sums[2 + j], v * inp[j, at, :])
        for m in range(C + 2):
            acc[(k * (C + 2) + m) * C + c] = sums[m]
        return carry

    lax.fori_loop(0, (STEPS - 1) * C, functools.partial(unit, False), 0)
    def add_up(start, stop):
        for q in range(start, stop):
            rows[q : q + 1, :] = jnp.sum(acc[q], axis=0, keepdims=True)

    add_up(0, (STEPS - 1) * (C + 2) * C)
    leaving = [pltpu.make_async_copy(rhs.at[pl.ds(0, C)], rhs_out, outsem.at[0])]
    leaving[0].start()
    lax.fori_loop((STEPS - 1) * C, STEPS * C, functools.partial(unit, True), 0)

    add_up((STEPS - 1) * (C + 2) * C, STEPS * (C + 2) * C)
    part = jnp.sum(rows[...].T, axis=0, keepdims=True)
    asend[...] = part
    arecv[0] = part

    def around(place, step, count):
        moved = place + step
        return lax.select(moved >= count, moved - count, moved) if step else place

    for i in range(1, N):
        a, b, c = i // (ny * nz), i // nz % ny, i % nz
        pltpu.make_async_remote_copy(
            src_ref=asend,
            dst_ref=arecv.at[i],
            send_sem=sendr,
            recv_sem=recvr,
            device_id=(around(gx, a, nx), around(gy, b, ny), around(gz, c, nz)),
            device_id_type=MESH,
        ).start()
    line_of = collect(C + 1, 2 * C + 1)
    for ix in range(8):
        for iy, v in enumerate(line_of(ix)):
            mts[block(8 * ix + iy), :] = v

    others = arecv.at[pl.ds(1, N - 1)]
    pltpu.make_async_copy(others, others, recvr).wait()
    total = jnp.sum(arecv[...], axis=0)

    def entry(k, m):
        q = (128 - (k * (C + 2) + m) * C) % 128
        return pltpu.roll(total, q, 1) if q else total

    G = [[None] * STEPS for _ in range(STEPS)]
    for k in range(STEPS):
        G[k][k] = entry(k, 0)
        if k:
            G[k - 1][k] = entry(k, 1)
    g = [entry(0, 1)]
    for gap in range(2, STEPS):
        for i in range(STEPS - gap):
            j = i + gap - 1
            G[i][j + 1] = G[i + 1][j] + float(THETA[i] - THETA[j]) * G[i][j]
    for i in range(1, STEPS):
        g.append(G[0][i - 1] - float(THETA[i - 1]) * g[i - 1])
    L = [[None] * STEPS for _ in range(STEPS)]
    inv = []
    for j in range(STEPS):
        lines = []
        for i in range(j, STEPS):
            t = G[j][i]
            for q in range(j):
                t = t - L[i][q] * lower[q][j]
            lines.append(t)
        if j == 0:
            lower = []
        lower.append([None] * j + lines)
        inv.append(1.0 / lines[0])
        for i in range(j + 1, STEPS):
            L[i][j] = lines[i - j] * inv[j]
    y = list(g)
    for i in range(STEPS):
        for q in range(i):
            y[i] = y[i] - L[i][q] * y[q]
    y = [t * d for t, d in zip(y, inv)]
    for i in reversed(range(STEPS)):
        for q in range(i + 1, STEPS):
            y[i] = y[i] - L[q][i] * y[q]
    couple = []
    for j in range(C):
        t = y[0] * entry(0, 2 + j)
        for k in range(1, STEPS):
            t = t + y[k] * entry(k, 2 + j)
        couple.append(t)

    def spread(line, c):
        return jnp.broadcast_to(line[:, c : c + 1], (8, Z))

    mixing = [[spread(y[k], c) for k in range(STEPS)] for c in range(C)]
    for n in range(64):
        at = block(n)
        m = mts[at, :]
        for c in range(C):
            t = mixing[c][0] * vecs[C + c, at, :]
            for k in range(1, STEPS):
                t = t + mixing[c][k] * vecs[(k + 1) * C + c, at, :]
            heat_out[c, at, :] = m * t
    kk = [[spread(couple[j], c) for j in range(C)] for c in range(C)]
    ymat = [[None] * C for _ in range(C)]
    for a in range(C):
        for b in range(C):
            if b < a:
                ymat[a][b] = ymat[b][a]
                continue
            t = kk[a][0] * kk[b][0]
            for j in range(1, C):
                t = t + kk[a][j] * kk[b][j]
            ymat[a][b] = t + 1.0 if a == b else t
    one = jnp.ones((8, Z), F32)
    nil = jnp.zeros((8, Z), F32)
    right = [[one if a == b else nil for b in range(C)] + kk[a] for a in range(C)]
    for a in range(C):
        scale = 1.0 / ymat[a][a]
        ymat[a] = [t * scale for t in ymat[a]]
        right[a] = [t * scale for t in right[a]]
        for b in range(C):
            if b != a:
                q = ymat[b][a]
                ymat[b] = [t - q * s for t, s in zip(ymat[b], ymat[a])]
                right[b] = [t - q * s for t, s in zip(right[b], right[a])]
    for c in range(C):
        for j in range(2 * C):
            q = 2 * C * c + j
            table[q : q + 1, :] = 2.0 * right[c][j][0:1, :]
    leaving.append(pltpu.make_async_copy(table, coef_out, outsem.at[1]))
    leaving[-1].start()
    pltpu.make_async_copy(others, others, sendr).wait()
    for copy in leaving:
        copy.wait()


def finish(C, E, F, lines, heat, rhs, coef, rf, fb):
    first = pl.program_id(0) * (64 * lines)

    def weight(q):
        return jnp.broadcast_to(coef[q : q + 1, :], (8, coef.shape[1]))

    weights = [[weight(2 * C * c + j) for j in range(2 * C)] for c in range(C)]
    for ix in range(lines):
        for iy in range(8):
            at = pl.ds(pl.multiple_of(first + 64 * ix + 8 * iy, 8), 8)
            hs = [heat[c, at, :] for c in range(C)]
            for j in range(2 * C):
                t = hs[0] * weights[0][j]
                for c in range(1, C):
                    t = t + hs[c] * weights[c][j]
                if j < C:
                    t = rhs[j, at, :] - t
                out = rf if j < C else fb
                for e in range(E):
                    out[j % C, e, ix, pl.ds(iy, F, stride=8), :] = t[e * F : (e + 1) * F]


def local(counts, metric, mass, shift, loads, inputs):
    C, X, Y, Z = loads.shape
    E, F = X // 8, Y // 8
    assert E * F == 8 and Z >= 128 and STEPS * (C + 2) * C <= 128
    N = counts[0] * counts[1] * counts[2]
    lz = jnp.asarray(right_matrices(Z))
    vm = lambda *shape: pltpu.VMEM(shape, F32)
    dma = pltpu.SemaphoreType.DMA
    anywhere = pl.BlockSpec(memory_space=pl.ANY)
    field = jax.ShapeDtypeStruct((C, 512, Z), F32)
    heat, rhs, coef = pl.pallas_call(
        functools.partial(kernel, (C, X, Y, Z), counts),
        out_shape=[pltpu.VMEM((C, 512, Z), F32), pltpu.VMEM((C, 512, Z), F32), jax.ShapeDtypeStruct((2 * C * C, Z), F32)],
        in_specs=[anywhere, anywhere, pl.BlockSpec(memory_space=pltpu.SMEM), anywhere, anywhere,
                  pl.BlockSpec(memory_space=pltpu.VMEM)],
        out_specs=[pl.BlockSpec(memory_space=pltpu.VMEM)] * 2 + [anywhere],
        scratch_shapes=[
            vm(2 * C + 7, 8, 64, Z), vm(2 * C * C, Z), vm(6, 512, Z), vm(C, 512, Z),
            vm((STEPS + 1) * C, 512, Z), vm(C + 2, 512, Z), vm(512, Z), vm(512, Z),
            vm(C + 1, 512, Z), vm(512, Z), vm(512, Z), vm(512, Z), vm(512, Z), vm(512, Z),
            vm(128, 8, Z), vm(128, Z),
            vm(C + 2, 2, 64 // E, Z), vm(2 * C + 2, 2, 64 // E, Z),
            vm(C + 2, 2, 64 // F, Z), vm(2 * C + 2, 2, 64 // F, Z),
            vm(2 * C + 2, 4, 8, Z), vm(C + 2, 8, Z), vm(2 * C + 2, 1 if counts[2] == 2 else 2, 9, 8, Z),
            vm(1, 128), vm(N, 1, 128),
            dma((4, E)), dma((2,)), dma((C + 2, 27)), dma((2 * C + 2, 27)), dma, dma,
            pltpu.SemaphoreType.REGULAR,
        ],
        compiler_params=pltpu.CompilerParams(
            collective_id=0, has_side_effects=True, vmem_limit_bytes=56 << 20
        ),
    )(metric, mass, shift, loads, inputs, lz)
    lines = 4
    whole = pl.BlockSpec((C, E, lines, Y, Z), lambda i: (0, 0, i, 0, 0))
    rf, fb = pl.pallas_call(
        functools.partial(finish, C, E, F, lines),
        grid=(8 // lines,),
        out_shape=[jax.ShapeDtypeStruct((C, E, 8, Y, Z), F32)] * 2,
        in_specs=[pl.BlockSpec(memory_space=pltpu.VMEM)] * 3,
        out_specs=[whole, whole],
        compiler_params=pltpu.CompilerParams(vmem_limit_bytes=24 << 20),
    )(heat, rhs, coef)
    return rf.reshape(loads.shape), fb.reshape(loads.shape)


def solution(mesh):
    counts = tuple(mesh.shape[a] for a in ("gx", "gy", "gz"))
    return jax.shard_map(
        functools.partial(local, counts),
        mesh=mesh,
        in_specs=(
            P(None, "gx", "gy", "gz"),
            P("gx", "gy", "gz"),
            P(),
            P(None, "gx", "gy", "gz"),
            P(None, "gx", "gy", "gz"),
        ),
        out_specs=(P(None, "gx", "gy", "gz"), P(None, "gx", "gy", "gz")),
        check_vma=False,
    )
```
